32 devices in a mesh: lat: 4 (over y, x), lon: 8 (over z, core).
Axes of the slice: x: 2, y: 2, z: 4, core: 2. Of those that a mesh axis runs over, the one named last changes fastest.
Arguments:
- temp: float32 [40, 64, 1024], P(None, 'lat', 'lon'), may hold values from -6 to 6
- uvel: float32 [40, 64, 1024], P(None, 'lat', 'lon'), may hold values from -3 to 3
- vvel: float32 [40, 64, 1024], P(None, 'lat', 'lon'), may hold values from -3 to 3
- vert_mixing: float32 [40, 64, 1024], P(None, 'lat', 'lon'), may hold values from 0.1 to 10
- inv_dx: float32 [64, 1024], P('lat', 'lon'), may hold values from 0.5 to 2
- inv_dy: float32 [64, 1024], P('lat', 'lon'), may hold values from 0.5 to 2
- horiz_mixing: float32 [64, 1024], P('lat', 'lon'), may hold values from 0.02 to 0.1
- coriolis: float32 [64, 1024], P('lat', 'lon'), may hold values from -0.5 to 0.5
- wet_mask: int32 [40, 64, 1024], P(None, 'lat', 'lon'), may hold values from 0 to 1, as said below
- levels: int32 [64, 1024], P('lat', 'lon'), may hold values from 0 to 40, as said below
Outputs:
- temp_new: float32 [40, 64, 1024], P(None, 'lat', 'lon')
- uvel_new: float32 [40, 64, 1024], P(None, 'lat', 'lon')
- vvel_new: float32 [40, 64, 1024], P(None, 'lat', 'lon')
The draws below stay inside these ranges and needn't reach their ends.
Inputs may be any that keep to these rules, and one draw needn't show every extreme that they name: `levels`: the number of active levels of each column; 0 marks land; some column has 40. `wet_mask`: zero at every level k with k >= levels of its column.
All inputs are finite; a program needn't handle non-finite values.
Results may differ from the reference program's by a relative error of at most 0.00002.
Values sent between devices are 32-bit elements; how exact they have to be, the bound alone decides.
No kernel may reach another device: no remote copies, remote signals or barrier semaphores. Data moves between devices by JAX's collectives and lax.ppermute only.
A program may use at most 64 MiB of HBM per device.

```python
import math
import jax
import jax.numpy as jnp
from jax import lax

K = 40
NX = 1024
NY = 64


def column_levels(key):
    land_key, depth_key = jax.random.split(key)
    land = jax.random.randint(land_key, (NY, NX), 0, 4)
    depth = jax.random.randint(depth_key, (NY, NX), 1, K + 1)
    levels = jnp.where(land == 0, 0, depth).astype(jnp.int32)
    levels = levels.at[0, 0].set(K)
    levels = levels.at[0, 1].set(0)
    return levels


def draw_levels(key, part):
    return column_levels(jax.random.fold_in(key, 11))


def draw_wet_mask(key, part):
    levels = column_levels(jax.random.fold_in(key, 11))
    sills = jax.random.randint(jax.random.fold_in(key, 12), (K, NY, NX), 0, 16)
    level_index = jnp.arange(K, dtype=jnp.int32)[:, None, None]
    wet = (level_index < levels[None]) & (sills != 0)
    return wet.astype(jnp.int32)


def level_of(rng, dims, cuts, least, largest):
    level, own = 1.0, jax.random.fold_in(rng, 6)
    for dim, shards_of in cuts:
        draws = jnp.exp(jax.random.uniform(jax.random.fold_in(own, dim), (shards_of,), jnp.float32, least / len(cuts), largest / len(cuts)))
        level = level * jnp.repeat(draws, dims[dim] // shards_of).reshape([-1 if axis == dim else 1 for axis in range(len(dims))])
    return level


def normal_values(rng, shape, scale, most, cuts=(), held_as=jnp.bfloat16):
    values = jax.random.normal(rng, shape, jnp.float32) * scale
    if len(cuts) > 0:
        values = level_of(rng, shape, cuts, -0.22, 0.18) * values
    return jnp.clip(values, min=-most, max=most).astype(held_as)


def setup_inputs(seed: int = 0) -> dict:
    streams_of = jax.random.split(jax.random.key(seed), 11)
    return {
        "temp": normal_values(streams_of[0], (K, NY, NX), 1.0, 6.0, ((1, 4), (2, 8)), jnp.float32),
        "uvel": normal_values(streams_of[1], (K, NY, NX), 0.5, 3.0, ((1, 4), (2, 8)), jnp.float32),
        "vvel": normal_values(streams_of[2], (K, NY, NX), 0.5, 3.0, ((1, 4), (2, 8)), jnp.float32),
        "vert_mixing": jnp.clip(jnp.exp(math.log(10.0) - 4.6051702 * jax.random.uniform(streams_of[3], (K, NY, NX), jnp.float32) ** level_of(streams_of[3], (K, NY, NX), ((1, 4), (2, 8)), -0.2, 0.2)), 0.1, 10.0),
        "inv_dx": jnp.clip(jnp.exp(math.log(2.0) - 1.3862944 * jax.random.uniform(streams_of[4], (NY, NX), jnp.float32) ** level_of(streams_of[4], (NY, NX), ((0, 4), (1, 8)), -0.2, 0.2)), 0.5, 2.0),
        "inv_dy": jnp.clip(jnp.exp(math.log(2.0) - 1.3862944 * jax.random.uniform(streams_of[5], (NY, NX), jnp.float32) ** level_of(streams_of[5], (NY, NX), ((0, 4), (1, 8)), -0.2, 0.2)), 0.5, 2.0),
        "horiz_mixing": jnp.clip(jnp.exp(math.log(0.1) - 1.609438 * jax.random.uniform(streams_of[6], (NY, NX), jnp.float32) ** level_of(streams_of[6], (NY, NX), ((0, 4), (1, 8)), -0.2, 0.2)), 0.02, 0.1),
        "coriolis": jnp.clip(jax.random.uniform(streams_of[7], (NY, NX), jnp.float32, -0.5, 0.5) * level_of(streams_of[7], (NY, NX), ((0, 4), (1, 8)), -0.4, 0.0), -0.5, 0.5),
        "wet_mask": draw_wet_mask(jax.random.fold_in(streams_of[10], 71), 0),
        "levels": draw_levels(jax.random.fold_in(streams_of[10], 71), 0),
    }


def flux_difference(part, direction_axis, length, inverse_width, mixing, speed_index):
    far_left = lax.slice_in_dim(part, 0, length + 1, axis=direction_axis)
    near_left = lax.slice_in_dim(part, 1, length + 2, axis=direction_axis)
    near_right = lax.slice_in_dim(part, 2, length + 3, axis=direction_axis)
    far_right = lax.slice_in_dim(part, 3, length + 4, axis=direction_axis)
    face_mask = near_left[3] * near_right[3]
    speed = 0.5 * (near_left[speed_index] + near_right[speed_index])
    value = (7.0 * (near_left[:3] + near_right[:3]) - (far_left[:3] + far_right[:3])) / 12.0
    advect = face_mask * speed * value
    spread = face_mask * (near_right[:3] - near_left[:3])
    advect_diff = lax.slice_in_dim(advect, 1, length + 1, axis=direction_axis) - lax.slice_in_dim(advect, 0, length, axis=direction_axis)
    spread_diff = lax.slice_in_dim(spread, 1, length + 1, axis=direction_axis) - lax.slice_in_dim(spread, 0, length, axis=direction_axis)
    return -inverse_width * advect_diff + mixing * inverse_width * inverse_width * spread_diff


def horizontal_step(extended, inv_dx, inv_dy, horiz_mixing, coriolis):
    rows_in = extended.shape[2] - 4
    cols_in = extended.shape[3] - 4
    zonal_part = extended[:, :, 2:rows_in + 2, :]
    merid_part = extended[:, :, :, 2:cols_in + 2]
    center = extended[:, :, 2:rows_in + 2, 2:cols_in + 2]
    tendency = flux_difference(zonal_part, 3, cols_in, inv_dx, horiz_mixing, 1)
    tendency = tendency + flux_difference(merid_part, 2, rows_in, inv_dy, horiz_mixing, 2)
    rotation = jnp.stack([jnp.zeros_like(center[0]), coriolis * center[2], -coriolis * center[1]])
    return center[:3] + center[3] * (tendency + rotation)


def column_solve(provisional, vert_mixing, levels):
    depth = vert_mixing.shape[0]
    level_index = jnp.arange(depth, dtype=jnp.int32)[:, None, None]
    mixing_next = jnp.concatenate([vert_mixing[1:], jnp.zeros_like(vert_mixing[:1])], axis=0)
    lower = jnp.where((level_index >= 1) & (level_index < levels[None]), vert_mixing, jnp.zeros_like(vert_mixing))
    upper = jnp.where(level_index + 1 < levels[None], mixing_next, jnp.zeros_like(vert_mixing))
    diagonal = 1.0 + lower + upper
    gains = []
    values = []
    gain_prev = jnp.zeros_like(diagonal[0])
    value_prev = jnp.zeros_like(provisional[:, 0])
    for level in range(depth):
        denom = diagonal[level] - lower[level] * gain_prev
        gain_prev = upper[level] / denom
        value_prev = (provisional[:, level] + lower[level] * value_prev) / denom
        gains.append(gain_prev)
        values.append(value_prev)
    result = [None] * depth
    below = values[depth - 1]
    result[depth - 1] = below
    for level in range(depth - 2, -1, -1):
        below = values[level] + gains[level] * below
        result[level] = below
    return jnp.stack(result, axis=1)


def reference(temp, uvel, vvel, vert_mixing, inv_dx, inv_dy, horiz_mixing, coriolis, wet_mask, levels):
    fields = jnp.stack([temp, uvel, vvel, wet_mask.astype(jnp.float32)])
    parity = jnp.array([1.0, -1.0, -1.0, 1.0], dtype=jnp.float32)[:, None, None, None]
    periodic = jnp.concatenate([fields[..., -2:], fields, fields[..., :2]], axis=3)
    north = jnp.flip(jnp.flip(periodic[:, :, -2:], axis=2), axis=3) * parity
    south = jnp.zeros_like(periodic[:, :, :2])
    extended = jnp.concatenate([south, periodic, north], axis=2)
    provisional = horizontal_step(extended, inv_dx, inv_dy, horiz_mixing, coriolis)
    solved = column_solve(provisional, vert_mixing, levels)
    return solved[0], solved[1], solved[2]
```

```python
import jax
import jax.numpy as jnp
from jax import lax
from jax.experimental import pallas as pl
from jax.experimental.pallas import tpu as pltpu
from jax.sharding import PartitionSpec as P

ROWS = 16
LANES = 128
VMEM = pl.BlockSpec(memory_space=pltpu.VMEM)
TAIL = 4


def lane_index(rows):
    return lax.broadcasted_iota(jnp.int32, (rows, LANES), 1)


def slab_place(depth, level, field):
    if level < 32:
        return field, 4 * level
    return TAIL, 32 * field + 4 * (level - 32)


def level_rows(row, depth):
    return pl.ds(row, depth, stride=ROWS)


def pack_kernel(temp, uvel, vvel, mask, first, second, edges):
    depth = temp.shape[0] // ROWS
    odd = lax.rem(lax.axis_index("lat"), 2)
    for out, near in ((first, (ROWS - 1) * (1 - odd)), (second, (ROWS - 1) * odd)):
        far = near + jnp.where(near == 0, 1, -1)
        for number, field in enumerate((temp, uvel, vvel)):
            base = 2 * depth * number
            out[base : base + depth, :] = field[level_rows(near, depth), :]
            out[base + depth : base + 2 * depth, :] = field[level_rows(far, depth), :]
        out[6 * depth : 7 * depth, :] = mask[level_rows(near, depth), :].astype(jnp.float32)
    lane = lane_index(ROWS)
    slabs = [jnp.zeros((ROWS, LANES), jnp.float32) for _ in range(TAIL + 1)]
    for level in range(depth):
        for number, field in enumerate((temp, uvel, vvel, mask)):
            block = field[level * ROWS : (level + 1) * ROWS, :].astype(jnp.float32)
            slab, start = slab_place(depth, level, number)
            moved = pltpu.roll(block, (start + 2) % LANES, 1)
            slabs[slab] = jnp.where(lane // 4 == start // 4, moved, slabs[slab])
    for number, slab in enumerate(slabs):
        edges[number * ROWS : (number + 1) * ROWS, :] = slab


def interior_kernel(
    temp, uvel, vvel, mask, mixing, inv_dx, inv_dy, spread, coriolis, levels, prov, solve
):
    depth = temp.shape[0] // ROWS
    lane = lane_index(ROWS)
    row = lax.broadcasted_iota(jnp.int32, (ROWS, LANES), 0)
    zonal = (inv_dx[...] * (-1.0 / 24.0), spread[...] * inv_dx[...] * inv_dx[...])
    merid = (inv_dy[...] * (-1.0 / 24.0), spread[...] * inv_dy[...] * inv_dy[...])
    turn = coriolis[...]
    active = levels[...]
    gain = jnp.zeros((ROWS, LANES), jnp.float32)
    lower = jnp.zeros((ROWS, LANES), jnp.float32)
    for level in range(depth):
        here = slice(level * ROWS, (level + 1) * ROWS)
        if level + 1 < depth:
            upper = jnp.where(
                level + 1 < active, mixing[(level + 1) * ROWS : (level + 2) * ROWS, :], 0.0
            )
        else:
            upper = jnp.zeros((ROWS, LANES), jnp.float32)
        inverse = 1.0 / (1.0 + lower + upper - lower * gain)
        gain = upper * inverse
        solve[0, here, :] = inverse
        solve[1, here, :] = lower * inverse
        solve[2, here, :] = gain
        lower = upper

        wet = mask[here, :].astype(jnp.float32)
        fields = [temp[here, :], uvel[here, :], vvel[here, :]]
        total = [None, None, None]
        for axis, size, index, scale, speed_of in (
            (1, LANES, lane, zonal, 1),
            (0, ROWS, row, merid, 2),
        ):
            face = jnp.where(index >= 1, pltpu.roll(wet, 1, axis), 0.0) * wet
            face_next = pltpu.roll(face, size - 1, axis)
            before = [pltpu.roll(q, 1, axis) for q in fields]
            speed = face * (before[speed_of] + fields[speed_of])
            for number, q in enumerate(fields):
                back = before[number]
                back2 = jnp.where(index >= 2, pltpu.roll(back, 1, axis), 0.0)
                ahead = pltpu.roll(q, size - 1, axis)
                ahead0 = jnp.where(index < size - 1, ahead, 0.0)
                advect = speed * (7.0 * (back + q) - (back2 + ahead0))
                advect_diff = pltpu.roll(advect, size - 1, axis) - advect
                spread_diff = face_next * (ahead - q) - face * (q - back)
                part = scale[0] * advect_diff + scale[1] * spread_diff
                total[number] = part if total[number] is None else total[number] + part
        total[1] = total[1] + turn * fields[2]
        total[2] = total[2] - turn * fields[1]
        for number, q in enumerate(fields):
            prov[number, here, :] = q + wet * total[number]


def finish_kernel(
    prov, solve, sent1, got1, sent2, got2, edges, east1, east2, mask, inv_dx, inv_dy, spread,
    temp_new, uvel_new, vvel_new, work, scratch
):
    depth = prov.shape[1] // ROWS
    odd = lax.rem(lax.axis_index("lat"), 2)
    fold = lax.axis_index("lat") == lax.axis_size("lat") - 1
    lon_odd = lax.rem(lax.axis_index("lon"), 2) == 1
    outs = (temp_new, uvel_new, vvel_new)

    lane = lane_index(ROWS)
    quad = lane % 4

    def wrap(x, shift):
        return pltpu.roll(x, shift % LANES, 1)

    four = jnp.where(quad < 2, LANES - 2 + quad, quad - 2)

    def replicate(x):
        return jnp.take_along_axis(x, four, axis=1, mode="promise_in_bounds")

    wide = replicate(inv_dx[...])
    wide2 = replicate(spread[...]) * wide * wide

    def slab_of(ref, number):
        return ref[number * ROWS : (number + 1) * ROWS, :]

    own = [slab_of(edges, s) for s in range(TAIL + 1)]
    first = [slab_of(east1, s) for s in range(TAIL + 1)]
    second = [slab_of(east2, s) for s in range(TAIL + 1)]
    west = [jnp.where(quad < 2, jnp.where(lon_odd, a, b), o) for a, b, o in zip(first, second, own)]
    east = [jnp.where(quad < 2, o, jnp.where(lon_odd, b, a)) for a, b, o in zip(first, second, own)]

    def split(slabs):
        tail = [slabs[TAIL] if f == 0 else wrap(slabs[TAIL], -32 * f) for f in range(4)]
        return [slabs[:TAIL], tail]

    corrections = []
    for west_part, east_part in zip(split(west), split(east)):
        wet = west_part[3]
        face = wrap(wet, 1) * wet
        face_next = wrap(face, -1)
        speed_sum = wrap(west_part[1], 1) + west_part[1]
        speed = face * speed_sum * (1.0 / 24.0)
        speed_next = wrap(speed, -1)
        wet_e = east_part[3]
        face_e = wrap(wet_e, -1) * wet_e
        speed_e = face_e * (wrap(east_part[1], -1) + east_part[1]) * (1.0 / 24.0)
        speed_e_before = wrap(speed_e, 1)
        part = []
        for number in range(3):
            q = west_part[number]
            back = wrap(q, 1)
            advect = speed * (7.0 * (back + q) - (wrap(q, 2) + wrap(q, -1)))
            reach = speed_next * back
            near = wide * (advect + reach) - wide2 * (face * (q - back))
            distant = wrap(reach, 1) * wide
            q = east_part[number]
            ahead = wrap(q, -1)
            advect = speed_e * (7.0 * (ahead + q) - (wrap(q, -2) + wrap(q, 1)))
            reach = speed_e_before * ahead
            near_e = wide2 * (face_e * (ahead - q)) - wide * (advect + reach)
            distant_e = wrap(reach, -1) * wide
            part.append(
                jnp.where(
                    quad < 2,
                    jnp.where(quad == 0, distant_e, near_e),
                    jnp.where(quad == 2, near, -distant),
                )
            )
        corrections.append(part)

    border = (lane < 2) | (lane >= LANES - 2)
    for level in range(depth):
        here = slice(level * ROWS, (level + 1) * ROWS)
        for number in range(3):
            if level < 32:
                source, start = corrections[0][number], 4 * level
            else:
                source, start = corrections[1][number], 4 * (level - 32)
            moved = jnp.where(border, wrap(source, -(start + 2)), 0.0)
            work[number, here, :] = prov[number, here, :] + moved

    flipped = lax.broadcasted_iota(jnp.int32, (7 * depth, LANES), 1)
    flipped = jnp.where(fold, LANES - 1 - flipped, flipped)
    scratch[...] = jnp.take_along_axis(got2[...], flipped, axis=1, mode="promise_in_bounds")
    minus = jnp.where(fold, -1.0, 1.0)
    for mine, ghost, near_row, turned in (
        (sent1, got1, (ROWS - 1) * (1 - odd), False),
        (sent2, scratch, (ROWS - 1) * odd, True),
    ):
        south = near_row == 0
        far_row = near_row + jnp.where(south, 1, -1)
        side = jnp.where(south, 1.0, -1.0)

        def piece(ref, number):
            return ref[number * depth : (number + 1) * depth, :]

        wet0 = piece(mine, 6)
        face = piece(ghost, 6) * wet0
        face_next = wet0 * mask[level_rows(far_row, depth), :].astype(jnp.float32)
        inv0 = inv_dy[pl.ds(near_row, 1), :]
        inv1 = inv_dy[pl.ds(far_row, 1), :] * side
        mix0 = spread[pl.ds(near_row, 1), :] * inv0 * inv0
        inv0 = inv0 * side
        flip = minus if turned else 1.0
        speed = face * (piece(ghost, 4) * flip + piece(mine, 4)) * (1.0 / 24.0)
        speed_next = face_next * (piece(mine, 4) + piece(mine, 5)) * (1.0 / 24.0)
        for number in range(3):
            sign = 1.0 if number == 0 else flip
            g0 = piece(ghost, 2 * number) * sign
            g1 = piece(ghost, 2 * number + 1) * sign
            o0 = piece(mine, 2 * number)
            o1 = piece(mine, 2 * number + 1)
            advect = speed * (7.0 * (g0 + o0) - (g1 + o1))
            reach = speed_next * g0
            near = inv0 * (advect + reach) + mix0 * (face * (g0 - o0))
            view = work.at[number]
            view[level_rows(near_row, depth), :] += near
            view[level_rows(far_row, depth), :] -= inv1 * reach

    values = [jnp.zeros((ROWS, LANES), jnp.float32)] * 3
    for level in range(depth):
        here = slice(level * ROWS, (level + 1) * ROWS)
        inverse = solve[0, here, :]
        carry = solve[1, here, :]
        for number in range(3):
            values[number] = inverse * work[number, here, :] + carry * values[number]
            work[number, here, :] = values[number]
    for number in range(3):
        outs[number][(depth - 1) * ROWS : depth * ROWS, :] = values[number]
    for level in range(depth - 2, -1, -1):
        here = slice(level * ROWS, (level + 1) * ROWS)
        gain = solve[2, here, :]
        for number in range(3):
            values[number] = work[number, here, :] + gain * values[number]
            outs[number][here, :] = values[number]


def swaps(pairs):
    return [route for a, b in pairs for route in ((a, b), (b, a))]


def exchange_routes(lats, lons):
    def at(lat, lon):
        return lat * lons + lon % lons

    every = range(lons)
    lon_first = [(at(l, c), at(l, c + 1)) for l in range(lats) for c in range(0, lons, 2)]
    lon_second = [(at(l, c), at(l, c + 1)) for l in range(lats) for c in range(1, lons, 2)]
    lat_first = [(at(l, c), at(l + 1, c)) for l in range(0, lats, 2) for c in every]
    lat_second = [(at(l, c), at(l + 1, c)) for l in range(1, lats - 1, 2) for c in every]
    lat_second += [(at(lats - 1, c), at(lats - 1, lons - 1 - c)) for c in range(lons // 2)]
    return [swaps(pairs) for pairs in (lon_first, lon_second, lat_first, lat_second)]


def per_device(
    temp, uvel, vvel, vert_mixing, inv_dx, inv_dy, horiz_mixing, coriolis, wet_mask, levels
):
    depth, rows, lanes = temp.shape
    assert (rows, lanes) == (ROWS, LANES) and depth == 40
    lats, lons = lax.axis_size("lat"), lax.axis_size("lon")
    assert lats % 2 == 0 and lons % 2 == 0
    flat = depth * rows

    def f32(*shape):
        return jax.ShapeDtypeStruct(shape, jnp.float32)

    temp, uvel, vvel, vert_mixing, wet_mask = (
        x.reshape(flat, lanes) for x in (temp, uvel, vvel, vert_mixing, wet_mask)
    )
    limit = pltpu.CompilerParams(vmem_limit_bytes=16 << 20)
    sent1, sent2, edges = pl.pallas_call(
        pack_kernel,
        name="pack",
        out_shape=(f32(7 * depth, lanes), f32(7 * depth, lanes), f32((TAIL + 1) * rows, lanes)),
        in_specs=[VMEM] * 4,
        out_specs=(VMEM,) * 3,
        compiler_params=limit,
    )(temp, uvel, vvel, wet_mask)
    lon_first, lon_second, lat_first, lat_second = exchange_routes(lats, lons)
    both = ("lat", "lon")
    got2 = lax.ppermute(sent2, both, lat_second)
    east2 = lax.ppermute(edges, both, lon_second)
    got1 = lax.ppermute(sent1, both, lat_first)
    east1 = lax.ppermute(edges, both, lon_first)
    prov, solve = pl.pallas_call(
        interior_kernel,
        name="interior",
        out_shape=(f32(3, flat, lanes), f32(3, flat, lanes)),
        in_specs=[VMEM] * 10,
        out_specs=(VMEM,) * 2,
        compiler_params=limit,
        cost_estimate=pl.CostEstimate(flops=20_000_000, bytes_accessed=6_000_000, transcendentals=0),
    )(temp, uvel, vvel, wet_mask, vert_mixing, inv_dx, inv_dy, horiz_mixing, coriolis, levels)
    outs = pl.pallas_call(
        finish_kernel,
        name="finish",
        out_shape=(f32(flat, lanes),) * 3,
        in_specs=[VMEM] * 13,
        out_specs=(VMEM,) * 3,
        scratch_shapes=[pltpu.VMEM((3, flat, lanes), jnp.float32), pltpu.VMEM((7 * depth, lanes), jnp.float32)],
        compiler_params=limit,
    )(prov, solve, sent1, got1, sent2, got2, edges, east1, east2, wet_mask, inv_dx, inv_dy, horiz_mixing)
    return tuple(x.reshape(depth, rows, lanes) for x in outs)


def solution(mesh):
    field, plane = P(None, "lat", "lon"), P("lat", "lon")
    return jax.shard_map(
        per_device,
        mesh=mesh,
        in_specs=(field,) * 4 + (plane,) * 4 + (field, plane),
        out_specs=(field,) * 3,
        check_vma=False,
    )
```

```python
import jax
import jax.numpy as jnp
from jax import lax
from jax.experimental import pallas as pl
from jax.experimental.pallas import tpu as pltpu
from jax.sharding import PartitionSpec as P

ROWS = 16
LANES = 128
TILE = 8
TAIL = 4
VMEM = pl.BlockSpec(memory_space=pltpu.VMEM)
HBM = pl.BlockSpec(memory_space=pltpu.HBM)


def lane_index(rows):
    return lax.broadcasted_iota(jnp.int32, (rows, LANES), 1)


def turn_lanes(x, shift):
    return pltpu.roll(x, shift % LANES, 1)


def level_rows(row, depth):
    return pl.ds(row, depth, stride=ROWS)


def piece(ref, number, depth):
    return ref[number * depth : (number + 1) * depth, :]


def level(ref, number):
    return ref[number * ROWS : (number + 1) * ROWS, :]


def slab_place(number, field):
    if number < 32:
        return field, 4 * number
    return TAIL, 32 * field + 4 * (number - 32)


def fold_pack_kernel(temp, uvel, vvel, mask, out, half0, half1, half2, halfm, sems):
    depth = temp.shape[0]
    odd = lax.rem(lax.axis_index("lat"), 2)
    copies = []
    for number, (field, half) in enumerate(
        zip((temp, uvel, vvel, mask), (half0, half1, half2, halfm))
    ):
        copies.append(
            pltpu.make_async_copy(
                field.at[:, pl.ds(pl.multiple_of(odd * TILE, TILE), TILE), :],
                half.reshape(depth, TILE, LANES),
                sems.at[number],
            )
        )
    for copy in copies:
        copy.start()
    near = (TILE - 1) * odd
    far = near + 1 - 2 * odd
    keep = jnp.where(lax.axis_index("lat") == 0, 0.0, 1.0)
    for number, half in enumerate((half0, half1, half2)):
        copies[number].wait()
        base = 2 * depth * number
        out[base : base + depth, :] = half[pl.ds(near, depth, stride=TILE), :] * keep
        out[base + depth : base + 2 * depth, :] = half[pl.ds(far, depth, stride=TILE), :] * keep
    copies[3].wait()
    out[6 * depth : 7 * depth, :] = halfm[pl.ds(near, depth, stride=TILE), :].astype(jnp.float32) * keep


def pack_kernel(temp, uvel, vvel, mask, first, edges):
    depth = temp.shape[0] // ROWS
    odd = lax.rem(lax.axis_index("lat"), 2)
    near = (ROWS - 1) * (1 - odd)
    far = near + 2 * odd - 1
    for number, field in enumerate((temp, uvel, vvel)):
        base = 2 * depth * number
        first[base : base + depth, :] = field[level_rows(near, depth), :]
        first[base + depth : base + 2 * depth, :] = field[level_rows(far, depth), :]
    first[6 * depth : 7 * depth, :] = mask[level_rows(near, depth), :].astype(jnp.float32)
    group = lane_index(ROWS) // 4
    slabs = [jnp.zeros((ROWS, LANES), jnp.float32) for _ in range(TAIL + 1)]
    for number in range(depth):
        for index, field in enumerate((temp, uvel, vvel, mask)):
            block = level(field, number).astype(jnp.float32)
            slab, start = slab_place(number, index)
            slabs[slab] = jnp.where(group == start // 4, turn_lanes(block, start + 2), slabs[slab])
    for number, slab in enumerate(slabs):
        edges[number * ROWS : (number + 1) * ROWS, :] = slab


def interior_kernel(
    temp, uvel, vvel, mask, mixing, inv_dx, inv_dy, spread, coriolis, levels, prov, solve, middle
):
    depth = temp.shape[0] // ROWS
    half = depth // 2
    lane = lane_index(depth)
    active = levels[...]
    zero = jnp.zeros((ROWS, LANES), jnp.float32)

    def coupling(number):
        if 0 <= number < depth - 1:
            return jnp.where(number + 1 < active, level(mixing, number + 1), 0.0)
        return zero

    chains = [zero, zero]

    def factor(step):
        for side, number in enumerate((step, depth - 1 - step)):
            above, below = coupling(number - 1), coupling(number)
            done, left = (above, below) if side == 0 else (below, above)
            inverse = 1.0 / (1.0 + left + done * (1.0 - chains[side]))
            chains[side] = left * inverse
            here = slice(number * ROWS, (number + 1) * ROWS)
            solve[0, here, :] = inverse
            solve[1, here, :] = done * inverse
            solve[2, here, :] = chains[side]

    def rows_of(ref, row):
        return ref[level_rows(row, depth), :]

    def wet_of(row):
        return rows_of(mask, row).astype(jnp.float32)

    fields = (temp, uvel, vvel)
    steps = 0
    advect_south = [0.0] * 3
    spread_south = [0.0] * 3
    for row in range(ROWS):
        while steps < half and steps * ROWS <= row * half + half - 1:
            factor(steps)
            steps += 1
        one = slice(row, row + 1)
        scale = inv_dx[one, :]
        spread_x = spread[one, :] * scale * scale
        scale = scale * (-1.0 / 24.0)
        wet = wet_of(row)
        face_w = wet * jnp.where(lane >= 1, turn_lanes(wet, 1), 0.0)
        face_e = wet * jnp.where(lane < LANES - 1, turn_lanes(wet, -1), 0.0)
        u = rows_of(uvel, row)
        speed_w = scale * face_w * (turn_lanes(u, 1) + u)
        speed_e = scale * face_e * (turn_lanes(u, -1) + u)
        face_w = spread_x * face_w
        face_e = spread_x * face_e
        scale_y = inv_dy[one, :]
        spread_y = spread[one, :] * scale_y * scale_y
        scale_y = scale_y * (-1.0 / 24.0)
        if row + 1 < ROWS:
            face_n = wet * wet_of(row + 1)
            speed_n = face_n * (rows_of(vvel, row) + rows_of(vvel, row + 1))
        turn = wet * coriolis[one, :]
        for number, field in enumerate(fields):
            q = rows_of(field, row)
            west, east = turn_lanes(q, 1), turn_lanes(q, -1)
            value_w = 7.0 * (west + q) - (turn_lanes(q, 2) + east)
            value_e = 7.0 * (east + q) - (west + turn_lanes(q, -2))
            total = speed_e * value_e - speed_w * value_w + face_e * (east - q) - face_w * (q - west)
            if row + 1 < ROWS:
                north = rows_of(field, row + 1)
                outer = None
                if row >= 1:
                    outer = rows_of(field, row - 1)
                if row + 2 < ROWS:
                    beyond = rows_of(field, row + 2)
                    outer = beyond if outer is None else outer + beyond
                advect_north = speed_n * (7.0 * (q + north) - outer)
                spread_north = face_n * (north - q)
            else:
                advect_north, spread_north = 0.0, 0.0
            total = total + scale_y * (advect_north - advect_south[number])
            total = total + spread_y * (spread_north - spread_south[number])
            advect_south[number], spread_south[number] = advect_north, spread_north
            if number == 1:
                total = total + turn * rows_of(vvel, row)
            if number == 2:
                total = total - turn * u
            target = prov.at[number]
            target[level_rows(row, depth), :] = q + total
    while steps < half:
        factor(steps)
        steps += 1
    middle[...] = 1.0 / (1.0 - chains[0] * chains[1])


def add_row_ghosts(prov, mine, ghost, near, odd_sign, mask, inv_dy, spread, flip):
    depth = prov.shape[1] // ROWS
    far = near + odd_sign
    side = odd_sign.astype(jnp.float32)
    wet = piece(mine, 6, depth)
    face = piece(ghost, 6, depth) * wet
    face_next = wet * mask[level_rows(far, depth), :].astype(jnp.float32)
    inv0 = inv_dy[pl.ds(near, 1), :]
    inv1 = inv_dy[pl.ds(far, 1), :] * side
    mix0 = spread[pl.ds(near, 1), :] * inv0 * inv0
    inv0 = inv0 * side
    speed = face * (piece(ghost, 4, depth) * flip + piece(mine, 4, depth)) * (1.0 / 24.0)
    speed_next = face_next * (piece(mine, 4, depth) + piece(mine, 5, depth)) * (1.0 / 24.0)
    for number in range(3):
        sign = 1.0 if number == 0 else flip
        g0 = piece(ghost, 2 * number, depth) * sign
        g1 = piece(ghost, 2 * number + 1, depth) * sign
        o0 = piece(mine, 2 * number, depth)
        o1 = piece(mine, 2 * number + 1, depth)
        advect = speed * (7.0 * (g0 + o0) - (g1 + o1))
        reach = speed_next * g0
        view = prov.at[number]
        view[level_rows(near, depth), :] += inv0 * (advect + reach) + mix0 * (face * (g0 - o0))
        view[level_rows(far, depth), :] -= inv1 * reach


def ghosts_kernel(
    prov_in, sent1, got1, edges, east1, east2, mask, inv_dx, inv_dy, spread, prov
):
    depth = prov.shape[1] // ROWS
    odd = lax.rem(lax.axis_index("lat"), 2)
    lon_odd = lax.rem(lax.axis_index("lon"), 2) == 1
    lane = lane_index(ROWS)
    quad = lane % 4
    four = jnp.where(quad < 2, LANES - 2 + quad, quad - 2)

    def replicate(x):
        return jnp.take_along_axis(x, four, axis=1, mode="promise_in_bounds")

    wide = replicate(inv_dx[...])
    wide2 = replicate(spread[...]) * wide * wide
    own = [level(edges, s) for s in range(TAIL + 1)]
    first = [level(east1, s) for s in range(TAIL + 1)]
    second = [level(east2, s) for s in range(TAIL + 1)]
    west = [jnp.where(quad < 2, jnp.where(lon_odd, a, b), o) for a, b, o in zip(first, second, own)]
    east = [jnp.where(quad < 2, o, jnp.where(lon_odd, b, a)) for a, b, o in zip(first, second, own)]

    def split(slabs):
        tail = [slabs[TAIL] if f == 0 else turn_lanes(slabs[TAIL], -32 * f) for f in range(4)]
        return [slabs[:TAIL], tail]

    corrections = []
    for west_part, east_part, own_part in zip(split(west), split(east), split(own)):
        wet = west_part[3]
        face = turn_lanes(wet, 1) * wet
        speed = face * (turn_lanes(west_part[1], 1) + west_part[1]) * (1.0 / 24.0)
        speed_next = turn_lanes(speed, -1)
        wet_e = east_part[3]
        face_e = turn_lanes(wet_e, -1) * wet_e
        speed_e = face_e * (turn_lanes(east_part[1], -1) + east_part[1]) * (1.0 / 24.0)
        speed_e_before = turn_lanes(speed_e, 1)
        part = []
        for number in range(3):
            mine = own_part[number]
            q = west_part[number]
            back = turn_lanes(q, 1)
            advect = speed * (7.0 * (back + q) - (turn_lanes(q, 2) + turn_lanes(q, -1)))
            reach = speed_next * turn_lanes(q - mine, 1)
            near = wide * (advect + reach) - wide2 * (face * (q - back))
            distant = turn_lanes(reach, 1) * wide
            q = east_part[number]
            ahead = turn_lanes(q, -1)
            advect = speed_e * (7.0 * (ahead + q) - (turn_lanes(q, -2) + turn_lanes(q, 1)))
            reach = speed_e_before * turn_lanes(q - mine, -1)
            near_e = wide2 * (face_e * (ahead - q)) - wide * (advect + reach)
            distant_e = turn_lanes(reach, -1) * wide
            part.append(
                jnp.where(
                    quad < 2,
                    jnp.where(quad == 0, distant_e, near_e),
                    jnp.where(quad == 2, near, -distant),
                )
            )
        corrections.append(part)

    border = (lane < 2) | (lane >= LANES - 2)
    for number in range(depth):
        here = slice(number * ROWS, (number + 1) * ROWS)
        for field in range(3):
            if number < 32:
                source, start = corrections[0][field], 4 * number
            else:
                source, start = corrections[1][field], 4 * (number - 32)
            moved = jnp.where(border, turn_lanes(source, -(start + 2)), 0.0)
            prov[field, here, :] = prov_in[field, here, :] + moved
    add_row_ghosts(prov, sent1, got1, (ROWS - 1) * (1 - odd), 2 * odd - 1, mask, inv_dy, spread, 1.0)


def finish_kernel(
    prov_in, solve, middle, mine, ghost, mask, inv_dy, spread,
    temp_new, uvel_new, vvel_new, prov, work, turned, sems
):
    depth = prov.shape[1] // ROWS
    half = depth // 2
    odd = lax.rem(lax.axis_index("lat"), 2)
    fold = lax.axis_index("lat") == lax.axis_size("lat") - 1
    lane = lane_index(7 * depth)
    lane = jnp.where(fold, LANES - 1 - lane, lane)
    turned[...] = jnp.take_along_axis(ghost[...], lane, axis=1, mode="promise_in_bounds")
    flip = jnp.where(fold, -1.0, 1.0)
    add_row_ghosts(prov, mine, turned, (ROWS - 1) * odd, 1 - 2 * odd, mask, inv_dy, spread, flip)

    outs = (temp_new, uvel_new, vvel_new)
    zero = jnp.zeros((ROWS, LANES), jnp.float32)
    values = [[zero] * 3, [zero] * 3]
    for step in range(half):
        for side, number in enumerate((step, depth - 1 - step)):
            here = slice(number * ROWS, (number + 1) * ROWS)
            inverse, carry = solve[0, here, :], solve[1, here, :]
            for field in range(3):
                value = inverse * prov[field, here, :] + carry * values[side][field]
                values[side][field] = value
                work[field, here, :] = value
    above, below = half - 1, half
    gain = solve[2, above * ROWS : (above + 1) * ROWS, :]
    scale = middle[...]
    for field in range(3):
        top = scale * (values[0][field] + gain * values[1][field])
        values[1][field] = top
        values[0][field] = None
    tops = values[1]
    for field in range(3):
        work[field, above * ROWS : (above + 1) * ROWS, :] = tops[field]
    chains = [list(tops), list(tops)]
    copies = []
    for step in range(half):
        for side, number in enumerate((above - 1 - step, below + step)):
            if number < 0:
                continue
            here = slice(number * ROWS, (number + 1) * ROWS)
            gain = solve[2, here, :]
            for field in range(3):
                value = work[field, here, :] + gain * chains[side][field]
                chains[side][field] = value
                work[field, here, :] = value
        if step == half // 2 - 1:
            low, high = above - 1 - step, below + step + 1
            for field in range(3):
                rows = pl.ds(low * ROWS, (high - low) * ROWS)
                copies.append(
                    pltpu.make_async_copy(
                        work.at[field, rows, :], outs[field].at[rows, :], sems.at[field]
                    )
                )
                copies[-1].start()
    for field in range(3):
        for part, (start, stop) in enumerate(((0, low), (high, depth))):
            rows = pl.ds(start * ROWS, (stop - start) * ROWS)
            copies.append(
                pltpu.make_async_copy(
                    work.at[field, rows, :], outs[field].at[rows, :], sems.at[3 + 2 * field + part]
                )
            )
            copies[-1].start()
    for copy in copies:
        copy.wait()


def swaps(pairs):
    return [route for a, b in pairs for route in ((a, b), (b, a))]


def exchange_routes(lats, lons):
    def at(lat, lon):
        return lat * lons + lon % lons

    every = range(lons)
    lon_first = [(at(l, c), at(l, c + 1)) for l in range(lats) for c in range(0, lons, 2)]
    lon_second = [(at(l, c), at(l, c + 1)) for l in range(lats) for c in range(1, lons, 2)]
    lat_first = [(at(l, c), at(l + 1, c)) for l in range(0, lats, 2) for c in every]
    lat_second = [(at(l, c), at(l + 1, c)) for l in range(1, lats - 1, 2) for c in every]
    lat_second += [(at(lats - 1, c), at(lats - 1, lons - 1 - c)) for c in range(lons // 2)]
    lat_second += [(at(0, c), at(0, c + 1)) for c in range(0, lons, 2)]
    return [swaps(pairs) for pairs in (lon_first, lon_second, lat_first, lat_second)]


def per_device(
    temp, uvel, vvel, vert_mixing, inv_dx, inv_dy, horiz_mixing, coriolis, wet_mask, levels
):
    depth, rows, lanes = temp.shape
    assert (rows, lanes) == (ROWS, LANES) and depth == 40
    lats, lons = lax.axis_size("lat"), lax.axis_size("lon")
    assert lats % 2 == 0 and lons % 2 == 0
    flat = depth * rows

    def f32(*shape):
        return jax.ShapeDtypeStruct(shape, jnp.float32)

    def vmem(*shape, dtype=jnp.float32):
        return pltpu.VMEM(shape, dtype)

    limit = pltpu.CompilerParams(vmem_limit_bytes=16 << 20)
    both = ("lat", "lon")
    lon_first, lon_second, lat_first, lat_second = exchange_routes(lats, lons)
    sent2 = pl.pallas_call(
        fold_pack_kernel,
        name="fold_pack",
        out_shape=f32(7 * depth, lanes),
        in_specs=[HBM] * 4,
        out_specs=VMEM,
        scratch_shapes=[vmem(depth * TILE, lanes)] * 3
        + [vmem(depth * TILE, lanes, dtype=jnp.int32), pltpu.SemaphoreType.DMA((4,))],
        compiler_params=limit,
    )(temp, uvel, vvel, wet_mask)
    got2 = lax.ppermute(sent2, both, lat_second)
    temp, uvel, vvel, vert_mixing, wet_mask = (
        x.reshape(flat, lanes) for x in (temp, uvel, vvel, vert_mixing, wet_mask)
    )
    sent1, edges = pl.pallas_call(
        pack_kernel,
        name="pack",
        out_shape=(f32(7 * depth, lanes), f32((TAIL + 1) * rows, lanes)),
        in_specs=[VMEM] * 4,
        out_specs=(VMEM,) * 2,
        compiler_params=limit,
    )(temp, uvel, vvel, wet_mask)
    got1 = lax.ppermute(sent1, both, lat_first)
    east2 = lax.ppermute(edges, both, lon_second)
    east1 = lax.ppermute(edges, both, lon_first)
    prov, solve, middle = pl.pallas_call(
        interior_kernel,
        name="interior",
        out_shape=(f32(3, flat, lanes), f32(3, flat, lanes), f32(rows, lanes)),
        in_specs=[VMEM] * 10,
        out_specs=(VMEM,) * 3,
        compiler_params=limit,
        cost_estimate=pl.CostEstimate(flops=20_000_000, bytes_accessed=6_000_000, transcendentals=0),
    )(temp, uvel, vvel, wet_mask, vert_mixing, inv_dx, inv_dy, horiz_mixing, coriolis, levels)
    prov = pl.pallas_call(
        ghosts_kernel,
        name="ghosts",
        out_shape=f32(3, flat, lanes),
        in_specs=[VMEM] * 10,
        out_specs=VMEM,
        input_output_aliases={0: 0},
        compiler_params=limit,
    )(prov, sent1, got1, edges, east1, east2, wet_mask, inv_dx, inv_dy, horiz_mixing)
    outs = pl.pallas_call(
        finish_kernel,
        name="finish",
        out_shape=(f32(flat, lanes),) * 3 + (f32(3, flat, lanes),),
        in_specs=[VMEM] * 8,
        out_specs=(HBM,) * 3 + (VMEM,),
        input_output_aliases={0: 3},
        scratch_shapes=[
            vmem(3, flat, lanes),
            vmem(7 * depth, lanes),
            pltpu.SemaphoreType.DMA((9,)),
        ],
        compiler_params=limit,
    )(prov, solve, middle, sent2, got2, wet_mask, inv_dy, horiz_mixing)
    return tuple(x.reshape(depth, rows, lanes) for x in outs[:3])


def solution(mesh):
    field, plane = P(None, "lat", "lon"), P("lat", "lon")
    return jax.shard_map(
        per_device,
        mesh=mesh,
        in_specs=(field,) * 4 + (plane,) * 4 + (field, plane),
        out_specs=(field,) * 3,
        check_vma=False,
    )
```

```python
import jax
import jax.numpy as jnp
from jax import lax
from jax.experimental import pallas as pl
from jax.experimental.pallas import tpu as pltpu
from jax.sharding import PartitionSpec as P

ROWS = 16
LANES = 128
TILE = 8
TAIL = 4
VMEM = pl.BlockSpec(memory_space=pltpu.VMEM)
HBM = pl.BlockSpec(memory_space=pltpu.HBM)


def lane_index(rows):
    return lax.broadcasted_iota(jnp.int32, (rows, LANES), 1)


def turn_lanes(x, shift):
    return pltpu.roll(x, shift % LANES, 1)


def level_rows(row, depth):
    return pl.ds(row, depth, stride=ROWS)


def piece(ref, number, depth):
    return ref[number * depth : (number + 1) * depth, :]


def level(ref, number):
    return ref[number * ROWS : (number + 1) * ROWS, :]


def slab_place(number, field):
    if number < 32:
        return field, 4 * number
    return TAIL, 32 * field + 4 * (number - 32)


def edges_kernel(
    temp_hbm, uvel_hbm, vvel_hbm, mask_hbm, temp, uvel, vvel, mask, first, second, edges, raw, sems
):
    depth = temp.shape[0] // ROWS
    odd = lax.rem(lax.axis_index("lat"), 2)
    sources = (temp_hbm, uvel_hbm, vvel_hbm, mask_hbm)
    copies = [
        pltpu.make_async_copy(source, target.reshape(depth, ROWS, LANES), sems.at[number])
        for number, (source, target) in enumerate(zip(sources, (temp, uvel, vvel, raw)))
    ]
    for copy in copies:
        copy.start()
    keep = jnp.where(lax.axis_index("lat") == 0, 0.0, 1.0)
    group = lane_index(ROWS) // 4
    slabs = [jnp.zeros((ROWS, LANES), jnp.float32) for _ in range(TAIL + 1)]
    for index, field in enumerate((temp, uvel, vvel, mask)):
        copies[index].wait()
        if index == 3:
            mask[...] = raw[...].astype(jnp.float32)
        for out, near in ((second, (ROWS - 1) * odd), (first, (ROWS - 1) * (1 - odd))):
            far = near + jnp.where(near == 0, 1, -1)
            factor = keep if out is second else 1.0
            base = 2 * depth * index
            out[base : base + depth, :] = field[level_rows(near, depth), :] * factor
            if index < 3:
                out[base + depth : base + 2 * depth, :] = field[level_rows(far, depth), :] * factor
        for number in range(depth):
            slab, start = slab_place(number, index)
            moved = turn_lanes(level(field, number), start + 2)
            slabs[slab] = jnp.where(group == start // 4, moved, slabs[slab])
    for number, slab in enumerate(slabs):
        edges[number * ROWS : (number + 1) * ROWS, :] = slab


def interior_kernel(
    temp, uvel, vvel, mask, mixing, inv_dx, inv_dy, spread, coriolis, levels, prov, solve, middle
):
    depth = temp.shape[0] // ROWS
    half = depth // 2
    lane = lane_index(depth)
    active = levels[...]
    zero = jnp.zeros((ROWS, LANES), jnp.float32)

    def coupling(number):
        if 0 <= number < depth - 1:
            return jnp.where(number + 1 < active, level(mixing, number + 1), 0.0)
        return zero

    chains = [zero, zero]

    def factor(step):
        for side, number in enumerate((step, depth - 1 - step)):
            above, below = coupling(number - 1), coupling(number)
            done, left = (above, below) if side == 0 else (below, above)
            inverse = 1.0 / (1.0 + left + done * (1.0 - chains[side]))
            chains[side] = left * inverse
            here = slice(number * ROWS, (number + 1) * ROWS)
            solve[0, here, :] = inverse
            solve[1, here, :] = done * inverse
            solve[2, here, :] = chains[side]

    def rows_of(ref, row):
        return ref[level_rows(row, depth), :]

    fields = (temp, uvel, vvel)
    steps = 0
    advect_south = [0.0] * 3
    spread_south = [0.0] * 3
    for row in range(ROWS):
        while steps < half and steps * ROWS <= row * half + half - 1:
            factor(steps)
            steps += 1
        one = slice(row, row + 1)
        scale = inv_dx[one, :]
        spread_x = spread[one, :] * scale * scale
        scale = scale * (-1.0 / 24.0)
        wet = rows_of(mask, row)
        face_w = wet * jnp.where(lane >= 1, turn_lanes(wet, 1), 0.0)
        face_e = wet * jnp.where(lane < LANES - 1, turn_lanes(wet, -1), 0.0)
        u = rows_of(uvel, row)
        speed_w = scale * face_w * (turn_lanes(u, 1) + u)
        speed_e = scale * face_e * (turn_lanes(u, -1) + u)
        face_w = spread_x * face_w
        face_e = spread_x * face_e
        scale_y = inv_dy[one, :]
        spread_y = spread[one, :] * scale_y * scale_y
        scale_y = scale_y * (-1.0 / 24.0)
        if row + 1 < ROWS:
            face_n = wet * rows_of(mask, row + 1)
            speed_n = face_n * (rows_of(vvel, row) + rows_of(vvel, row + 1))
        turn = wet * coriolis[one, :]
        for number, field in enumerate(fields):
            q = rows_of(field, row)
            west, east = turn_lanes(q, 1), turn_lanes(q, -1)
            value_w = 7.0 * (west + q) - (turn_lanes(q, 2) + east)
            value_e = 7.0 * (east + q) - (west + turn_lanes(q, -2))
            total = speed_e * value_e - speed_w * value_w + face_e * (east - q) - face_w * (q - west)
            if row + 1 < ROWS:
                north = rows_of(field, row + 1)
                outer = None
                if row >= 1:
                    outer = rows_of(field, row - 1)
                if row + 2 < ROWS:
                    beyond = rows_of(field, row + 2)
                    outer = beyond if outer is None else outer + beyond
                advect_north = speed_n * (7.0 * (q + north) - outer)
                spread_north = face_n * (north - q)
            else:
                advect_north, spread_north = 0.0, 0.0
            total = total + scale_y * (advect_north - advect_south[number])
            total = total + spread_y * (spread_north - spread_south[number])
            advect_south[number], spread_south[number] = advect_north, spread_north
            if number == 1:
                total = total + turn * rows_of(vvel, row)
            if number == 2:
                total = total - turn * u
            target = prov.at[number]
            target[level_rows(row, depth), :] = q + total
    while steps < half:
        factor(steps)
        steps += 1
    middle[...] = 1.0 / (1.0 - chains[0] * chains[1])


def add_row_ghosts(prov, mine, ghost, near, odd_sign, mask, inv_dy, spread, flip):
    depth = prov.shape[1] // ROWS
    far = near + odd_sign
    side = odd_sign.astype(jnp.float32)
    wet = piece(mine, 6, depth)
    face = piece(ghost, 6, depth) * wet
    face_next = wet * mask[level_rows(far, depth), :]
    inv0 = inv_dy[pl.ds(near, 1), :]
    inv1 = inv_dy[pl.ds(far, 1), :] * side
    mix0 = spread[pl.ds(near, 1), :] * inv0 * inv0
    inv0 = inv0 * side
    speed = face * (piece(ghost, 4, depth) * flip + piece(mine, 4, depth)) * (1.0 / 24.0)
    speed_next = face_next * (piece(mine, 4, depth) + piece(mine, 5, depth)) * (1.0 / 24.0)
    for number in range(3):
        sign = 1.0 if number == 0 else flip
        g0 = piece(ghost, 2 * number, depth) * sign
        g1 = piece(ghost, 2 * number + 1, depth) * sign
        o0 = piece(mine, 2 * number, depth)
        o1 = piece(mine, 2 * number + 1, depth)
        advect = speed * (7.0 * (g0 + o0) - (g1 + o1))
        reach = speed_next * g0
        view = prov.at[number]
        view[level_rows(near, depth), :] += inv0 * (advect + reach) + mix0 * (face * (g0 - o0))
        view[level_rows(far, depth), :] -= inv1 * reach


def ghosts_kernel(
    prov_in, sent1, got1, edges, east1, east2, mask, inv_dx, inv_dy, spread, prov
):
    depth = prov.shape[1] // ROWS
    odd = lax.rem(lax.axis_index("lat"), 2)
    lon_odd = lax.rem(lax.axis_index("lon"), 2) == 1
    lane = lane_index(ROWS)
    quad = lane % 4
    four = jnp.where(quad < 2, LANES - 2 + quad, quad - 2)

    def replicate(x):
        return jnp.take_along_axis(x, four, axis=1, mode="promise_in_bounds")

    wide = replicate(inv_dx[...])
    wide2 = replicate(spread[...]) * wide * wide
    own = [level(edges, s) for s in range(TAIL + 1)]
    first = [level(east1, s) for s in range(TAIL + 1)]
    second = [level(east2, s) for s in range(TAIL + 1)]
    west = [jnp.where(quad < 2, jnp.where(lon_odd, a, b), o) for a, b, o in zip(first, second, own)]
    east = [jnp.where(quad < 2, o, jnp.where(lon_odd, b, a)) for a, b, o in zip(first, second, own)]

    def split(slabs):
        tail = [slabs[TAIL] if f == 0 else turn_lanes(slabs[TAIL], -32 * f) for f in range(4)]
        return [slabs[:TAIL], tail]

    corrections = []
    for west_part, east_part, own_part in zip(split(west), split(east), split(own)):
        wet = west_part[3]
        face = turn_lanes(wet, 1) * wet
        speed = face * (turn_lanes(west_part[1], 1) + west_part[1]) * (1.0 / 24.0)
        speed_next = turn_lanes(speed, -1)
        wet_e = east_part[3]
        face_e = turn_lanes(wet_e, -1) * wet_e
        speed_e = face_e * (turn_lanes(east_part[1], -1) + east_part[1]) * (1.0 / 24.0)
        speed_e_before = turn_lanes(speed_e, 1)
        part = []
        for number in range(3):
            mine = own_part[number]
            q = west_part[number]
            back = turn_lanes(q, 1)
            advect = speed * (7.0 * (back + q) - (turn_lanes(q, 2) + turn_lanes(q, -1)))
            reach = speed_next * turn_lanes(q - mine, 1)
            near = wide * (advect + reach) - wide2 * (face * (q - back))
            distant = turn_lanes(reach, 1) * wide
            q = east_part[number]
            ahead = turn_lanes(q, -1)
            advect = speed_e * (7.0 * (ahead + q) - (turn_lanes(q, -2) + turn_lanes(q, 1)))
            reach = speed_e_before * turn_lanes(q - mine, -1)
            near_e = wide2 * (face_e * (ahead - q)) - wide * (advect + reach)
            distant_e = turn_lanes(reach, -1) * wide
            part.append(
                jnp.where(
                    quad < 2,
                    jnp.where(quad == 0, distant_e, near_e),
                    jnp.where(quad == 2, near, -distant),
                )
            )
        corrections.append(part)

    border = (lane < 2) | (lane >= LANES - 2)
    for number in range(depth):
        here = slice(number * ROWS, (number + 1) * ROWS)
        for field in range(3):
            if number < 32:
                source, start = corrections[0][field], 4 * number
            else:
                source, start = corrections[1][field], 4 * (number - 32)
            moved = jnp.where(border, turn_lanes(source, -(start + 2)), 0.0)
            prov[field, here, :] = prov_in[field, here, :] + moved
    add_row_ghosts(prov, sent1, got1, (ROWS - 1) * (1 - odd), 2 * odd - 1, mask, inv_dy, spread, 1.0)


def finish_kernel(
    prov_in, solve, middle, mine, ghost, mask, inv_dy, spread,
    temp_new, uvel_new, vvel_new, prov, work, turned, sems
):
    depth = prov.shape[1] // ROWS
    half = depth // 2
    odd = lax.rem(lax.axis_index("lat"), 2)
    fold = lax.axis_index("lat") == lax.axis_size("lat") - 1
    lane = lane_index(7 * depth)
    lane = jnp.where(fold, LANES - 1 - lane, lane)
    turned[...] = jnp.take_along_axis(ghost[...], lane, axis=1, mode="promise_in_bounds")
    flip = jnp.where(fold, -1.0, 1.0)
    add_row_ghosts(prov, mine, turned, (ROWS - 1) * odd, 1 - 2 * odd, mask, inv_dy, spread, flip)

    outs = (temp_new, uvel_new, vvel_new)
    zero = jnp.zeros((ROWS, LANES), jnp.float32)
    values = [[zero] * 3, [zero] * 3]
    for step in range(half):
        for side, number in enumerate((step, depth - 1 - step)):
            here = slice(number * ROWS, (number + 1) * ROWS)
            inverse, carry = solve[0, here, :], solve[1, here, :]
            for field in range(3):
                value = inverse * prov[field, here, :] + carry * values[side][field]
                values[side][field] = value
                work[field, here, :] = value
    above, below = half - 1, half
    gain = solve[2, above * ROWS : (above + 1) * ROWS, :]
    scale = middle[...]
    for field in range(3):
        top = scale * (values[0][field] + gain * values[1][field])
        values[1][field] = top
        values[0][field] = None
    tops = values[1]
    for field in range(3):
        work[field, above * ROWS : (above + 1) * ROWS, :] = tops[field]
    chains = [list(tops), list(tops)]
    copies = []
    for step in range(half):
        for side, number in enumerate((above - 1 - step, below + step)):
            if number < 0:
                continue
            here = slice(number * ROWS, (number + 1) * ROWS)
            gain = solve[2, here, :]
            for field in range(3):
                value = work[field, here, :] + gain * chains[side][field]
                chains[side][field] = value
                work[field, here, :] = value
        if step == half // 2 - 1:
            low, high = above - 1 - step, below + step + 1
            for field in range(3):
                rows = pl.ds(low * ROWS, (high - low) * ROWS)
                copies.append(
                    pltpu.make_async_copy(
                        work.at[field, rows, :], outs[field].at[rows, :], sems.at[field]
                    )
                )
                copies[-1].start()
    for field in range(3):
        for part, (start, stop) in enumerate(((0, low), (high, depth))):
            rows = pl.ds(start * ROWS, (stop - start) * ROWS)
            copies.append(
                pltpu.make_async_copy(
                    work.at[field, rows, :], outs[field].at[rows, :], sems.at[3 + 2 * field + part]
                )
            )
            copies[-1].start()
    for copy in copies:
        copy.wait()


def swaps(pairs):
    return [route for a, b in pairs for route in ((a, b), (b, a))]


def exchange_routes(lats, lons):
    def at(lat, lon):
        return lat * lons + lon % lons

    every = range(lons)
    lon_first = [(at(l, c), at(l, c + 1)) for l in range(lats) for c in range(0, lons, 2)]
    lon_second = [(at(l, c), at(l, c + 1)) for l in range(lats) for c in range(1, lons, 2)]
    lat_first = [(at(l, c), at(l + 1, c)) for l in range(0, lats, 2) for c in every]
    lat_second = [(at(l, c), at(l + 1, c)) for l in range(1, lats - 1, 2) for c in every]
    lat_second += [(at(lats - 1, c), at(lats - 1, lons - 1 - c)) for c in range(lons // 2)]
    lat_second += [(at(0, c), at(0, c + 1)) for c in range(0, lons, 2)]
    return [swaps(pairs) for pairs in (lon_first, lon_second, lat_first, lat_second)]


def per_device(
    temp, uvel, vvel, vert_mixing, inv_dx, inv_dy, horiz_mixing, coriolis, wet_mask, levels
):
    depth, rows, lanes = temp.shape
    assert (rows, lanes) == (ROWS, LANES) and depth == 40
    lats, lons = lax.axis_size("lat"), lax.axis_size("lon")
    assert lats % 2 == 0 and lons % 2 == 0
    flat = depth * rows

    def f32(*shape):
        return jax.ShapeDtypeStruct(shape, jnp.float32)

    def vmem(*shape, dtype=jnp.float32):
        return pltpu.VMEM(shape, dtype)

    limit = pltpu.CompilerParams(vmem_limit_bytes=16 << 20)
    both = ("lat", "lon")
    lon_first, lon_second, lat_first, lat_second = exchange_routes(lats, lons)
    inputs = [pltpu.with_memory_space_constraint(x, pltpu.HBM) for x in (temp, uvel, vvel, wet_mask)]
    temp, uvel, vvel, wet, sent1, sent2, edges = pl.pallas_call(
        edges_kernel,
        name="edges",
        out_shape=(f32(flat, lanes),) * 4
        + (f32(7 * depth, lanes),) * 2
        + (f32((TAIL + 1) * rows, lanes),),
        in_specs=[HBM] * 4,
        out_specs=(VMEM,) * 7,
        scratch_shapes=[vmem(flat, lanes, dtype=jnp.int32), pltpu.SemaphoreType.DMA((4,))],
        compiler_params=limit,
    )(*inputs)
    vert_mixing = vert_mixing.reshape(flat, lanes)
    got2 = lax.ppermute(sent2, both, lat_second)
    got1 = lax.ppermute(sent1, both, lat_first)
    east2 = lax.ppermute(edges, both, lon_second)
    east1 = lax.ppermute(edges, both, lon_first)
    prov, solve, middle = pl.pallas_call(
        interior_kernel,
        name="interior",
        out_shape=(f32(3, flat, lanes), f32(3, flat, lanes), f32(rows, lanes)),
        in_specs=[VMEM] * 10,
        out_specs=(VMEM,) * 3,
        compiler_params=limit,
        cost_estimate=pl.CostEstimate(flops=20_000_000, bytes_accessed=6_000_000, transcendentals=0),
    )(temp, uvel, vvel, wet, vert_mixing, inv_dx, inv_dy, horiz_mixing, coriolis, levels)
    prov = pl.pallas_call(
        ghosts_kernel,
        name="ghosts",
        out_shape=f32(3, flat, lanes),
        in_specs=[VMEM] * 10,
        out_specs=VMEM,
        input_output_aliases={0: 0},
        compiler_params=limit,
    )(prov, sent1, got1, edges, east1, east2, wet, inv_dx, inv_dy, horiz_mixing)
    outs = pl.pallas_call(
        finish_kernel,
        name="finish",
        out_shape=(f32(flat, lanes),) * 3 + (f32(3, flat, lanes),),
        in_specs=[VMEM] * 8,
        out_specs=(HBM,) * 3 + (VMEM,),
        input_output_aliases={0: 3},
        scratch_shapes=[
            vmem(3, flat, lanes),
            vmem(7 * depth, lanes),
            pltpu.SemaphoreType.DMA((9,)),
        ],
        compiler_params=limit,
    )(prov, solve, middle, sent2, got2, wet, inv_dy, horiz_mixing)
    return tuple(x.reshape(depth, rows, lanes) for x in outs[:3])


def solution(mesh):
    field, plane = P(None, "lat", "lon"), P("lat", "lon")
    return jax.shard_map(
        per_device,
        mesh=mesh,
        in_specs=(field,) * 4 + (plane,) * 4 + (field, plane),
        out_specs=(field,) * 3,
        check_vma=False,
    )
```

```python
import jax
import jax.numpy as jnp
from jax import lax
from jax.experimental import pallas as pl
from jax.experimental.pallas import tpu as pltpu
from jax.sharding import PartitionSpec as P

ROWS = 16
LANES = 128
TILE = 8
TAIL = 4
VMEM = pl.BlockSpec(memory_space=pltpu.VMEM)
HBM = pl.BlockSpec(memory_space=pltpu.HBM)


def lane_index(rows):
    return lax.broadcasted_iota(jnp.int32, (rows, LANES), 1)


def turn_lanes(x, shift):
    return pltpu.roll(x, shift % LANES, 1)


def level_rows(row, depth):
    return pl.ds(row, depth, stride=ROWS)


def piece(ref, number, depth):
    return ref[number * depth : (number + 1) * depth, :]


def level(ref, number):
    return ref[number * ROWS : (number + 1) * ROWS, :]


def slab_place(number, field):
    if number < 32:
        return field, 4 * number
    return TAIL, 32 * field + 4 * (number - 32)


def fold_pack_kernel(temp, uvel, vvel, mask, out, half0, half1, half2, halfm, sems):
    depth = temp.shape[0]
    odd = lax.rem(lax.axis_index("lat"), 2)
    copies = []
    for number, (field, half) in enumerate(
        zip((temp, uvel, vvel, mask), (half0, half1, half2, halfm))
    ):
        copies.append(
            pltpu.make_async_copy(
                field.at[:, pl.ds(pl.multiple_of(odd * TILE, TILE), TILE), :],
                half.reshape(depth, TILE, LANES),
                sems.at[number],
            )
        )
    for copy in copies:
        copy.start()
    near = (TILE - 1) * odd
    far = near + 1 - 2 * odd
    keep = jnp.where(lax.axis_index("lat") == 0, 0.0, 1.0)
    for number, half in enumerate((half0, half1, half2)):
        copies[number].wait()
        base = 2 * depth * number
        out[base : base + depth, :] = half[pl.ds(near, depth, stride=TILE), :] * keep
        out[base + depth : base + 2 * depth, :] = half[pl.ds(far, depth, stride=TILE), :] * keep
    copies[3].wait()
    out[6 * depth : 7 * depth, :] = halfm[pl.ds(near, depth, stride=TILE), :].astype(jnp.float32) * keep
    out[7 * depth :, :] = jnp.zeros((TILE, LANES), jnp.float32)


def rows_pack_kernel(temp, uvel, vvel, mask, after, first):
    depth = temp.shape[0] // ROWS
    odd = lax.rem(lax.axis_index("lat"), 2)
    near = (ROWS - 1) * (1 - odd)
    far = near + 2 * odd - 1
    for number, field in enumerate((temp, uvel, vvel)):
        base = 2 * depth * number
        first[base : base + depth, :] = field[level_rows(near, depth), :]
        first[base + depth : base + 2 * depth, :] = field[level_rows(far, depth), :]
    first[6 * depth : 7 * depth, :] = mask[level_rows(near, depth), :].astype(jnp.float32)


def columns_kernel(temp, uvel, vvel, mask, mixing, levels, edges, longer, solve, middle):
    depth = temp.shape[0] // ROWS
    half = depth // 2
    active = levels[...]
    zero = jnp.zeros((ROWS, LANES), jnp.float32)

    def coupling(number):
        if 0 <= number < depth - 1:
            return jnp.where(number + 1 < active, level(mixing, number + 1), 0.0)
        return zero

    group = lane_index(ROWS) // 4
    slabs = [zero] * (TAIL + 1)
    chains = [zero, zero]
    for step in range(half):
        for side, number in enumerate((step, depth - 1 - step)):
            above, below = coupling(number - 1), coupling(number)
            done, left = (above, below) if side == 0 else (below, above)
            inverse = 1.0 / (1.0 + left + done * (1.0 - chains[side]))
            chains[side] = left * inverse
            here = slice(number * ROWS, (number + 1) * ROWS)
            solve[0, here, :] = inverse
            solve[1, here, :] = done * inverse
            solve[2, here, :] = chains[side]
            for index, field in enumerate((temp, uvel, vvel, mask)):
                block = level(field, number).astype(jnp.float32)
                slab, start = slab_place(number, index)
                moved = turn_lanes(block, start + 2)
                slabs[slab] = jnp.where(group == start // 4, moved, slabs[slab])
    middle[...] = 1.0 / (1.0 - chains[0] * chains[1])
    for number, slab in enumerate(slabs):
        edges[number * ROWS : (number + 1) * ROWS, :] = slab
        longer[number * ROWS : (number + 1) * ROWS, :] = slab
    longer[(TAIL + 1) * ROWS :, :] = jnp.zeros((TILE, LANES), jnp.float32)


def interior_kernel(
    temp, uvel, vvel, mask, inv_dx, inv_dy, spread, coriolis, prov
):
    depth = temp.shape[0] // ROWS
    lane = lane_index(depth)

    def rows_of(ref, row):
        return ref[level_rows(row, depth), :]

    def wet_of(row):
        return rows_of(mask, row).astype(jnp.float32)

    fields = (temp, uvel, vvel)
    advect_south = [0.0] * 3
    spread_south = [0.0] * 3
    for row in range(ROWS):
        one = slice(row, row + 1)
        scale = inv_dx[one, :]
        spread_x = spread[one, :] * scale * scale
        scale = scale * (-1.0 / 24.0)
        wet = wet_of(row)
        face_w = wet * jnp.where(lane >= 1, turn_lanes(wet, 1), 0.0)
        face_e = wet * jnp.where(lane < LANES - 1, turn_lanes(wet, -1), 0.0)
        u = rows_of(uvel, row)
        speed_w = scale * face_w * (turn_lanes(u, 1) + u)
        speed_e = scale * face_e * (turn_lanes(u, -1) + u)
        face_w = spread_x * face_w
        face_e = spread_x * face_e
        scale_y = inv_dy[one, :]
        spread_y = spread[one, :] * scale_y * scale_y
        scale_y = scale_y * (-1.0 / 24.0)
        if row + 1 < ROWS:
            face_n = wet * wet_of(row + 1)
            speed_n = face_n * (rows_of(vvel, row) + rows_of(vvel, row + 1))
        turn = wet * coriolis[one, :]
        for number, field in enumerate(fields):
            q = rows_of(field, row)
            west, east = turn_lanes(q, 1), turn_lanes(q, -1)
            value_w = 7.0 * (west + q) - (turn_lanes(q, 2) + east)
            value_e = 7.0 * (east + q) - (west + turn_lanes(q, -2))
            total = speed_e * value_e - speed_w * value_w + face_e * (east - q) - face_w * (q - west)
            if row + 1 < ROWS:
                north = rows_of(field, row + 1)
                outer = None
                if row >= 1:
                    outer = rows_of(field, row - 1)
                if row + 2 < ROWS:
                    beyond = rows_of(field, row + 2)
                    outer = beyond if outer is None else outer + beyond
                advect_north = speed_n * (7.0 * (q + north) - outer)
                spread_north = face_n * (north - q)
            else:
                advect_north, spread_north = 0.0, 0.0
            total = total + scale_y * (advect_north - advect_south[number])
            total = total + spread_y * (spread_north - spread_south[number])
            advect_south[number], spread_south[number] = advect_north, spread_north
            if number == 1:
                total = total + turn * rows_of(vvel, row)
            if number == 2:
                total = total - turn * u
            target = prov.at[number]
            target[level_rows(row, depth), :] = q + total


def add_row_ghosts(prov, mine, ghost, near, odd_sign, mask, inv_dy, spread, flip):
    depth = prov.shape[1] // ROWS
    far = near + odd_sign
    side = odd_sign.astype(jnp.float32)
    wet = piece(mine, 6, depth)
    face = piece(ghost, 6, depth) * wet
    face_next = wet * mask[level_rows(far, depth), :].astype(jnp.float32)
    inv0 = inv_dy[pl.ds(near, 1), :]
    inv1 = inv_dy[pl.ds(far, 1), :] * side
    mix0 = spread[pl.ds(near, 1), :] * inv0 * inv0
    inv0 = inv0 * side
    speed = face * (piece(ghost, 4, depth) * flip + piece(mine, 4, depth)) * (1.0 / 24.0)
    speed_next = face_next * (piece(mine, 4, depth) + piece(mine, 5, depth)) * (1.0 / 24.0)
    for number in range(3):
        sign = 1.0 if number == 0 else flip
        g0 = piece(ghost, 2 * number, depth) * sign
        g1 = piece(ghost, 2 * number + 1, depth) * sign
        o0 = piece(mine, 2 * number, depth)
        o1 = piece(mine, 2 * number + 1, depth)
        advect = speed * (7.0 * (g0 + o0) - (g1 + o1))
        reach = speed_next * g0
        view = prov.at[number]
        view[level_rows(near, depth), :] += inv0 * (advect + reach) + mix0 * (face * (g0 - o0))
        view[level_rows(far, depth), :] -= inv1 * reach


def column_ghosts(edges, other, west, inv_dx, spread):
    quad = lane_index(ROWS) % 4
    four = jnp.where(quad < 2, LANES - 2 + quad, quad - 2)
    side = jnp.where(west, 1, -1)

    def toward(x, count):
        return pltpu.roll(x, lax.rem(side * count + LANES, LANES), 1)

    def replicate(x):
        return jnp.take_along_axis(x, four, axis=1, mode="promise_in_bounds")

    wide = replicate(inv_dx[...])
    wide2 = replicate(spread[...]) * wide * wide
    wide = wide * side.astype(jnp.float32)
    own = [level(edges, s) for s in range(TAIL + 1)]
    ghost = quad * side < jnp.where(west, 2, -1)
    both = [jnp.where(ghost, level(other, s), own[s]) for s in range(TAIL + 1)]
    near_lane = quad == jnp.where(west, 2, 1)

    def split(slabs):
        tail = [slabs[TAIL] if f == 0 else turn_lanes(slabs[TAIL], -32 * f) for f in range(4)]
        return [slabs[:TAIL], tail]

    corrections = []
    for part, mine in zip(split(both), split(own)):
        face = toward(part[3], 1) * part[3]
        speed = face * (toward(part[1], 1) + part[1]) * (1.0 / 24.0)
        speed_next = toward(speed, -1)
        result = []
        for number in range(3):
            q = part[number]
            ahead = toward(q, 1)
            advect = speed * (7.0 * (ahead + q) - (toward(q, 2) + toward(q, -1)))
            reach = speed_next * toward(q - mine[number], 1)
            near = wide * (advect + reach) + wide2 * (face * (ahead - q))
            result.append(jnp.where(near_lane, near, -wide * toward(reach, 1)))
        corrections.append(result)
    return corrections


def border_of(west):
    lane = lane_index(ROWS)
    return jnp.where(west, lane, LANES - 1 - lane) < 2


def border_part(corrections, border, number, field):
    if number < 32:
        source, start = corrections[0][field], 4 * number
    else:
        source, start = corrections[1][field], 4 * (number - 32)
    return jnp.where(border, turn_lanes(source, -(start + 2)), 0.0)


def ghosts_kernel(prov_in, sent1, got1, edges, other, mask, inv_dx, inv_dy, spread, prov):
    depth = prov.shape[1] // ROWS
    odd = lax.rem(lax.axis_index("lat"), 2)
    west = lax.rem(lax.axis_index("lon"), 2) == 1
    corrections = column_ghosts(edges, other, west, inv_dx, spread)
    border = border_of(west)
    for number in range(depth):
        here = slice(number * ROWS, (number + 1) * ROWS)
        for field in range(3):
            moved = border_part(corrections, border, number, field)
            prov[field, here, :] = prov_in[field, here, :] + moved
    add_row_ghosts(prov, sent1, got1, (ROWS - 1) * (1 - odd), 2 * odd - 1, mask, inv_dy, spread, 1.0)


def finish_kernel(
    prov_in, solve, middle, mine, ghost, edges, other, mask, inv_dx, inv_dy, spread,
    temp_new, uvel_new, vvel_new, prov, work, turned, sems
):
    depth = prov.shape[1] // ROWS
    half = depth // 2
    odd = lax.rem(lax.axis_index("lat"), 2)
    fold = lax.axis_index("lat") == lax.axis_size("lat") - 1
    lane = lane_index(7 * depth)
    lane = jnp.where(fold, LANES - 1 - lane, lane)
    turned[...] = jnp.take_along_axis(ghost[: 7 * depth, :], lane, axis=1, mode="promise_in_bounds")
    flip = jnp.where(fold, -1.0, 1.0)
    add_row_ghosts(prov, mine, turned, (ROWS - 1) * odd, 1 - 2 * odd, mask, inv_dy, spread, flip)

    west = lax.rem(lax.axis_index("lon"), 2) == 0
    corrections = column_ghosts(edges, other, west, inv_dx, spread)
    border = border_of(west)

    outs = (temp_new, uvel_new, vvel_new)
    zero = jnp.zeros((ROWS, LANES), jnp.float32)
    values = [[zero] * 3, [zero] * 3]
    for step in range(half):
        for side, number in enumerate((step, depth - 1 - step)):
            here = slice(number * ROWS, (number + 1) * ROWS)
            inverse, carry = solve[0, here, :], solve[1, here, :]
            for field in range(3):
                known = prov[field, here, :] + border_part(corrections, border, number, field)
                value = inverse * known + carry * values[side][field]
                values[side][field] = value
                work[field, here, :] = value
    above, below = half - 1, half
    gain = solve[2, above * ROWS : (above + 1) * ROWS, :]
    scale = middle[...]
    for field in range(3):
        top = scale * (values[0][field] + gain * values[1][field])
        values[1][field] = top
        values[0][field] = None
    tops = values[1]
    for field in range(3):
        work[field, above * ROWS : (above + 1) * ROWS, :] = tops[field]
    chains = [list(tops), list(tops)]
    copies = []
    for step in range(half):
        for side, number in enumerate((above - 1 - step, below + step)):
            if number < 0:
                continue
            here = slice(number * ROWS, (number + 1) * ROWS)
            gain = solve[2, here, :]
            for field in range(3):
                value = work[field, here, :] + gain * chains[side][field]
                chains[side][field] = value
                work[field, here, :] = value
        if step == half // 2 - 1:
            low, high = above - 1 - step, below + step + 1
            for field in range(3):
                rows = pl.ds(low * ROWS, (high - low) * ROWS)
                copies.append(
                    pltpu.make_async_copy(
                        work.at[field, rows, :], outs[field].at[rows, :], sems.at[field]
                    )
                )
                copies[-1].start()
    for field in range(3):
        for part, (start, stop) in enumerate(((0, low), (high, depth))):
            rows = pl.ds(start * ROWS, (stop - start) * ROWS)
            copies.append(
                pltpu.make_async_copy(
                    work.at[field, rows, :], outs[field].at[rows, :], sems.at[3 + 2 * field + part]
                )
            )
            copies[-1].start()
    for copy in copies:
        copy.wait()


def swaps(pairs):
    return [route for a, b in pairs for route in ((a, b), (b, a))]


def exchange_routes(lats, lons):
    def at(lat, lon):
        return lat * lons + lon % lons

    every = range(lons)
    lon_first = [(at(l, c), at(l, c + 1)) for l in range(lats) for c in range(0, lons, 2)]
    lon_second = [(at(l, c), at(l, c + 1)) for l in range(lats) for c in range(1, lons, 2)]
    lat_first = [(at(l, c), at(l + 1, c)) for l in range(0, lats, 2) for c in every]
    lat_second = [(at(l, c), at(l + 1, c)) for l in range(1, lats - 1, 2) for c in every]
    lat_second += [(at(lats - 1, c), at(lats - 1, lons - 1 - c)) for c in range(lons // 2)]
    lat_second += [(at(0, c), at(0, c + 1)) for c in range(0, lons, 2)]
    return [swaps(pairs) for pairs in (lon_first, lon_second, lat_first, lat_second)]


def per_device(
    temp, uvel, vvel, vert_mixing, inv_dx, inv_dy, horiz_mixing, coriolis, wet_mask, levels
):
    depth, rows, lanes = temp.shape
    assert (rows, lanes) == (ROWS, LANES) and depth == 40
    lats, lons = lax.axis_size("lat"), lax.axis_size("lon")
    assert lats % 2 == 0 and lons % 2 == 0
    flat = depth * rows

    def f32(*shape):
        return jax.ShapeDtypeStruct(shape, jnp.float32)

    def vmem(*shape, dtype=jnp.float32):
        return pltpu.VMEM(shape, dtype)

    limit = pltpu.CompilerParams(vmem_limit_bytes=16 << 20)
    cheap = pl.CostEstimate(flops=1, bytes_accessed=1, transcendentals=0)
    both = ("lat", "lon")
    lon_first, lon_second, lat_first, lat_second = exchange_routes(lats, lons)
    inputs = [pltpu.with_memory_space_constraint(x, pltpu.HBM) for x in (temp, uvel, vvel, wet_mask)]
    sent2 = pl.pallas_call(
        fold_pack_kernel,
        name="fold_pack",
        out_shape=f32(7 * depth + TILE, lanes),
        in_specs=[HBM] * 4,
        out_specs=VMEM,
        scratch_shapes=[vmem(depth * TILE, lanes)] * 3
        + [vmem(depth * TILE, lanes, dtype=jnp.int32), pltpu.SemaphoreType.DMA((4,))],
        compiler_params=limit,
        cost_estimate=cheap,
    )(*inputs)
    got2 = lax.ppermute(sent2, both, lat_second)
    temp, uvel, vvel, vert_mixing, wet_mask = (
        x.reshape(flat, lanes) for x in (temp, uvel, vvel, vert_mixing, wet_mask)
    )
    sent1 = pl.pallas_call(
        rows_pack_kernel,
        name="rows_pack",
        out_shape=f32(7 * depth, lanes),
        in_specs=[VMEM] * 4 + [pl.BlockSpec(memory_space=pl.ANY)],
        out_specs=VMEM,
        compiler_params=limit,
        cost_estimate=cheap,
    )(temp, uvel, vvel, wet_mask, sent2)
    got1 = lax.ppermute(sent1, both, lat_first)
    edges, longer, solve, middle = pl.pallas_call(
        columns_kernel,
        name="columns",
        out_shape=(
            f32((TAIL + 1) * rows, lanes),
            f32((TAIL + 1) * rows + TILE, lanes),
            f32(3, flat, lanes),
            f32(rows, lanes),
        ),
        in_specs=[VMEM] * 6,
        out_specs=(VMEM,) * 4,
        compiler_params=limit,
        cost_estimate=cheap,
    )(temp, uvel, vvel, wet_mask, vert_mixing, levels)
    second = lax.ppermute(longer, both, lon_second)
    first = lax.ppermute(edges, both, lon_first)
    prov = pl.pallas_call(
        interior_kernel,
        name="interior",
        out_shape=f32(3, flat, lanes),
        in_specs=[VMEM] * 8,
        out_specs=VMEM,
        compiler_params=limit,
        cost_estimate=cheap,
    )(temp, uvel, vvel, wet_mask, inv_dx, inv_dy, horiz_mixing, coriolis)
    prov = pl.pallas_call(
        ghosts_kernel,
        name="ghosts",
        out_shape=f32(3, flat, lanes),
        in_specs=[VMEM] * 9,
        out_specs=VMEM,
        input_output_aliases={0: 0},
        compiler_params=limit,
        cost_estimate=cheap,
    )(prov, sent1, got1, edges, first, wet_mask, inv_dx, inv_dy, horiz_mixing)
    outs = pl.pallas_call(
        finish_kernel,
        name="finish",
        out_shape=(f32(flat, lanes),) * 3 + (f32(3, flat, lanes),),
        in_specs=[VMEM] * 11,
        out_specs=(HBM,) * 3 + (VMEM,),
        input_output_aliases={0: 3},
        scratch_shapes=[
            vmem(3, flat, lanes),
            vmem(7 * depth, lanes),
            pltpu.SemaphoreType.DMA((9,)),
        ],
        compiler_params=limit,
        cost_estimate=cheap,
    )(prov, solve, middle, sent2, got2, edges, second, wet_mask, inv_dx, inv_dy, horiz_mixing)
    return tuple(x.reshape(depth, rows, lanes) for x in outs[:3])


def solution(mesh):
    field, plane = P(None, "lat", "lon"), P("lat", "lon")
    return jax.shard_map(
        per_device,
        mesh=mesh,
        in_specs=(field,) * 4 + (plane,) * 4 + (field, plane),
        out_specs=(field,) * 3,
        check_vma=False,
    )
```

```python
import functools

import jax
import jax.numpy as jnp
from jax import lax
from jax.experimental import pallas as pl
from jax.experimental.pallas import tpu as pltpu
from jax.sharding import PartitionSpec as P

ROWS = 16
LANES = 128
TILE = 8
TAIL = 4
ORDER = (2, 1)
VMEM = pl.BlockSpec(memory_space=pltpu.VMEM)
HBM = pl.BlockSpec(memory_space=pltpu.HBM)


def lane_index(rows):
    return lax.broadcasted_iota(jnp.int32, (rows, LANES), 1)


def turn_lanes(x, shift):
    return pltpu.roll(x, shift % LANES, 1)


def level_rows(row, depth):
    return pl.ds(row, depth, stride=ROWS)


def piece(ref, number, depth):
    return ref[number * depth : (number + 1) * depth, :]


def level(ref, number):
    return ref[number * ROWS : (number + 1) * ROWS, :]


def slab_place(number, field):
    if number < 32:
        return field, 4 * number
    return TAIL, 32 * field + 4 * (number - 32)


def fold_pack_kernel(temp, uvel, vvel, mask, out, half0, half1, half2, halfm, sems):
    depth = temp.shape[0]
    odd = lax.rem(lax.axis_index("lat"), 2)
    copies = []
    for number, (field, half) in enumerate(
        zip((temp, uvel, vvel, mask), (half0, half1, half2, halfm))
    ):
        copies.append(
            pltpu.make_async_copy(
                field.at[:, pl.ds(pl.multiple_of(odd * TILE, TILE), TILE), :],
                half.reshape(depth, TILE, LANES),
                sems.at[number],
            )
        )
    for copy in copies:
        copy.start()
    near = (TILE - 1) * odd
    far = near + 1 - 2 * odd
    keep = jnp.where(lax.axis_index("lat") == 0, 0.0, 1.0)
    for number, half in enumerate((half0, half1, half2)):
        copies[number].wait()
        base = 2 * depth * number
        out[base : base + depth, :] = half[pl.ds(near, depth, stride=TILE), :] * keep
        out[base + depth : base + 2 * depth, :] = half[pl.ds(far, depth, stride=TILE), :] * keep
    copies[3].wait()
    out[6 * depth : 7 * depth, :] = halfm[pl.ds(near, depth, stride=TILE), :].astype(jnp.float32) * keep
    out[7 * depth :, :] = jnp.zeros((TILE, LANES), jnp.float32)


def own_slabs(fields, depth):
    group = lane_index(ROWS) // 4
    slabs = [jnp.zeros((ROWS, LANES), jnp.float32)] * (TAIL + 1)
    for number in range(depth):
        for index, field in enumerate(fields):
            slab, start = slab_place(number, index)
            moved = turn_lanes(level(field, number).astype(jnp.float32), start + 2)
            slabs[slab] = jnp.where(group == start // 4, moved, slabs[slab])
    return slabs


def edges_pack_kernel(temp, uvel, vvel, mask, after, first, zonal1, zonal2, edges):
    depth = temp.shape[0] // ROWS
    odd = lax.rem(lax.axis_index("lat"), 2)
    near = (ROWS - 1) * (1 - odd)
    far = near + 2 * odd - 1
    for number, field in enumerate((temp, uvel, vvel)):
        base = 2 * depth * number
        first[base : base + depth, :] = field[level_rows(near, depth), :]
        first[base + depth : base + 2 * depth, :] = field[level_rows(far, depth), :]
    first[6 * depth : 7 * depth, :] = mask[level_rows(near, depth), :].astype(jnp.float32)
    slabs = own_slabs((temp, uvel, vvel, mask), depth)
    for number, slab in enumerate(slabs):
        edges[number * ROWS : (number + 1) * ROWS, :] = slab
    lane = lane_index(ROWS)
    lon_odd = lax.rem(lax.axis_index("lon"), 2)
    for out, column in ((zonal1, 2 * lon_odd), (zonal2, 2 - 2 * lon_odd)):
        source = 4 * (lane % 64 // 2) + lane % 2 + column

        def chosen(x):
            return jnp.take_along_axis(x, source, axis=1, mode="promise_in_bounds")

        for pair in range(2):
            both = jnp.where(lane < 64, chosen(slabs[2 * pair]), chosen(slabs[2 * pair + 1]))
            out[pair * ROWS : (pair + 1) * ROWS, :] = both
        out[2 * ROWS : 3 * ROWS, :] = chosen(slabs[TAIL])
        if out is zonal2:
            out[3 * ROWS :, :] = jnp.zeros((TILE, LANES), jnp.float32)


def columns_kernel(mixing, levels, solve, middle):
    depth = mixing.shape[0] // ROWS
    half = depth // 2
    active = levels[...]
    zero = jnp.zeros((ROWS, LANES), jnp.float32)

    def coupling(number):
        if 0 <= number < depth - 1:
            return jnp.where(number + 1 < active, level(mixing, number + 1), 0.0)
        return zero

    chains = [zero, zero]
    for step in range(half):
        for side, number in enumerate((step, depth - 1 - step)):
            above, below = coupling(number - 1), coupling(number)
            done, left = (above, below) if side == 0 else (below, above)
            inverse = 1.0 / (1.0 + left + done * (1.0 - chains[side]))
            chains[side] = left * inverse
            here = slice(number * ROWS, (number + 1) * ROWS)
            solve[0, here, :] = inverse
            solve[1, here, :] = done * inverse
            solve[2, here, :] = chains[side]
    middle[...] = 1.0 / (1.0 - chains[0] * chains[1])


def interior_kernel(
    temp, uvel, vvel, mask, inv_dx, inv_dy, spread, coriolis, prov
):
    depth = temp.shape[0] // ROWS
    lane = lane_index(depth)

    def rows_of(ref, row):
        return ref[level_rows(row, depth), :]

    def wet_of(row):
        return rows_of(mask, row).astype(jnp.float32)

    fields = (temp, uvel, vvel)
    advect_south = [0.0] * 3
    spread_south = [0.0] * 3
    for row in range(ROWS):
        one = slice(row, row + 1)
        scale = inv_dx[one, :]
        spread_x = spread[one, :] * scale * scale
        scale = scale * (-1.0 / 24.0)
        wet = wet_of(row)
        face_w = wet * jnp.where(lane >= 1, turn_lanes(wet, 1), 0.0)
        face_e = wet * jnp.where(lane < LANES - 1, turn_lanes(wet, -1), 0.0)
        u = rows_of(uvel, row)
        speed_w = scale * face_w * (turn_lanes(u, 1) + u)
        speed_e = scale * face_e * (turn_lanes(u, -1) + u)
        face_w = spread_x * face_w
        face_e = spread_x * face_e
        scale_y = inv_dy[one, :]
        spread_y = spread[one, :] * scale_y * scale_y
        scale_y = scale_y * (-1.0 / 24.0)
        if row + 1 < ROWS:
            face_n = wet * wet_of(row + 1)
            speed_n = face_n * (rows_of(vvel, row) + rows_of(vvel, row + 1))
        turn = wet * coriolis[one, :]
        for number, field in enumerate(fields):
            q = rows_of(field, row)
            west, east = turn_lanes(q, 1), turn_lanes(q, -1)
            value_w = 7.0 * (west + q) - (turn_lanes(q, 2) + east)
            value_e = 7.0 * (east + q) - (west + turn_lanes(q, -2))
            total = speed_e * value_e - speed_w * value_w + face_e * (east - q) - face_w * (q - west)
            if row + 1 < ROWS:
                north = rows_of(field, row + 1)
                outer = None
                if row >= 1:
                    outer = rows_of(field, row - 1)
                if row + 2 < ROWS:
                    beyond = rows_of(field, row + 2)
                    outer = beyond if outer is None else outer + beyond
                advect_north = speed_n * (7.0 * (q + north) - outer)
                spread_north = face_n * (north - q)
            else:
                advect_north, spread_north = 0.0, 0.0
            total = total + scale_y * (advect_north - advect_south[number])
            total = total + spread_y * (spread_north - spread_south[number])
            advect_south[number], spread_south[number] = advect_north, spread_north
            if number == 1:
                total = total + turn * rows_of(vvel, row)
            if number == 2:
                total = total - turn * u
            target = prov.at[number]
            target[level_rows(row, depth), :] = q + total


def add_row_ghosts(work, stride, near, base, mine, ghost, inner, mask, inv_dy, spread, flip):
    depth = work.shape[1] // stride
    far = near + inner
    side = inner.astype(jnp.float32)
    wet = piece(mine, 6, depth)
    face = piece(ghost, 6, depth) * wet
    face_next = wet * mask[level_rows(base + far, depth), :].astype(jnp.float32)
    inv0 = inv_dy[pl.ds(base + near, 1), :]
    inv1 = inv_dy[pl.ds(base + far, 1), :] * side
    mix0 = spread[pl.ds(base + near, 1), :] * inv0 * inv0
    inv0 = inv0 * side
    speed = face * (piece(ghost, 4, depth) * flip + piece(mine, 4, depth)) * (1.0 / 24.0)
    speed_next = face_next * (piece(mine, 4, depth) + piece(mine, 5, depth)) * (1.0 / 24.0)
    for number in range(3):
        sign = 1.0 if number == 0 else flip
        g0 = piece(ghost, 2 * number, depth) * sign
        g1 = piece(ghost, 2 * number + 1, depth) * sign
        o0 = piece(mine, 2 * number, depth)
        o1 = piece(mine, 2 * number + 1, depth)
        advect = speed * (7.0 * (g0 + o0) - (g1 + o1))
        reach = speed_next * g0
        view = work.at[number]
        at_near, at_far = (pl.ds(row, depth, stride=stride) for row in (near, far))
        view[at_near, :] += inv0 * (advect + reach) + mix0 * (face * (g0 - o0))
        view[at_far, :] -= inv1 * reach


def column_ghosts(edges, other, west, inv_dx, spread):
    quad = lane_index(ROWS) % 4
    four = jnp.where(quad < 2, LANES - 2 + quad, quad - 2)
    side = jnp.where(west, 1, -1)

    def toward(x, count):
        return pltpu.roll(x, lax.rem(side * count + LANES, LANES), 1)

    def replicate(x):
        return jnp.take_along_axis(x, four, axis=1, mode="promise_in_bounds")

    wide = replicate(inv_dx[...])
    wide2 = replicate(spread[...]) * wide * wide
    wide = wide * side.astype(jnp.float32)
    own = [level(edges, s) for s in range(TAIL + 1)]
    ghost = quad * side < jnp.where(west, 2, -1)
    lane = lane_index(ROWS)
    place = 2 * (lane // 4) + lane % 2

    def spread_out(x, offset):
        return jnp.take_along_axis(x, place + offset, axis=1, mode="promise_in_bounds")

    theirs = [spread_out(level(other, s // 2), 64 * (s % 2)) for s in range(TAIL)]
    theirs.append(spread_out(level(other, 2), 0))
    both = [jnp.where(ghost, theirs[s], own[s]) for s in range(TAIL + 1)]
    near_lane = quad == jnp.where(west, 2, 1)

    def split(slabs):
        tail = [slabs[TAIL] if f == 0 else turn_lanes(slabs[TAIL], -32 * f) for f in range(4)]
        return [slabs[:TAIL], tail]

    corrections = []
    for part, mine in zip(split(both), split(own)):
        face = toward(part[3], 1) * part[3]
        speed = face * (toward(part[1], 1) + part[1]) * (1.0 / 24.0)
        speed_next = toward(speed, -1)
        result = []
        for number in range(3):
            q = part[number]
            ahead = toward(q, 1)
            advect = speed * (7.0 * (ahead + q) - (toward(q, 2) + toward(q, -1)))
            reach = speed_next * toward(q - mine[number], 1)
            near = wide * (advect + reach) + wide2 * (face * (ahead - q))
            result.append(jnp.where(near_lane, near, -wide * toward(reach, 1)))
        corrections.append(result)
    return corrections


def border_part(corrections, border, number, field):
    if number < 32:
        source, start = corrections[0][field], 4 * number
    else:
        source, start = corrections[1][field], 4 * (number - 32)
    return jnp.where(border, turn_lanes(source, -(start + 2)), 0.0)


def ghosts_kernel(prov_in, edges, first, second, inv_dx, spread, prov):
    depth = prov.shape[1] // ROWS
    odd = lax.rem(lax.axis_index("lon"), 2) == 1
    one = column_ghosts(edges, first, odd, inv_dx, spread)
    two = column_ghosts(edges, second, jnp.logical_not(odd), inv_dx, spread)
    lane = lane_index(ROWS)
    from_first = lane % 4 // 2 == lax.rem(lax.axis_index("lon"), 2)
    corrections = [
        [jnp.where(from_first, a, b) for a, b in zip(part1, part2)] for part1, part2 in zip(one, two)
    ]
    border = (lane < 2) | (lane >= LANES - 2)
    for number in range(depth):
        here = slice(number * ROWS, (number + 1) * ROWS)
        for field in range(3):
            moved = border_part(corrections, border, number, field)
            prov[field, here, :] = prov_in[field, here, :] + moved


def half_kernel(partner, *refs):
    prov, solve, middle, mine, ghost, mask, inv_dy, spread = refs[:8]
    outs = refs[-6:-3]
    work, turned, sems = refs[-3:]
    depth = prov.shape[1] // ROWS
    half = depth // 2
    odd = lax.rem(lax.axis_index("lat"), 2)
    north = odd if partner == 2 else 1 - odd
    base = pl.multiple_of(north * TILE, TILE)
    near = (TILE - 1) * north
    inner = 1 - 2 * north
    flip = 1.0
    if partner == 2:
        fold = lax.axis_index("lat") == lax.axis_size("lat") - 1
        lane = lane_index(7 * depth)
        lane = jnp.where(fold, LANES - 1 - lane, lane)
        turned[...] = jnp.take_along_axis(ghost[: 7 * depth, :], lane, axis=1, mode="promise_in_bounds")
        flip = jnp.where(fold, -1.0, 1.0)
        ghost = turned

    def rows_at(number):
        return pl.ds(pl.multiple_of(number * ROWS + base, TILE), TILE)

    def tile(number):
        return slice(number * TILE, (number + 1) * TILE)

    for number in range(depth):
        for field in range(3):
            work[field, tile(number), :] = prov[field, rows_at(number), :]
    add_row_ghosts(work, TILE, near, base, mine, ghost, inner, mask, inv_dy, spread, flip)

    zero = jnp.zeros((TILE, LANES), jnp.float32)
    values = [[zero] * 3, [zero] * 3]
    for step in range(half):
        for side, number in enumerate((step, depth - 1 - step)):
            inverse, carry = solve[0, rows_at(number), :], solve[1, rows_at(number), :]
            for field in range(3):
                value = inverse * work[field, tile(number), :] + carry * values[side][field]
                values[side][field] = value
                work[field, tile(number), :] = value
    above, below = half - 1, half
    gain = solve[2, rows_at(above), :]
    scale = middle[pl.ds(base, TILE), :]
    tops = [scale * (values[0][field] + gain * values[1][field]) for field in range(3)]
    for field in range(3):
        work[field, tile(above), :] = tops[field]
    chains = [list(tops), list(tops)]
    copies = []

    def store(start, stop):
        for field in range(3):
            source = work.at[field, pl.ds(start * TILE, (stop - start) * TILE), :]
            target = outs[field].at[pl.ds(start, stop - start), pl.ds(base, TILE), :]
            copy = pltpu.make_async_copy(
                source.reshape(stop - start, TILE, LANES), target, sems.at[len(copies)]
            )
            copy.start()
            copies.append(copy)

    for step in range(half):
        for side, number in enumerate((above - 1 - step, below + step)):
            if number < 0:
                continue
            gain = solve[2, rows_at(number), :]
            for field in range(3):
                value = work[field, tile(number), :] + gain * chains[side][field]
                chains[side][field] = value
                work[field, tile(number), :] = value
        if step == half // 2 - 1:
            low, high = above - 1 - step, below + step + 1
            store(low, high)
    store(0, low)
    store(high, depth)
    for copy in copies:
        copy.wait()


def swaps(pairs):
    return [route for a, b in pairs for route in ((a, b), (b, a))]


def exchange_routes(lats, lons):
    def at(lat, lon):
        return lat * lons + lon % lons

    every = range(lons)
    lon_first = [(at(l, c), at(l, c + 1)) for l in range(lats) for c in range(0, lons, 2)]
    lon_second = [(at(l, c), at(l, c + 1)) for l in range(lats) for c in range(1, lons, 2)]
    lat_first = [(at(l, c), at(l + 1, c)) for l in range(0, lats, 2) for c in every]
    lat_second = [(at(l, c), at(l + 1, c)) for l in range(1, lats - 1, 2) for c in every]
    lat_second += [(at(lats - 1, c), at(lats - 1, lons - 1 - c)) for c in range(lons // 2)]
    lat_second += [(at(0, c), at(0, c + 1)) for c in range(0, lons, 2)]
    return [swaps(pairs) for pairs in (lon_first, lon_second, lat_first, lat_second)]


def per_device(
    temp, uvel, vvel, vert_mixing, inv_dx, inv_dy, horiz_mixing, coriolis, wet_mask, levels
):
    depth, rows, lanes = temp.shape
    assert (rows, lanes) == (ROWS, LANES) and depth == 40
    lats, lons = lax.axis_size("lat"), lax.axis_size("lon")
    assert lats % 2 == 0 and lons % 2 == 0
    flat = depth * rows

    def f32(*shape):
        return jax.ShapeDtypeStruct(shape, jnp.float32)

    def vmem(*shape, dtype=jnp.float32):
        return pltpu.VMEM(shape, dtype)

    limit = pltpu.CompilerParams(vmem_limit_bytes=16 << 20)
    cheap = pl.CostEstimate(flops=1, bytes_accessed=1, transcendentals=0)
    both = ("lat", "lon")
    lon_first, lon_second, lat_first, lat_second = exchange_routes(lats, lons)
    inputs = [pltpu.with_memory_space_constraint(x, pltpu.HBM) for x in (temp, uvel, vvel, wet_mask)]
    sent2 = pl.pallas_call(
        fold_pack_kernel,
        name="fold_pack",
        out_shape=f32(7 * depth + TILE, lanes),
        in_specs=[HBM] * 4,
        out_specs=VMEM,
        scratch_shapes=[vmem(depth * TILE, lanes)] * 3
        + [vmem(depth * TILE, lanes, dtype=jnp.int32), pltpu.SemaphoreType.DMA((4,))],
        compiler_params=limit,
        cost_estimate=cheap,
    )(*inputs)
    got2 = lax.ppermute(sent2, both, lat_second)
    temp, uvel, vvel, vert_mixing, wet_mask = (
        x.reshape(flat, lanes) for x in (temp, uvel, vvel, vert_mixing, wet_mask)
    )
    slab_rows = (TAIL + 1) * rows
    sent1, zonal1, zonal2, edges = pl.pallas_call(
        edges_pack_kernel,
        name="edges_pack",
        out_shape=(
            f32(7 * depth, lanes),
            f32(3 * rows, lanes),
            f32(3 * rows + TILE, lanes),
            f32(slab_rows, lanes),
        ),
        in_specs=[VMEM] * 4 + [pl.BlockSpec(memory_space=pl.ANY)],
        out_specs=(VMEM,) * 4,
        compiler_params=limit,
        cost_estimate=cheap,
    )(temp, uvel, vvel, wet_mask, sent2)
    got1 = lax.ppermute(sent1, both, lat_first)
    second = lax.ppermute(zonal2, both, lon_second)
    first = lax.ppermute(zonal1, both, lon_first)
    solve, middle = pl.pallas_call(
        columns_kernel,
        name="columns",
        out_shape=(f32(3, flat, lanes), f32(rows, lanes)),
        in_specs=[VMEM] * 2,
        out_specs=(VMEM,) * 2,
        compiler_params=limit,
        cost_estimate=cheap,
    )(vert_mixing, levels)
    prov = pl.pallas_call(
        interior_kernel,
        name="interior",
        out_shape=f32(3, flat, lanes),
        in_specs=[VMEM] * 8,
        out_specs=VMEM,
        compiler_params=limit,
        cost_estimate=cheap,
    )(temp, uvel, vvel, wet_mask, inv_dx, inv_dy, horiz_mixing, coriolis)
    prov = pl.pallas_call(
        ghosts_kernel,
        name="ghosts",
        out_shape=f32(3, flat, lanes),
        in_specs=[VMEM] * 6,
        out_specs=VMEM,
        input_output_aliases={0: 0},
        compiler_params=limit,
        cost_estimate=cheap,
    )(prov, edges, first, second, inv_dx, horiz_mixing)
    outs = ()
    for partner in ORDER:
        mine, ghost = (sent1, got1) if partner == 1 else (sent2, got2)
        outs = pl.pallas_call(
            functools.partial(half_kernel, partner),
            name="half" + str(partner),
            out_shape=(f32(depth, rows, lanes),) * 3,
            in_specs=[VMEM] * 8 + [HBM] * len(outs),
            out_specs=(HBM,) * 3,
            input_output_aliases={8 + i: i for i in range(len(outs))},
            scratch_shapes=[
                vmem(3, depth * TILE, lanes),
                vmem(7 * depth, lanes),
                pltpu.SemaphoreType.DMA((9,)),
            ],
            compiler_params=limit,
            cost_estimate=cheap,
        )(prov, solve, middle, mine, ghost, wet_mask, inv_dy, horiz_mixing, *outs)
    return outs


def solution(mesh):
    field, plane = P(None, "lat", "lon"), P("lat", "lon")
    return jax.shard_map(
        per_device,
        mesh=mesh,
        in_specs=(field,) * 4 + (plane,) * 4 + (field, plane),
        out_specs=(field,) * 3,
        check_vma=False,
    )
```

```python
import jax
import jax.numpy as jnp
from jax import lax
from jax.experimental import pallas as pl
from jax.experimental.pallas import tpu as pltpu
from jax.sharding import PartitionSpec as P

ROWS = 16
LANES = 128
TILE = 8
TAIL = 4
STORE_AFTER = (4, 11, 19)
VMEM = pl.BlockSpec(memory_space=pltpu.VMEM)
HBM = pl.BlockSpec(memory_space=pltpu.HBM)


def lane_index(rows):
    return lax.broadcasted_iota(jnp.int32, (rows, LANES), 1)


def turn_lanes(x, shift):
    return pltpu.roll(x, shift % LANES, 1)


def level_rows(row, depth):
    return pl.ds(row, depth, stride=ROWS)


def piece(ref, number, depth):
    return ref[number * depth : (number + 1) * depth, :]


def level(ref, number):
    return ref[number * ROWS : (number + 1) * ROWS, :]


def slab_place(number, field):
    if number < 32:
        return field, 4 * number
    return TAIL, 32 * field + 4 * (number - 32)


def sends_north(exchange):
    return jnp.where(lax.rem(lax.axis_index("lat"), 3) == exchange, 1, 0)


def first_rows_kernel(
    temp, uvel, vvel, mask, dx_in, dy_in, spread_in, turn_in, levels_in,
    out, dx, dy, spread, turn, levels, half0, half1, half2, halfm, sems
):
    depth = temp.shape[0]
    north = sends_north(0)
    copies = []
    for field, half in ((temp, half0), (uvel, half1), (vvel, half2), (mask, halfm)):
        copies.append(
            pltpu.make_async_copy(
                field.at[:, pl.ds(pl.multiple_of(north * TILE, TILE), TILE), :],
                half.reshape(depth, TILE, LANES),
                sems.at[len(copies)],
            )
        )
    for plane, target in (
        (dx_in, dx), (dy_in, dy), (spread_in, spread), (turn_in, turn), (levels_in, levels)
    ):
        copies.append(pltpu.make_async_copy(plane, target, sems.at[len(copies)]))
    for copy in copies:
        copy.start()
    near = (TILE - 1) * north
    far = near + 1 - 2 * north
    out[7 * depth :, :] = jnp.zeros((2 * TILE, LANES), jnp.float32)
    for number, half in enumerate((half0, half1, half2)):
        copies[number].wait()
        base = 2 * depth * number
        out[base : base + depth, :] = half[pl.ds(near, depth, stride=TILE), :]
        out[base + depth : base + 2 * depth, :] = half[pl.ds(far, depth, stride=TILE), :]
    copies[3].wait()
    out[6 * depth : 7 * depth, :] = halfm[pl.ds(near, depth, stride=TILE), :].astype(jnp.float32)
    for copy in copies[4:]:
        copy.wait()


def own_slabs(fields, depth):
    group = lane_index(ROWS) // 4
    slabs = [jnp.zeros((ROWS, LANES), jnp.float32)] * (TAIL + 1)
    for number in range(depth):
        for index, field in enumerate(fields):
            slab, start = slab_place(number, index)
            moved = turn_lanes(level(field, number).astype(jnp.float32), start + 2)
            slabs[slab] = jnp.where(group == start // 4, moved, slabs[slab])
    return slabs


def edges_pack_kernel(temp, uvel, vvel, mask, after, second, third, zonal1, zonal2, edges):
    depth = temp.shape[0] // ROWS
    for exchange, out in ((1, second), (2, third)):
        north = sends_north(exchange)
        near = (ROWS - 1) * north
        far = near + 1 - 2 * north
        for number, field in enumerate((temp, uvel, vvel)):
            base = 2 * depth * number
            out[base : base + depth, :] = field[level_rows(near, depth), :]
            out[base + depth : base + 2 * depth, :] = field[level_rows(far, depth), :]
        out[6 * depth : 7 * depth, :] = mask[level_rows(near, depth), :].astype(jnp.float32)
    second[7 * depth :, :] = jnp.zeros((TILE, LANES), jnp.float32)
    slabs = own_slabs((temp, uvel, vvel, mask), depth)
    for number, slab in enumerate(slabs):
        edges[number * ROWS : (number + 1) * ROWS, :] = slab
    lane = lane_index(ROWS)
    lon_odd = lax.rem(lax.axis_index("lon"), 2)
    for out, column in ((zonal1, 2 * lon_odd), (zonal2, 2 - 2 * lon_odd)):
        source = 4 * (lane % 64 // 2) + lane % 2 + column

        def chosen(x):
            return jnp.take_along_axis(x, source, axis=1, mode="promise_in_bounds")

        for pair in range(2):
            both = jnp.where(lane < 64, chosen(slabs[2 * pair]), chosen(slabs[2 * pair + 1]))
            out[pair * ROWS : (pair + 1) * ROWS, :] = both
        out[2 * ROWS : 3 * ROWS, :] = chosen(slabs[TAIL])
        if out is zonal2:
            out[3 * ROWS :, :] = jnp.zeros((TILE, LANES), jnp.float32)


def columns_kernel(mixing, levels, solve, middle):
    depth = mixing.shape[0] // ROWS
    half = depth // 2
    active = levels[...]
    zero = jnp.zeros((ROWS, LANES), jnp.float32)

    def coupling(number):
        if 0 <= number < depth - 1:
            return jnp.where(number + 1 < active, level(mixing, number + 1), 0.0)
        return zero

    chains = [zero, zero]
    for step in range(half):
        for side, number in enumerate((step, depth - 1 - step)):
            above, below = coupling(number - 1), coupling(number)
            done, left = (above, below) if side == 0 else (below, above)
            inverse = 1.0 / (1.0 + left + done * (1.0 - chains[side]))
            chains[side] = left * inverse
            here = slice(number * ROWS, (number + 1) * ROWS)
            solve[0, here, :] = inverse
            solve[1, here, :] = done * inverse
            solve[2, here, :] = chains[side]
    middle[...] = 1.0 / (1.0 - chains[0] * chains[1])


def interior_kernel(
    temp, uvel, vvel, mask, inv_dx, inv_dy, spread, coriolis, prov
):
    depth = temp.shape[0] // ROWS
    lane = lane_index(depth)

    def rows_of(ref, row):
        return ref[level_rows(row, depth), :]

    def wet_of(row):
        return rows_of(mask, row).astype(jnp.float32)

    fields = (temp, uvel, vvel)
    advect_south = [0.0] * 3
    spread_south = [0.0] * 3
    for row in range(ROWS):
        one = slice(row, row + 1)
        scale = inv_dx[one, :]
        spread_x = spread[one, :] * scale * scale
        scale = scale * (-1.0 / 24.0)
        wet = wet_of(row)
        face_w = wet * jnp.where(lane >= 1, turn_lanes(wet, 1), 0.0)
        face_e = wet * jnp.where(lane < LANES - 1, turn_lanes(wet, -1), 0.0)
        u = rows_of(uvel, row)
        speed_w = scale * face_w * (turn_lanes(u, 1) + u)
        speed_e = scale * face_e * (turn_lanes(u, -1) + u)
        face_w = spread_x * face_w
        face_e = spread_x * face_e
        scale_y = inv_dy[one, :]
        spread_y = spread[one, :] * scale_y * scale_y
        scale_y = scale_y * (-1.0 / 24.0)
        if row + 1 < ROWS:
            face_n = wet * wet_of(row + 1)
            speed_n = face_n * (rows_of(vvel, row) + rows_of(vvel, row + 1))
        turn = wet * coriolis[one, :]
        for number, field in enumerate(fields):
            q = rows_of(field, row)
            west, east = turn_lanes(q, 1), turn_lanes(q, -1)
            value_w = 7.0 * (west + q) - (turn_lanes(q, 2) + east)
            value_e = 7.0 * (east + q) - (west + turn_lanes(q, -2))
            total = speed_e * value_e - speed_w * value_w + face_e * (east - q) - face_w * (q - west)
            if row + 1 < ROWS:
                north = rows_of(field, row + 1)
                outer = None
                if row >= 1:
                    outer = rows_of(field, row - 1)
                if row + 2 < ROWS:
                    beyond = rows_of(field, row + 2)
                    outer = beyond if outer is None else outer + beyond
                advect_north = speed_n * (7.0 * (q + north) - outer)
                spread_north = face_n * (north - q)
            else:
                advect_north, spread_north = 0.0, 0.0
            total = total + scale_y * (advect_north - advect_south[number])
            total = total + spread_y * (spread_north - spread_south[number])
            advect_south[number], spread_south[number] = advect_north, spread_north
            if number == 1:
                total = total + turn * rows_of(vvel, row)
            if number == 2:
                total = total - turn * u
            target = prov.at[number]
            target[level_rows(row, depth), :] = q + total


def add_row_ghosts(prov, fields, mask, ghost, near, inv_dy, spread, flip):
    depth = prov.shape[1] // ROWS
    far, side = (1, 1.0) if near == 0 else (near - 1, -1.0)
    at_near, at_far = level_rows(near, depth), level_rows(far, depth)
    wet = mask[at_near, :].astype(jnp.float32)
    face = piece(ghost, 6, depth) * wet
    face_next = wet * mask[at_far, :].astype(jnp.float32)
    inv0 = inv_dy[near : near + 1, :]
    inv1 = inv_dy[far : far + 1, :] * side
    mix0 = spread[near : near + 1, :] * inv0 * inv0
    inv0 = inv0 * side
    v0 = fields[2][at_near, :]
    speed = face * (piece(ghost, 4, depth) * flip + v0) * (1.0 / 24.0)
    speed_next = face_next * (v0 + fields[2][at_far, :]) * (1.0 / 24.0)
    for number in range(3):
        sign = 1.0 if number == 0 else flip
        g0 = piece(ghost, 2 * number, depth) * sign
        g1 = piece(ghost, 2 * number + 1, depth) * sign
        o0 = fields[number][at_near, :]
        o1 = fields[number][at_far, :]
        advect = speed * (7.0 * (g0 + o0) - (g1 + o1))
        reach = speed_next * g0
        view = prov.at[number]
        view[at_near, :] += inv0 * (advect + reach) + mix0 * (face * (g0 - o0))
        view[at_far, :] -= inv1 * reach


def column_ghosts(edges, other, west, inv_dx, spread):
    quad = lane_index(ROWS) % 4
    four = jnp.where(quad < 2, LANES - 2 + quad, quad - 2)
    side = jnp.where(west, 1, -1)

    def toward(x, count):
        return pltpu.roll(x, lax.rem(side * count + LANES, LANES), 1)

    def replicate(x):
        return jnp.take_along_axis(x, four, axis=1, mode="promise_in_bounds")

    wide = replicate(inv_dx[...])
    wide2 = replicate(spread[...]) * wide * wide
    wide = wide * side.astype(jnp.float32)
    own = [level(edges, s) for s in range(TAIL + 1)]
    ghost = quad * side < jnp.where(west, 2, -1)
    lane = lane_index(ROWS)
    place = 2 * (lane // 4) + lane % 2

    def spread_out(x, offset):
        return jnp.take_along_axis(x, place + offset, axis=1, mode="promise_in_bounds")

    theirs = [spread_out(level(other, s // 2), 64 * (s % 2)) for s in range(TAIL)]
    theirs.append(spread_out(level(other, 2), 0))
    both = [jnp.where(ghost, theirs[s], own[s]) for s in range(TAIL + 1)]
    near_lane = quad == jnp.where(west, 2, 1)

    def split(slabs):
        tail = [slabs[TAIL] if f == 0 else turn_lanes(slabs[TAIL], -32 * f) for f in range(4)]
        return [slabs[:TAIL], tail]

    corrections = []
    for part, mine in zip(split(both), split(own)):
        face = toward(part[3], 1) * part[3]
        speed = face * (toward(part[1], 1) + part[1]) * (1.0 / 24.0)
        speed_next = toward(speed, -1)
        result = []
        for number in range(3):
            q = part[number]
            ahead = toward(q, 1)
            advect = speed * (7.0 * (ahead + q) - (toward(q, 2) + toward(q, -1)))
            reach = speed_next * toward(q - mine[number], 1)
            near = wide * (advect + reach) + wide2 * (face * (ahead - q))
            result.append(jnp.where(near_lane, near, -wide * toward(reach, 1)))
        corrections.append(result)
    return corrections


def border_part(corrections, border, number, field):
    if number < 32:
        source, start = corrections[0][field], 4 * number
    else:
        source, start = corrections[1][field], 4 * (number - 32)
    return jnp.where(border, turn_lanes(source, -(start + 2)), 0.0)


def first_columns_kernel(edges, first, inv_dx, spread, out):
    odd = lax.rem(lax.axis_index("lon"), 2) == 1
    for part, slabs in enumerate(column_ghosts(edges, first, odd, inv_dx, spread)):
        for field in range(3):
            place = (3 * part + field) * ROWS
            out[place : place + ROWS, :] = slabs[field]


def finish_kernel(
    prov_in, solve, middle, temp, uvel, vvel, mask, got0, got1, got2, edges, packed, second,
    inv_dx, inv_dy, spread, temp_new, uvel_new, vvel_new, prov, work, south, north, sems
):
    depth = prov.shape[1] // ROWS
    half = depth // 2
    used = slice(0, 7 * depth)
    lat = lax.axis_index("lat")
    fold = lat == lax.axis_size("lat") - 1

    def received(exchange):
        return jnp.where(
            exchange == 0, got0[used, :], jnp.where(exchange == 1, got1[used, :], got2[used, :])
        )

    lane = lane_index(7 * depth)
    lane = jnp.where(fold, LANES - 1 - lane, lane)
    north[...] = jnp.take_along_axis(received(lax.rem(lat, 3)), lane, axis=1, mode="promise_in_bounds")
    south[...] = jnp.where(lat == 0, 0.0, received(lax.rem(lat + 2, 3)))
    flip = jnp.where(fold, -1.0, 1.0)
    fields = (temp, uvel, vvel)
    add_row_ghosts(prov, fields, mask, south, 0, inv_dy, spread, 1.0)
    add_row_ghosts(prov, fields, mask, north, ROWS - 1, inv_dy, spread, flip)

    odd = lax.rem(lax.axis_index("lon"), 2)
    lane = lane_index(ROWS)
    from_first = lane % 4 // 2 == odd
    corrections = []
    for part, slabs in enumerate(column_ghosts(edges, second, odd == 0, inv_dx, spread)):
        corrections.append(
            [jnp.where(from_first, level(packed, 3 * part + f), slabs[f]) for f in range(3)]
        )
    border = (lane < 2) | (lane >= LANES - 2)

    def border_part(number, field):
        part, start = (0, 4 * number) if number < 32 else (1, 4 * (number - 32))
        return jnp.where(border, turn_lanes(corrections[part][field], -(start + 2)), 0.0)

    outs = (temp_new, uvel_new, vvel_new)
    zero = jnp.zeros((ROWS, LANES), jnp.float32)
    values = [[zero] * 3, [zero] * 3]
    for step in range(half):
        for side, number in enumerate((step, depth - 1 - step)):
            here = slice(number * ROWS, (number + 1) * ROWS)
            inverse, carry = solve[0, here, :], solve[1, here, :]
            for field in range(3):
                known = prov[field, here, :] + border_part(number, field)
                value = inverse * known + carry * values[side][field]
                values[side][field] = value
                work[field, here, :] = value
    above, below = half - 1, half
    gain = level(solve.at[2], above)
    scale = middle[...]
    tops = [scale * (values[0][field] + gain * values[1][field]) for field in range(3)]
    for field in range(3):
        work[field, above * ROWS : (above + 1) * ROWS, :] = tops[field]
    chains = [list(tops), list(tops)]
    copies = []

    def store(start, stop):
        rows = pl.ds(start * ROWS, (stop - start) * ROWS)
        for field in range(3):
            copy = pltpu.make_async_copy(
                work.at[field, rows, :], outs[field].at[rows, :], sems.at[len(copies)]
            )
            copy.start()
            copies.append(copy)

    low, high = half, half
    for step in range(half):
        for side, number in enumerate((above - 1 - step, below + step)):
            if number < 0:
                continue
            here = slice(number * ROWS, (number + 1) * ROWS)
            gain = solve[2, here, :]
            for field in range(3):
                value = work[field, here, :] + gain * chains[side][field]
                chains[side][field] = value
                work[field, here, :] = value
        if step in STORE_AFTER:
            start, stop = max(above - 1 - step, 0), below + step + 1
            if low == high:
                store(start, stop)
            else:
                store(start, low)
                store(high, stop)
            low, high = start, stop
    for copy in copies:
        copy.wait()


def swaps(pairs):
    return [route for a, b in pairs for route in ((a, b), (b, a))]


def exchange_routes(lats, lons):
    def at(lat, lon):
        return lat * lons + lon % lons

    lon_first = [(at(l, c), at(l, c + 1)) for l in range(lats) for c in range(0, lons, 2)]
    lon_second = [(at(l, c), at(l, c + 1)) for l in range(lats) for c in range(1, lons, 2)]
    routes = [swaps(lon_first), swaps(lon_second)]
    for exchange in range(3):
        pairs, idle = [], set(range(lats))
        for l in range(exchange, lats, 3):
            if l == lats - 1:
                pairs += [(at(l, c), at(l, lons - 1 - c)) for c in range(lons // 2)]
            else:
                pairs += [(at(l, c), at(l + 1, c)) for c in range(lons)]
            idle -= {l, l + 1}
        pairs += [(at(l, c), at(l, c + 1)) for l in sorted(idle) for c in range(0, lons, 2)]
        routes.append(swaps(pairs))
    return routes


def per_device(
    temp, uvel, vvel, vert_mixing, inv_dx, inv_dy, horiz_mixing, coriolis, wet_mask, levels
):
    depth, rows, lanes = temp.shape
    assert (rows, lanes) == (ROWS, LANES) and depth == 40
    lats, lons = lax.axis_size("lat"), lax.axis_size("lon")
    assert lons % 2 == 0
    flat = depth * rows

    def f32(*shape):
        return jax.ShapeDtypeStruct(shape, jnp.float32)

    def vmem(*shape, dtype=jnp.float32):
        return pltpu.VMEM(shape, dtype)

    limit = pltpu.CompilerParams(vmem_limit_bytes=16 << 20)
    cheap = pl.CostEstimate(flops=1, bytes_accessed=1, transcendentals=0)
    both = ("lat", "lon")
    zonal_first, zonal_second, *meridional = exchange_routes(lats, lons)
    arrays = (temp, uvel, vvel, wet_mask, inv_dx, inv_dy, horiz_mixing, coriolis, levels)
    arrays = [pltpu.with_memory_space_constraint(x, pltpu.HBM) for x in arrays]
    sent0, inv_dx, inv_dy, horiz_mixing, coriolis, levels = pl.pallas_call(
        first_rows_kernel,
        name="first_rows",
        out_shape=(f32(7 * depth + 2 * TILE, lanes),)
        + (f32(rows, lanes),) * 4
        + (jax.ShapeDtypeStruct((rows, lanes), jnp.int32),),
        in_specs=[HBM] * 9,
        out_specs=(VMEM,) * 6,
        scratch_shapes=[vmem(depth * TILE, lanes)] * 3
        + [vmem(depth * TILE, lanes, dtype=jnp.int32), pltpu.SemaphoreType.DMA((9,))],
        compiler_params=limit,
        cost_estimate=cheap,
    )(*arrays)
    got0 = lax.ppermute(sent0, both, meridional[0])
    temp, uvel, vvel, vert_mixing, wet_mask = (
        x.reshape(flat, lanes) for x in (temp, uvel, vvel, vert_mixing, wet_mask)
    )
    sent1, sent2, zonal1, zonal2, edges = pl.pallas_call(
        edges_pack_kernel,
        name="edges_pack",
        out_shape=(
            f32(7 * depth + TILE, lanes),
            f32(7 * depth, lanes),
            f32(3 * rows, lanes),
            f32(3 * rows + TILE, lanes),
            f32((TAIL + 1) * rows, lanes),
        ),
        in_specs=[VMEM] * 4 + [pl.BlockSpec(memory_space=pl.ANY)],
        out_specs=(VMEM,) * 5,
        compiler_params=limit,
        cost_estimate=cheap,
    )(temp, uvel, vvel, wet_mask, sent0)
    got1 = lax.ppermute(sent1, both, meridional[1])
    got2 = lax.ppermute(sent2, both, meridional[2])
    second = lax.ppermute(zonal2, both, zonal_second)
    first = lax.ppermute(zonal1, both, zonal_first)
    solve, middle = pl.pallas_call(
        columns_kernel,
        name="columns",
        out_shape=(f32(3, flat, lanes), f32(rows, lanes)),
        in_specs=[VMEM] * 2,
        out_specs=(VMEM,) * 2,
        compiler_params=limit,
        cost_estimate=cheap,
    )(vert_mixing, levels)
    prov = pl.pallas_call(
        interior_kernel,
        name="interior",
        out_shape=f32(3, flat, lanes),
        in_specs=[VMEM] * 8,
        out_specs=VMEM,
        compiler_params=limit,
        cost_estimate=cheap,
    )(temp, uvel, vvel, wet_mask, inv_dx, inv_dy, horiz_mixing, coriolis)
    packed = pl.pallas_call(
        first_columns_kernel,
        name="first_columns",
        out_shape=f32(6 * rows, lanes),
        in_specs=[VMEM] * 4,
        out_specs=VMEM,
        compiler_params=limit,
        cost_estimate=cheap,
    )(edges, first, inv_dx, horiz_mixing)
    outs = pl.pallas_call(
        finish_kernel,
        name="finish",
        out_shape=(f32(flat, lanes),) * 3 + (f32(3, flat, lanes),),
        in_specs=[VMEM] * 16,
        out_specs=(HBM,) * 3 + (VMEM,),
        input_output_aliases={0: 3},
        scratch_shapes=[
            vmem(3, flat, lanes),
            vmem(7 * depth, lanes),
            vmem(7 * depth, lanes),
            pltpu.SemaphoreType.DMA((15,)),
        ],
        compiler_params=limit,
        cost_estimate=cheap,
    )(
        prov, solve, middle, temp, uvel, vvel, wet_mask, got0, got1, got2, edges, packed, second,
        inv_dx, inv_dy, horiz_mixing,
    )
    return tuple(x.reshape(depth, rows, lanes) for x in outs[:3])


def solution(mesh):
    field, plane = P(None, "lat", "lon"), P("lat", "lon")
    return jax.shard_map(
        per_device,
        mesh=mesh,
        in_specs=(field,) * 4 + (plane,) * 4 + (field, plane),
        out_specs=(field,) * 3,
        check_vma=False,
    )
```

```python
import functools

import jax
import jax.numpy as jnp
from jax import lax
from jax.experimental import pallas as pl
from jax.experimental.pallas import tpu as pltpu
from jax.sharding import PartitionSpec as P

ROWS = 16
LANES = 128
TILE = 8
TAIL = 4
STORE_AFTER = (4, 11, 19)
VMEM = pl.BlockSpec(memory_space=pltpu.VMEM)
HBM = pl.BlockSpec(memory_space=pltpu.HBM)


def lane_index(rows):
    return lax.broadcasted_iota(jnp.int32, (rows, LANES), 1)


def turn_lanes(x, shift):
    return pltpu.roll(x, shift % LANES, 1)


def level_rows(row, depth):
    return pl.ds(row, depth, stride=ROWS)


def piece(ref, number, depth):
    return ref[number * depth : (number + 1) * depth, :]


def level(ref, number):
    return ref[number * ROWS : (number + 1) * ROWS, :]


def slab_place(number, field):
    if number < 32:
        return field, 4 * number
    return TAIL, 32 * field + 4 * (number - 32)


def sends_north(exchange):
    return jnp.where(lax.rem(lax.axis_index("lat"), 3) == exchange, 1, 0)


def first_rows_kernel(
    temp, uvel, vvel, mask, dx_in, dy_in, spread_in, turn_in, levels_in,
    out, dx, dy, spread, turn, levels, wet, sems
):
    depth = temp.shape[0]
    north = sends_north(0)
    near = (ROWS - 1) * north
    far = near + 1 - 2 * north
    moves = [(mask.at[:, near, :], wet)]
    for number, field in enumerate((temp, uvel, vvel)):
        for place, row in ((2 * number, near), (2 * number + 1, far)):
            moves.append((field.at[:, row, :], out.at[place * depth : (place + 1) * depth, :]))
    moves += [(dx_in, dx), (dy_in, dy), (spread_in, spread), (turn_in, turn), (levels_in, levels)]
    copies = [pltpu.make_async_copy(*move, sems.at[i]) for i, move in enumerate(moves)]
    for copy in copies:
        copy.start()
    out[7 * depth :, :] = jnp.zeros((2 * TILE, LANES), jnp.float32)
    copies[0].wait()
    out[6 * depth : 7 * depth, :] = wet[...].astype(jnp.float32)
    for copy in copies[1:]:
        copy.wait()


def own_slabs(fields, depth):
    group = lane_index(ROWS) // 4
    slabs = [jnp.zeros((ROWS, LANES), jnp.float32)] * (TAIL + 1)
    for number in range(depth):
        for index, field in enumerate(fields):
            slab, start = slab_place(number, index)
            moved = turn_lanes(level(field, number).astype(jnp.float32), start + 2)
            slabs[slab] = jnp.where(group == start // 4, moved, slabs[slab])
    return slabs


def edges_pack_kernel(temp, uvel, vvel, mask, after, second, third, zonal1, zonal2, edges):
    depth = temp.shape[0] // ROWS
    for exchange, out in ((1, second), (2, third)):
        north = sends_north(exchange)
        near = (ROWS - 1) * north
        far = near + 1 - 2 * north
        for number, field in enumerate((temp, uvel, vvel)):
            base = 2 * depth * number
            out[base : base + depth, :] = field[level_rows(near, depth), :]
            out[base + depth : base + 2 * depth, :] = field[level_rows(far, depth), :]
        out[6 * depth : 7 * depth, :] = mask[level_rows(near, depth), :].astype(jnp.float32)
    second[7 * depth :, :] = jnp.zeros((TILE, LANES), jnp.float32)
    slabs = own_slabs((temp, uvel, vvel, mask), depth)
    for number, slab in enumerate(slabs):
        edges[number * ROWS : (number + 1) * ROWS, :] = slab
    lane = lane_index(ROWS)
    lon_odd = lax.rem(lax.axis_index("lon"), 2)
    for out, column in ((zonal1, 2 * lon_odd), (zonal2, 2 - 2 * lon_odd)):
        source = 4 * (lane % 64 // 2) + lane % 2 + column

        def chosen(x):
            return jnp.take_along_axis(x, source, axis=1, mode="promise_in_bounds")

        for pair in range(2):
            both = jnp.where(lane < 64, chosen(slabs[2 * pair]), chosen(slabs[2 * pair + 1]))
            out[pair * ROWS : (pair + 1) * ROWS, :] = both
        out[2 * ROWS : 3 * ROWS, :] = chosen(slabs[TAIL])
        if out is zonal2:
            out[3 * ROWS :, :] = jnp.zeros((TILE, LANES), jnp.float32)


def columns_kernel(mixing, levels, solve, middle):
    depth = mixing.shape[0] // ROWS
    half = depth // 2
    active = levels[...]
    zero = jnp.zeros((ROWS, LANES), jnp.float32)

    def coupling(number):
        if 0 <= number < depth - 1:
            return jnp.where(number + 1 < active, level(mixing, number + 1), 0.0)
        return zero

    chains = [zero, zero]
    for step in range(half):
        for side, number in enumerate((step, depth - 1 - step)):
            above, below = coupling(number - 1), coupling(number)
            done, left = (above, below) if side == 0 else (below, above)
            inverse = 1.0 / (1.0 + left + done * (1.0 - chains[side]))
            chains[side] = left * inverse
            here = slice(number * ROWS, (number + 1) * ROWS)
            solve[0, here, :] = inverse
            solve[1, here, :] = done * inverse
            solve[2, here, :] = chains[side]
    middle[...] = 1.0 / (1.0 - chains[0] * chains[1])


def interior_kernel(temp, uvel, vvel, mask, inv_dx, inv_dy, spread, coriolis, prov):
    depth = temp.shape[0] // ROWS
    lane = lane_index(ROWS)
    row = lax.broadcasted_iota(jnp.int32, (ROWS, LANES), 0)
    spread_x = spread[...] * inv_dx[...] * inv_dx[...]
    spread_y = spread[...] * inv_dy[...] * inv_dy[...]
    scale_x = inv_dx[...] * (-1.0 / 24.0)
    scale_y = inv_dy[...] * (-1.0 / 24.0)
    turn = coriolis[...]

    def shifted_rows(ref, number, count):
        start = number * ROWS + count
        if start < 0 or start + ROWS > ref.shape[0]:
            return pltpu.roll(level(ref, number), -count % ROWS, 0)
        return ref[start : start + ROWS, :]

    def weights(face_low, face_high, speed_low, speed_high):
        return (
            speed_low,
            face_low - speed_high - 7.0 * speed_low,
            7.0 * (speed_high - speed_low) - face_low - face_high,
            face_high + speed_low + 7.0 * speed_high,
            -speed_high,
        )

    for number in range(depth):
        here = slice(number * ROWS, (number + 1) * ROWS)
        wet = level(mask, number).astype(jnp.float32)
        u, v = level(uvel, number), level(vvel, number)
        face_w = wet * jnp.where(lane >= 1, turn_lanes(wet, 1), 0.0)
        face_e = wet * jnp.where(lane < LANES - 1, turn_lanes(wet, -1), 0.0)
        face_s = wet * jnp.where(row >= 1, shifted_rows(mask, number, -1).astype(jnp.float32), 0.0)
        face_n = wet * jnp.where(row < ROWS - 1, shifted_rows(mask, number, 1).astype(jnp.float32), 0.0)
        west2, west, here_x, east, east2 = weights(
            spread_x * face_w,
            spread_x * face_e,
            scale_x * face_w * (turn_lanes(u, 1) + u),
            scale_x * face_e * (turn_lanes(u, -1) + u),
        )
        south2, south, here_y, north, north2 = weights(
            spread_y * face_s,
            spread_y * face_n,
            scale_y * face_s * (shifted_rows(vvel, number, -1) + v),
            scale_y * face_n * (shifted_rows(vvel, number, 1) + v),
        )
        south2 = jnp.where(row >= 2, south2, 0.0)
        south = jnp.where(row >= 1, south, 0.0)
        north = jnp.where(row < ROWS - 1, north, 0.0)
        north2 = jnp.where(row < ROWS - 2, north2, 0.0)
        middle = 1.0 + here_x + here_y
        wet_turn = wet * turn
        for index, ref in enumerate((temp, uvel, vvel)):
            q = level(ref, number)
            total = middle * q
            total += west * turn_lanes(q, 1) + east * turn_lanes(q, -1)
            total += west2 * turn_lanes(q, 2) + east2 * turn_lanes(q, -2)
            total += south * shifted_rows(ref, number, -1) + north * shifted_rows(ref, number, 1)
            total += south2 * shifted_rows(ref, number, -2) + north2 * shifted_rows(ref, number, 2)
            if index == 1:
                total += wet_turn * v
            if index == 2:
                total -= wet_turn * u
            prov[index, here, :] = total


def add_row_ghosts(prov, fields, mask, ghost, near, inv_dy, spread, flip):
    depth = prov.shape[1] // ROWS
    far, side = (1, 1.0) if near == 0 else (near - 1, -1.0)
    at_near, at_far = level_rows(near, depth), level_rows(far, depth)
    wet = mask[at_near, :].astype(jnp.float32)
    face = piece(ghost, 6, depth) * wet
    face_next = wet * mask[at_far, :].astype(jnp.float32)
    inv0 = inv_dy[near : near + 1, :]
    inv1 = inv_dy[far : far + 1, :] * side
    mix0 = spread[near : near + 1, :] * inv0 * inv0
    inv0 = inv0 * side
    v0 = fields[2][at_near, :]
    speed = face * (piece(ghost, 4, depth) * flip + v0) * (1.0 / 24.0)
    speed_next = face_next * (v0 + fields[2][at_far, :]) * (1.0 / 24.0)
    for number in range(3):
        sign = 1.0 if number == 0 else flip
        g0 = piece(ghost, 2 * number, depth) * sign
        g1 = piece(ghost, 2 * number + 1, depth) * sign
        o0 = fields[number][at_near, :]
        o1 = fields[number][at_far, :]
        advect = speed * (7.0 * (g0 + o0) - (g1 + o1))
        reach = speed_next * g0
        view = prov.at[number]
        view[at_near, :] += inv0 * (advect + reach) + mix0 * (face * (g0 - o0))
        view[at_far, :] -= inv1 * reach


def column_ghosts(edges, other, west, inv_dx, spread):
    quad = lane_index(ROWS) % 4
    four = jnp.where(quad < 2, LANES - 2 + quad, quad - 2)
    side = jnp.where(west, 1, -1)

    def toward(x, count):
        return pltpu.roll(x, lax.rem(side * count + LANES, LANES), 1)

    def replicate(x):
        return jnp.take_along_axis(x, four, axis=1, mode="promise_in_bounds")

    wide = replicate(inv_dx[...])
    wide2 = replicate(spread[...]) * wide * wide
    wide = wide * side.astype(jnp.float32)
    own = [level(edges, s) for s in range(TAIL + 1)]
    ghost = quad * side < jnp.where(west, 2, -1)
    lane = lane_index(ROWS)
    place = 2 * (lane // 4) + lane % 2

    def spread_out(x, offset):
        return jnp.take_along_axis(x, place + offset, axis=1, mode="promise_in_bounds")

    theirs = [spread_out(level(other, s // 2), 64 * (s % 2)) for s in range(TAIL)]
    theirs.append(spread_out(level(other, 2), 0))
    both = [jnp.where(ghost, theirs[s], own[s]) for s in range(TAIL + 1)]
    near_lane = quad == jnp.where(west, 2, 1)

    def split(slabs):
        tail = [slabs[TAIL] if f == 0 else turn_lanes(slabs[TAIL], -32 * f) for f in range(4)]
        return [slabs[:TAIL], tail]

    corrections = []
    for part, mine in zip(split(both), split(own)):
        face = toward(part[3], 1) * part[3]
        speed = face * (toward(part[1], 1) + part[1]) * (1.0 / 24.0)
        speed_next = toward(speed, -1)
        result = []
        for number in range(3):
            q = part[number]
            ahead = toward(q, 1)
            advect = speed * (7.0 * (ahead + q) - (toward(q, 2) + toward(q, -1)))
            reach = speed_next * toward(q - mine[number], 1)
            near = wide * (advect + reach) + wide2 * (face * (ahead - q))
            result.append(jnp.where(near_lane, near, -wide * toward(reach, 1)))
        corrections.append(result)
    return corrections


def border_part(corrections, border, number, field):
    if number < 32:
        source, start = corrections[0][field], 4 * number
    else:
        source, start = corrections[1][field], 4 * (number - 32)
    return jnp.where(border, turn_lanes(source, -(start + 2)), 0.0)


def columns_ghosts_kernel(parity, edges, other, inv_dx, spread, out):
    west = lax.rem(lax.axis_index("lon"), 2) == parity
    for part, slabs in enumerate(column_ghosts(edges, other, west, inv_dx, spread)):
        for field in range(3):
            place = (3 * part + field) * ROWS
            out[place : place + ROWS, :] = slabs[field]


def finish_kernel(
    prov_in, solve, middle, temp, uvel, vvel, mask, got0, got1, got2, packed1, packed2,
    inv_dy, spread, temp_new, uvel_new, vvel_new, prov, work, south, north, sems
):
    depth = prov.shape[1] // ROWS
    half = depth // 2
    used = slice(0, 7 * depth)
    lat = lax.axis_index("lat")
    fold = lat == lax.axis_size("lat") - 1

    def received(exchange):
        return jnp.where(
            exchange == 0, got0[used, :], jnp.where(exchange == 1, got1[used, :], got2[used, :])
        )

    lane = lane_index(7 * depth)
    lane = jnp.where(fold, LANES - 1 - lane, lane)
    north[...] = jnp.take_along_axis(received(lax.rem(lat, 3)), lane, axis=1, mode="promise_in_bounds")
    south[...] = jnp.where(lat == 0, 0.0, received(lax.rem(lat + 2, 3)))
    flip = jnp.where(fold, -1.0, 1.0)
    fields = (temp, uvel, vvel)
    add_row_ghosts(prov, fields, mask, south, 0, inv_dy, spread, 1.0)
    add_row_ghosts(prov, fields, mask, north, ROWS - 1, inv_dy, spread, flip)

    lane = lane_index(ROWS)
    from_first = lane % 4 // 2 == lax.rem(lax.axis_index("lon"), 2)
    corrections = [
        [jnp.where(from_first, level(packed1, place), level(packed2, place)) for place in range(part, part + 3)]
        for part in (0, 3)
    ]
    border = (lane < 2) | (lane >= LANES - 2)

    def border_part(number, field):
        part, start = (0, 4 * number) if number < 32 else (1, 4 * (number - 32))
        return jnp.where(border, turn_lanes(corrections[part][field], -(start + 2)), 0.0)

    outs = (temp_new, uvel_new, vvel_new)
    zero = jnp.zeros((ROWS, LANES), jnp.float32)
    values = [[zero] * 3, [zero] * 3]
    for step in range(half):
        for side, number in enumerate((step, depth - 1 - step)):
            here = slice(number * ROWS, (number + 1) * ROWS)
            inverse, carry = solve[0, here, :], solve[1, here, :]
            for field in range(3):
                known = prov[field, here, :] + border_part(number, field)
                value = inverse * known + carry * values[side][field]
                values[side][field] = value
                work[field, here, :] = value
    above, below = half - 1, half
    gain = level(solve.at[2], above)
    scale = middle[...]
    tops = [scale * (values[0][field] + gain * values[1][field]) for field in range(3)]
    for field in range(3):
        work[field, above * ROWS : (above + 1) * ROWS, :] = tops[field]
    chains = [list(tops), list(tops)]
    copies = []

    def store(start, stop):
        rows = pl.ds(start * ROWS, (stop - start) * ROWS)
        for field in range(3):
            copy = pltpu.make_async_copy(
                work.at[field, rows, :], outs[field].at[rows, :], sems.at[len(copies)]
            )
            copy.start()
            copies.append(copy)

    low, high = half, half
    for step in range(half):
        for side, number in enumerate((above - 1 - step, below + step)):
            if number < 0:
                continue
            here = slice(number * ROWS, (number + 1) * ROWS)
            gain = solve[2, here, :]
            for field in range(3):
                value = work[field, here, :] + gain * chains[side][field]
                chains[side][field] = value
                work[field, here, :] = value
        if step in STORE_AFTER:
            start, stop = max(above - 1 - step, 0), below + step + 1
            if low == high:
                store(start, stop)
            else:
                store(start, low)
                store(high, stop)
            low, high = start, stop
    for copy in copies:
        copy.wait()


def swaps(pairs):
    return [route for a, b in pairs for route in ((a, b), (b, a))]


def exchange_routes(lats, lons):
    def at(lat, lon):
        return lat * lons + lon % lons

    lon_first = [(at(l, c), at(l, c + 1)) for l in range(lats) for c in range(0, lons, 2)]
    lon_second = [(at(l, c), at(l, c + 1)) for l in range(lats) for c in range(1, lons, 2)]
    routes = [swaps(lon_first), swaps(lon_second)]
    for exchange in range(3):
        pairs, idle = [], set(range(lats))
        for l in range(exchange, lats, 3):
            if l == lats - 1:
                pairs += [(at(l, c), at(l, lons - 1 - c)) for c in range(lons // 2)]
            else:
                pairs += [(at(l, c), at(l + 1, c)) for c in range(lons)]
            idle -= {l, l + 1}
        pairs += [(at(l, c), at(l, c + 1)) for l in sorted(idle) for c in range(0, lons, 2)]
        routes.append(swaps(pairs))
    return routes


def per_device(
    temp, uvel, vvel, vert_mixing, inv_dx, inv_dy, horiz_mixing, coriolis, wet_mask, levels
):
    depth, rows, lanes = temp.shape
    assert (rows, lanes) == (ROWS, LANES) and depth == 40
    lats, lons = lax.axis_size("lat"), lax.axis_size("lon")
    assert lons % 2 == 0
    flat = depth * rows

    def f32(*shape):
        return jax.ShapeDtypeStruct(shape, jnp.float32)

    def vmem(*shape, dtype=jnp.float32):
        return pltpu.VMEM(shape, dtype)

    limit = pltpu.CompilerParams(vmem_limit_bytes=16 << 20)
    cheap = pl.CostEstimate(flops=1, bytes_accessed=1, transcendentals=0)
    both = ("lat", "lon")
    zonal_first, zonal_second, *meridional = exchange_routes(lats, lons)
    arrays = (temp, uvel, vvel, wet_mask, inv_dx, inv_dy, horiz_mixing, coriolis, levels)
    arrays = [pltpu.with_memory_space_constraint(x, pltpu.HBM) for x in arrays]
    sent0, inv_dx, inv_dy, horiz_mixing, coriolis, levels = pl.pallas_call(
        first_rows_kernel,
        name="first_rows",
        out_shape=(f32(7 * depth + 2 * TILE, lanes),)
        + (f32(rows, lanes),) * 4
        + (jax.ShapeDtypeStruct((rows, lanes), jnp.int32),),
        in_specs=[HBM] * 9,
        out_specs=(VMEM,) * 6,
        scratch_shapes=[vmem(depth, lanes, dtype=jnp.int32), pltpu.SemaphoreType.DMA((12,))],
        compiler_params=limit,
        cost_estimate=cheap,
    )(*arrays)
    got0 = lax.ppermute(sent0, both, meridional[0])
    temp, uvel, vvel, vert_mixing, wet_mask = (
        x.reshape(flat, lanes) for x in (temp, uvel, vvel, vert_mixing, wet_mask)
    )
    sent1, sent2, zonal1, zonal2, edges = pl.pallas_call(
        edges_pack_kernel,
        name="edges_pack",
        out_shape=(
            f32(7 * depth + TILE, lanes),
            f32(7 * depth, lanes),
            f32(3 * rows, lanes),
            f32(3 * rows + TILE, lanes),
            f32((TAIL + 1) * rows, lanes),
        ),
        in_specs=[VMEM] * 4 + [pl.BlockSpec(memory_space=pl.ANY)],
        out_specs=(VMEM,) * 5,
        compiler_params=limit,
        cost_estimate=cheap,
    )(temp, uvel, vvel, wet_mask, sent0)
    got1 = lax.ppermute(sent1, both, meridional[1])
    got2 = lax.ppermute(sent2, both, meridional[2])
    second = lax.ppermute(zonal2, both, zonal_second)
    first = lax.ppermute(zonal1, both, zonal_first)
    solve, middle = pl.pallas_call(
        columns_kernel,
        name="columns",
        out_shape=(f32(3, flat, lanes), f32(rows, lanes)),
        in_specs=[VMEM] * 2,
        out_specs=(VMEM,) * 2,
        compiler_params=limit,
        cost_estimate=cheap,
    )(vert_mixing, levels)
    prov = pl.pallas_call(
        interior_kernel,
        name="interior",
        out_shape=f32(3, flat, lanes),
        in_specs=[VMEM] * 8,
        out_specs=VMEM,
        compiler_params=limit,
        cost_estimate=cheap,
    )(temp, uvel, vvel, wet_mask, inv_dx, inv_dy, horiz_mixing, coriolis)
    packed1, packed2 = (
        pl.pallas_call(
            functools.partial(columns_ghosts_kernel, parity),
            name="columns_ghosts" + str(parity),
            out_shape=f32(6 * rows, lanes),
            in_specs=[VMEM] * 4,
            out_specs=VMEM,
            compiler_params=limit,
            cost_estimate=cost,
        )(edges, other, inv_dx, horiz_mixing)
        for parity, other, cost in ((1, first, cheap), (0, second, cheap))
    )
    outs = pl.pallas_call(
        finish_kernel,
        name="finish",
        out_shape=(f32(flat, lanes),) * 3 + (f32(3, flat, lanes),),
        in_specs=[VMEM] * 14,
        out_specs=(HBM,) * 3 + (VMEM,),
        input_output_aliases={0: 3},
        scratch_shapes=[
            vmem(3, flat, lanes),
            vmem(7 * depth, lanes),
            vmem(7 * depth, lanes),
            pltpu.SemaphoreType.DMA((15,)),
        ],
        compiler_params=limit,
        cost_estimate=cheap,
    )(
        prov, solve, middle, temp, uvel, vvel, wet_mask, got0, got1, got2, packed1, packed2,
        inv_dy, horiz_mixing,
    )
    return tuple(x.reshape(depth, rows, lanes) for x in outs[:3])


def solution(mesh):
    field, plane = P(None, "lat", "lon"), P("lat", "lon")
    return jax.shard_map(
        per_device,
        mesh=mesh,
        in_specs=(field,) * 4 + (plane,) * 4 + (field, plane),
        out_specs=(field,) * 3,
        check_vma=False,
    )
```

```python
import functools

import jax
import jax.numpy as jnp
from jax import lax
from jax.experimental import pallas as pl
from jax.experimental.pallas import tpu as pltpu
from jax.sharding import PartitionSpec as P

ROWS = 16
LANES = 128
TILE = 8
TAIL = 4
STORE_AFTER = (4, 11, 19)
VMEM = pl.BlockSpec(memory_space=pltpu.VMEM)
HBM = pl.BlockSpec(memory_space=pltpu.HBM)


def lane_index(rows):
    return lax.broadcasted_iota(jnp.int32, (rows, LANES), 1)


def turn_lanes(x, shift):
    return pltpu.roll(x, shift % LANES, 1)


def level_rows(row, depth):
    return pl.ds(row, depth, stride=ROWS)


def piece(ref, number, depth):
    return ref[number * depth : (number + 1) * depth, :]


def level(ref, number):
    return ref[number * ROWS : (number + 1) * ROWS, :]


def slab_place(number, field):
    if number < 32:
        return field, 4 * number
    return TAIL, 32 * field + 4 * (number - 32)


def sends_north(exchange):
    return jnp.where(lax.rem(lax.axis_index("lat"), 3) == exchange, 1, 0)


def first_rows_kernel(
    temp, uvel, vvel, mask, dx_in, dy_in, spread_in, turn_in, levels_in,
    out, dx, dy, spread, turn, levels, wet, sems
):
    depth = temp.shape[0]
    north = sends_north(0)
    near = (ROWS - 1) * north
    far = near + 1 - 2 * north
    moves = [(mask.at[:, near, :], wet)]
    for number, field in enumerate((temp, uvel, vvel)):
        for place, row in ((2 * number, near), (2 * number + 1, far)):
            moves.append((field.at[:, row, :], out.at[place * depth : (place + 1) * depth, :]))
    moves += [(dx_in, dx), (dy_in, dy), (spread_in, spread), (turn_in, turn), (levels_in, levels)]
    copies = [pltpu.make_async_copy(*move, sems.at[i]) for i, move in enumerate(moves)]
    for copy in copies:
        copy.start()
    out[7 * depth :, :] = jnp.zeros((TILE, LANES), jnp.float32)
    copies[0].wait()
    out[6 * depth : 7 * depth, :] = wet[...].astype(jnp.float32)
    for copy in copies[1:]:
        copy.wait()


def own_slabs(fields, depth):
    group = lane_index(ROWS) // 4
    slabs = [jnp.zeros((ROWS, LANES), jnp.float32)] * (TAIL + 1)
    for number in range(depth):
        for index, field in enumerate(fields):
            slab, start = slab_place(number, index)
            moved = turn_lanes(level(field, number).astype(jnp.float32), start + 2)
            slabs[slab] = jnp.where(group == start // 4, moved, slabs[slab])
    return slabs


def edges_pack_kernel(temp, uvel, vvel, mask, after, second, third, zonal1, zonal2, edges):
    depth = temp.shape[0] // ROWS
    for exchange, out in ((1, second), (2, third)):
        north = sends_north(exchange)
        near = (ROWS - 1) * north
        far = near + 1 - 2 * north
        for number, field in enumerate((temp, uvel, vvel)):
            base = 2 * depth * number
            out[base : base + depth, :] = field[level_rows(near, depth), :]
            out[base + depth : base + 2 * depth, :] = field[level_rows(far, depth), :]
        out[6 * depth : 7 * depth, :] = mask[level_rows(near, depth), :].astype(jnp.float32)
    second[7 * depth :, :] = jnp.zeros((TILE, LANES), jnp.float32)
    slabs = own_slabs((temp, uvel, vvel, mask), depth)
    for number, slab in enumerate(slabs):
        edges[number * ROWS : (number + 1) * ROWS, :] = slab
    lane = lane_index(ROWS)
    lon_odd = lax.rem(lax.axis_index("lon"), 2)
    for out, column in ((zonal1, 2 * lon_odd), (zonal2, 2 - 2 * lon_odd)):
        source = 4 * (lane % 64 // 2) + lane % 2 + column

        def chosen(x):
            return jnp.take_along_axis(x, source, axis=1, mode="promise_in_bounds")

        for pair in range(2):
            both = jnp.where(lane < 64, chosen(slabs[2 * pair]), chosen(slabs[2 * pair + 1]))
            out[pair * ROWS : (pair + 1) * ROWS, :] = both
        out[2 * ROWS : 3 * ROWS, :] = chosen(slabs[TAIL])
        if out is zonal2:
            out[3 * ROWS :, :] = jnp.zeros((TILE, LANES), jnp.float32)


def columns_kernel(mixing, levels, solve, middle):
    depth = mixing.shape[0] // ROWS
    half = depth // 2
    active = levels[...]
    zero = jnp.zeros((ROWS, LANES), jnp.float32)

    def coupling(number):
        if 0 <= number < depth - 1:
            return jnp.where(number + 1 < active, level(mixing, number + 1), 0.0)
        return zero

    chains = [zero, zero]
    for step in range(half):
        for side, number in enumerate((step, depth - 1 - step)):
            above, below = coupling(number - 1), coupling(number)
            done, left = (above, below) if side == 0 else (below, above)
            inverse = 1.0 / (1.0 + left + done * (1.0 - chains[side]))
            chains[side] = left * inverse
            here = slice(number * ROWS, (number + 1) * ROWS)
            solve[0, here, :] = inverse
            solve[1, here, :] = done * inverse
            solve[2, here, :] = chains[side]
    middle[...] = 1.0 / (1.0 - chains[0] * chains[1])


def interior_kernel(temp, uvel, vvel, mask, inv_dx, inv_dy, spread, coriolis, prov):
    depth = temp.shape[0] // ROWS
    lane = lane_index(ROWS)
    row = lax.broadcasted_iota(jnp.int32, (ROWS, LANES), 0)
    spread_x = spread[...] * inv_dx[...] * inv_dx[...]
    spread_y = spread[...] * inv_dy[...] * inv_dy[...]
    scale_x = inv_dx[...] * (-1.0 / 24.0)
    scale_y = inv_dy[...] * (-1.0 / 24.0)
    turn = coriolis[...]

    def shifted_rows(ref, number, count):
        start = number * ROWS + count
        if start < 0 or start + ROWS > ref.shape[0]:
            return pltpu.roll(level(ref, number), -count % ROWS, 0)
        return ref[start : start + ROWS, :]

    def weights(face_low, face_high, speed_low, speed_high):
        return (
            speed_low,
            face_low - speed_high - 7.0 * speed_low,
            7.0 * (speed_high - speed_low) - face_low - face_high,
            face_high + speed_low + 7.0 * speed_high,
            -speed_high,
        )

    for number in range(depth):
        here = slice(number * ROWS, (number + 1) * ROWS)
        wet = level(mask, number).astype(jnp.float32)
        u, v = level(uvel, number), level(vvel, number)
        face_w = wet * jnp.where(lane >= 1, turn_lanes(wet, 1), 0.0)
        face_e = wet * jnp.where(lane < LANES - 1, turn_lanes(wet, -1), 0.0)
        face_s = wet * jnp.where(row >= 1, shifted_rows(mask, number, -1).astype(jnp.float32), 0.0)
        face_n = wet * jnp.where(row < ROWS - 1, shifted_rows(mask, number, 1).astype(jnp.float32), 0.0)
        west2, west, here_x, east, east2 = weights(
            spread_x * face_w,
            spread_x * face_e,
            scale_x * face_w * (turn_lanes(u, 1) + u),
            scale_x * face_e * (turn_lanes(u, -1) + u),
        )
        south2, south, here_y, north, north2 = weights(
            spread_y * face_s,
            spread_y * face_n,
            scale_y * face_s * (shifted_rows(vvel, number, -1) + v),
            scale_y * face_n * (shifted_rows(vvel, number, 1) + v),
        )
        south2 = jnp.where(row >= 2, south2, 0.0)
        south = jnp.where(row >= 1, south, 0.0)
        north = jnp.where(row < ROWS - 1, north, 0.0)
        north2 = jnp.where(row < ROWS - 2, north2, 0.0)
        middle = 1.0 + here_x + here_y
        wet_turn = wet * turn
        for index, ref in enumerate((temp, uvel, vvel)):
            q = level(ref, number)
            total = middle * q
            total += west * turn_lanes(q, 1) + east * turn_lanes(q, -1)
            total += west2 * turn_lanes(q, 2) + east2 * turn_lanes(q, -2)
            total += south * shifted_rows(ref, number, -1) + north * shifted_rows(ref, number, 1)
            total += south2 * shifted_rows(ref, number, -2) + north2 * shifted_rows(ref, number, 2)
            if index == 1:
                total += wet_turn * v
            if index == 2:
                total -= wet_turn * u
            prov[index, here, :] = total


def add_row_ghosts(prov, fields, mask, ghost, near, inv_dy, spread, flip):
    depth = prov.shape[1] // ROWS
    far, side = (1, 1.0) if near == 0 else (near - 1, -1.0)
    at_near, at_far = level_rows(near, depth), level_rows(far, depth)
    wet = mask[at_near, :].astype(jnp.float32)
    face = piece(ghost, 6, depth) * wet
    face_next = wet * mask[at_far, :].astype(jnp.float32)
    inv0 = inv_dy[near : near + 1, :]
    inv1 = inv_dy[far : far + 1, :] * side
    mix0 = spread[near : near + 1, :] * inv0 * inv0
    inv0 = inv0 * side
    v0 = fields[2][at_near, :]
    speed = face * (piece(ghost, 4, depth) * flip + v0) * (1.0 / 24.0)
    speed_next = face_next * (v0 + fields[2][at_far, :]) * (1.0 / 24.0)
    for number in range(3):
        sign = 1.0 if number == 0 else flip
        g0 = piece(ghost, 2 * number, depth) * sign
        g1 = piece(ghost, 2 * number + 1, depth) * sign
        o0 = fields[number][at_near, :]
        o1 = fields[number][at_far, :]
        advect = speed * (7.0 * (g0 + o0) - (g1 + o1))
        reach = speed_next * g0
        view = prov.at[number]
        view[at_near, :] += inv0 * (advect + reach) + mix0 * (face * (g0 - o0))
        view[at_far, :] -= inv1 * reach


def column_ghosts(edges, other, west, inv_dx, spread):
    quad = lane_index(ROWS) % 4
    four = jnp.where(quad < 2, LANES - 2 + quad, quad - 2)
    side = jnp.where(west, 1, -1)

    def toward(x, count):
        return pltpu.roll(x, lax.rem(side * count + LANES, LANES), 1)

    def replicate(x):
        return jnp.take_along_axis(x, four, axis=1, mode="promise_in_bounds")

    wide = replicate(inv_dx[...])
    wide2 = replicate(spread[...]) * wide * wide
    wide = wide * side.astype(jnp.float32)
    own = [level(edges, s) for s in range(TAIL + 1)]
    ghost = quad * side < jnp.where(west, 2, -1)
    lane = lane_index(ROWS)
    place = 2 * (lane // 4) + lane % 2

    def spread_out(x, offset):
        return jnp.take_along_axis(x, place + offset, axis=1, mode="promise_in_bounds")

    theirs = [spread_out(level(other, s // 2), 64 * (s % 2)) for s in range(TAIL)]
    theirs.append(spread_out(level(other, 2), 0))
    both = [jnp.where(ghost, theirs[s], own[s]) for s in range(TAIL + 1)]
    near_lane = quad == jnp.where(west, 2, 1)

    def split(slabs):
        tail = [slabs[TAIL] if f == 0 else turn_lanes(slabs[TAIL], -32 * f) for f in range(4)]
        return [slabs[:TAIL], tail]

    corrections = []
    for part, mine in zip(split(both), split(own)):
        face = toward(part[3], 1) * part[3]
        speed = face * (toward(part[1], 1) + part[1]) * (1.0 / 24.0)
        speed_next = toward(speed, -1)
        result = []
        for number in range(3):
            q = part[number]
            ahead = toward(q, 1)
            advect = speed * (7.0 * (ahead + q) - (toward(q, 2) + toward(q, -1)))
            reach = speed_next * toward(q - mine[number], 1)
            near = wide * (advect + reach) + wide2 * (face * (ahead - q))
            result.append(jnp.where(near_lane, near, -wide * toward(reach, 1)))
        corrections.append(result)
    return corrections


def border_part(corrections, border, number, field):
    if number < 32:
        source, start = corrections[0][field], 4 * number
    else:
        source, start = corrections[1][field], 4 * (number - 32)
    return jnp.where(border, turn_lanes(source, -(start + 2)), 0.0)


def columns_ghosts_kernel(parity, edges, other, inv_dx, spread, out):
    west = lax.rem(lax.axis_index("lon"), 2) == parity
    for part, slabs in enumerate(column_ghosts(edges, other, west, inv_dx, spread)):
        for field in range(3):
            place = (3 * part + field) * ROWS
            out[place : place + ROWS, :] = slabs[field]


def finish_kernel(
    prov_in, solve, middle, temp, uvel, vvel, mask, got0, got1, got2, packed1, packed2,
    inv_dy, spread, temp_new, uvel_new, vvel_new, prov, work, south, north, sems
):
    depth = prov.shape[1] // ROWS
    half = depth // 2
    used = slice(0, 7 * depth)
    lat = lax.axis_index("lat")
    fold = lat == lax.axis_size("lat") - 1

    def received(exchange):
        return jnp.where(
            exchange == 0, got0[used, :], jnp.where(exchange == 1, got1[used, :], got2[used, :])
        )

    lane = lane_index(7 * depth)
    lane = jnp.where(fold, LANES - 1 - lane, lane)
    north[...] = jnp.take_along_axis(received(lax.rem(lat, 3)), lane, axis=1, mode="promise_in_bounds")
    south[...] = jnp.where(lat == 0, 0.0, received(lax.rem(lat + 2, 3)))
    flip = jnp.where(fold, -1.0, 1.0)
    fields = (temp, uvel, vvel)
    add_row_ghosts(prov, fields, mask, south, 0, inv_dy, spread, 1.0)
    add_row_ghosts(prov, fields, mask, north, ROWS - 1, inv_dy, spread, flip)

    lane = lane_index(ROWS)
    from_first = lane % 4 // 2 == lax.rem(lax.axis_index("lon"), 2)
    corrections = [
        [jnp.where(from_first, level(packed1, place), level(packed2, place)) for place in range(part, part + 3)]
        for part in (0, 3)
    ]
    border = (lane < 2) | (lane >= LANES - 2)

    def border_part(number, field):
        part, start = (0, 4 * number) if number < 32 else (1, 4 * (number - 32))
        return jnp.where(border, turn_lanes(corrections[part][field], -(start + 2)), 0.0)

    outs = (temp_new, uvel_new, vvel_new)
    zero = jnp.zeros((ROWS, LANES), jnp.float32)
    values = [[zero] * 3, [zero] * 3]
    for step in range(half):
        for side, number in enumerate((step, depth - 1 - step)):
            here = slice(number * ROWS, (number + 1) * ROWS)
            inverse, carry = solve[0, here, :], solve[1, here, :]
            for field in range(3):
                known = prov[field, here, :] + border_part(number, field)
                value = inverse * known + carry * values[side][field]
                values[side][field] = value
                work[field, here, :] = value
    above, below = half - 1, half
    gain = level(solve.at[2], above)
    scale = middle[...]
    tops = [scale * (values[0][field] + gain * values[1][field]) for field in range(3)]
    for field in range(3):
        work[field, above * ROWS : (above + 1) * ROWS, :] = tops[field]
    chains = [list(tops), list(tops)]
    copies = []

    def store(start, stop):
        rows = pl.ds(start * ROWS, (stop - start) * ROWS)
        for field in range(3):
            copy = pltpu.make_async_copy(
                work.at[field, rows, :], outs[field].at[rows, :], sems.at[len(copies)]
            )
            copy.start()
            copies.append(copy)

    low, high = half, half
    for step in range(half):
        for side, number in enumerate((above - 1 - step, below + step)):
            if number < 0:
                continue
            here = slice(number * ROWS, (number + 1) * ROWS)
            gain = solve[2, here, :]
            for field in range(3):
                value = work[field, here, :] + gain * chains[side][field]
                chains[side][field] = value
                work[field, here, :] = value
        if step in STORE_AFTER:
            start, stop = max(above - 1 - step, 0), below + step + 1
            if low == high:
                store(start, stop)
            else:
                store(start, low)
                store(high, stop)
            low, high = start, stop
    for copy in copies:
        copy.wait()


def swaps(pairs):
    return [route for a, b in pairs for route in ((a, b), (b, a))]


def exchange_routes(lats, lons):
    def at(lat, lon):
        return lat * lons + lon % lons

    lon_first = [(at(l, c), at(l, c + 1)) for l in range(lats) for c in range(0, lons, 2)]
    lon_second = [(at(l, c), at(l, c + 1)) for l in range(lats) for c in range(1, lons, 2)]
    routes = [swaps(lon_first), swaps(lon_second)]
    for exchange in range(3):
        pairs, idle = [], set(range(lats))
        for l in range(exchange, lats, 3):
            if l == lats - 1:
                pairs += [(at(l, c), at(l, lons - 1 - c)) for c in range(lons // 2)]
            else:
                pairs += [(at(l, c), at(l + 1, c)) for c in range(lons)]
            idle -= {l, l + 1}
        pairs += [(at(l, c), at(l, c + 1)) for l in sorted(idle) for c in range(0, lons, 2)]
        routes.append(swaps(pairs))
    return routes


def per_device(
    temp, uvel, vvel, vert_mixing, inv_dx, inv_dy, horiz_mixing, coriolis, wet_mask, levels
):
    depth, rows, lanes = temp.shape
    assert (rows, lanes) == (ROWS, LANES) and depth == 40
    lats, lons = lax.axis_size("lat"), lax.axis_size("lon")
    assert lons % 2 == 0
    flat = depth * rows

    def f32(*shape):
        return jax.ShapeDtypeStruct(shape, jnp.float32)

    def vmem(*shape, dtype=jnp.float32):
        return pltpu.VMEM(shape, dtype)

    limit = pltpu.CompilerParams(vmem_limit_bytes=16 << 20)
    cheap = pl.CostEstimate(flops=1, bytes_accessed=1, transcendentals=0)
    both = ("lat", "lon")
    zonal_first, zonal_second, *meridional = exchange_routes(lats, lons)
    arrays = (temp, uvel, vvel, wet_mask, inv_dx, inv_dy, horiz_mixing, coriolis, levels)
    arrays = [pltpu.with_memory_space_constraint(x, pltpu.HBM) for x in arrays]
    sent0, inv_dx, inv_dy, horiz_mixing, coriolis, levels = pl.pallas_call(
        first_rows_kernel,
        name="first_rows",
        out_shape=(f32(7 * depth + TILE, lanes),)
        + (f32(rows, lanes),) * 4
        + (jax.ShapeDtypeStruct((rows, lanes), jnp.int32),),
        in_specs=[HBM] * 9,
        out_specs=(VMEM,) * 6,
        scratch_shapes=[vmem(depth, lanes, dtype=jnp.int32), pltpu.SemaphoreType.DMA((12,))],
        compiler_params=limit,
        cost_estimate=cheap,
    )(*arrays)
    got0 = lax.ppermute(sent0, both, meridional[0])
    temp, uvel, vvel, vert_mixing, wet_mask = (
        x.reshape(flat, lanes) for x in (temp, uvel, vvel, vert_mixing, wet_mask)
    )
    sent1, sent2, zonal1, zonal2, edges = pl.pallas_call(
        edges_pack_kernel,
        name="edges_pack",
        out_shape=(
            f32(7 * depth + TILE, lanes),
            f32(7 * depth, lanes),
            f32(3 * rows, lanes),
            f32(3 * rows + TILE, lanes),
            f32((TAIL + 1) * rows, lanes),
        ),
        in_specs=[VMEM] * 4 + [pl.BlockSpec(memory_space=pl.ANY)],
        out_specs=(VMEM,) * 5,
        compiler_params=limit,
        cost_estimate=cheap,
    )(temp, uvel, vvel, wet_mask, sent0)
    got1 = lax.ppermute(sent1, both, meridional[1])
    got2 = lax.ppermute(sent2, both, meridional[2])
    second = lax.ppermute(zonal2, both, zonal_second)
    first = lax.ppermute(zonal1, both, zonal_first)
    solve, middle = pl.pallas_call(
        columns_kernel,
        name="columns",
        out_shape=(f32(3, flat, lanes), f32(rows, lanes)),
        in_specs=[VMEM] * 2,
        out_specs=(VMEM,) * 2,
        compiler_params=limit,
        cost_estimate=cheap,
    )(vert_mixing, levels)
    prov = pl.pallas_call(
        interior_kernel,
        name="interior",
        out_shape=f32(3, flat, lanes),
        in_specs=[VMEM] * 8,
        out_specs=VMEM,
        compiler_params=limit,
        cost_estimate=cheap,
    )(temp, uvel, vvel, wet_mask, inv_dx, inv_dy, horiz_mixing, coriolis)
    packed1, packed2 = (
        pl.pallas_call(
            functools.partial(columns_ghosts_kernel, parity),
            name="columns_ghosts" + str(parity),
            out_shape=f32(6 * rows, lanes),
            in_specs=[VMEM] * 4,
            out_specs=VMEM,
            compiler_params=limit,
            cost_estimate=cost,
        )(edges, other, inv_dx, horiz_mixing)
        for parity, other, cost in ((1, first, cheap), (0, second, pl.CostEstimate(flops=1250000000, bytes_accessed=1, transcendentals=0)))
    )
    outs = pl.pallas_call(
        finish_kernel,
        name="finish",
        out_shape=(f32(flat, lanes),) * 3 + (f32(3, flat, lanes),),
        in_specs=[VMEM] * 14,
        out_specs=(HBM,) * 3 + (VMEM,),
        input_output_aliases={0: 3},
        scratch_shapes=[
            vmem(3, flat, lanes),
            vmem(7 * depth, lanes),
            vmem(7 * depth, lanes),
            pltpu.SemaphoreType.DMA((15,)),
        ],
        compiler_params=limit,
        cost_estimate=cheap,
    )(
        prov, solve, middle, temp, uvel, vvel, wet_mask, got0, got1, got2, packed1, packed2,
        inv_dy, horiz_mixing,
    )
    return tuple(x.reshape(depth, rows, lanes) for x in outs[:3])


def solution(mesh):
    field, plane = P(None, "lat", "lon"), P("lat", "lon")
    return jax.shard_map(
        per_device,
        mesh=mesh,
        in_specs=(field,) * 4 + (plane,) * 4 + (field, plane),
        out_specs=(field,) * 3,
        check_vma=False,
    )
```

```python
import jax
import jax.numpy as jnp
from jax import lax
from jax.experimental import pallas as pl
from jax.experimental.pallas import tpu as pltpu
from jax.sharding import PartitionSpec as P

ROWS = 16
LANES = 128
TILE = 8
TAIL = 4
STORE_AFTER = (4, 11, 19)
VMEM = pl.BlockSpec(memory_space=pltpu.VMEM)
HBM = pl.BlockSpec(memory_space=pltpu.HBM)


def lane_index(rows):
    return lax.broadcasted_iota(jnp.int32, (rows, LANES), 1)


def turn_lanes(x, shift):
    return pltpu.roll(x, shift % LANES, 1)


def level_rows(row, depth):
    return pl.ds(row, depth, stride=ROWS)


def piece(ref, number, depth):
    return ref[number * depth : (number + 1) * depth, :]


def level(ref, number):
    return ref[number * ROWS : (number + 1) * ROWS, :]


def slab_place(number, field):
    if number < 32:
        return field, 4 * number
    return TAIL, 32 * field + 4 * (number - 32)


def sends_north(exchange):
    return jnp.where(lax.rem(lax.axis_index("lat"), 3) == exchange, 1, 0)


def first_rows_kernel(
    temp, uvel, vvel, mask, dx_in, dy_in, spread_in, turn_in, levels_in,
    out, dx, dy, spread, turn, levels, wet, sems
):
    depth = temp.shape[0]
    north = sends_north(0)
    near = (ROWS - 1) * north
    far = near + 1 - 2 * north
    moves = [(mask.at[:, near, :], wet)]
    for number, field in enumerate((temp, uvel, vvel)):
        for place, row in ((2 * number, near), (2 * number + 1, far)):
            moves.append((field.at[:, row, :], out.at[place * depth : (place + 1) * depth, :]))
    moves += [(dx_in, dx), (dy_in, dy), (spread_in, spread), (turn_in, turn), (levels_in, levels)]
    copies = [pltpu.make_async_copy(*move, sems.at[i]) for i, move in enumerate(moves)]
    for copy in copies:
        copy.start()
    out[7 * depth :, :] = jnp.zeros((TILE, LANES), jnp.float32)
    copies[0].wait()
    out[6 * depth : 7 * depth, :] = wet[...].astype(jnp.float32)
    for copy in copies[1:]:
        copy.wait()


def own_slabs(fields, depth):
    group = lane_index(ROWS) // 4
    slabs = [jnp.zeros((ROWS, LANES), jnp.float32)] * (TAIL + 1)
    for number in range(depth):
        for index, field in enumerate(fields):
            slab, start = slab_place(number, index)
            moved = turn_lanes(level(field, number).astype(jnp.float32), start + 2)
            slabs[slab] = jnp.where(group == start // 4, moved, slabs[slab])
    return slabs


def edges_pack_kernel(
    temp, uvel, vvel, mask, after, second, third, zonal1, zonal2, edges, south, north
):
    depth = temp.shape[0] // ROWS
    for near, out in ((0, south), (ROWS - 1, north)):
        far = 1 if near == 0 else near - 1
        for number, field in enumerate((temp, uvel, vvel)):
            base = 2 * depth * number
            out[base : base + depth, :] = field[level_rows(near, depth), :]
            out[base + depth : base + 2 * depth, :] = field[level_rows(far, depth), :]
        out[6 * depth : 7 * depth, :] = mask[level_rows(near, depth), :].astype(jnp.float32)
        out[7 * depth :, :] = mask[level_rows(far, depth), :].astype(jnp.float32)
    sent = slice(0, 7 * depth)
    for exchange, out in ((1, second), (2, third)):
        out[sent, :] = jnp.where(sends_north(exchange) == 1, north[sent, :], south[sent, :])
    second[7 * depth :, :] = jnp.zeros((TILE, LANES), jnp.float32)
    slabs = own_slabs((temp, uvel, vvel, mask), depth)
    for number, slab in enumerate(slabs):
        edges[number * ROWS : (number + 1) * ROWS, :] = slab
    lane = lane_index(ROWS)
    lon_odd = lax.rem(lax.axis_index("lon"), 2)
    for out, column in ((zonal1, 2 * lon_odd), (zonal2, 2 - 2 * lon_odd)):
        source = 4 * (lane % 64 // 2) + lane % 2 + column

        def chosen(x):
            return jnp.take_along_axis(x, source, axis=1, mode="promise_in_bounds")

        for pair in range(2):
            both = jnp.where(lane < 64, chosen(slabs[2 * pair]), chosen(slabs[2 * pair + 1]))
            out[pair * ROWS : (pair + 1) * ROWS, :] = both
        out[2 * ROWS : 3 * ROWS, :] = chosen(slabs[TAIL])
        if out is zonal2:
            out[3 * ROWS :, :] = jnp.zeros((TILE, LANES), jnp.float32)


def columns_kernel(mixing, levels, solve, middle):
    depth = mixing.shape[0] // ROWS
    half = depth // 2
    active = levels[...]
    zero = jnp.zeros((ROWS, LANES), jnp.float32)

    def coupling(number):
        if 0 <= number < depth - 1:
            return jnp.where(number + 1 < active, level(mixing, number + 1), 0.0)
        return zero

    chains = [zero, zero]
    for step in range(half):
        for side, number in enumerate((step, depth - 1 - step)):
            above, below = coupling(number - 1), coupling(number)
            done, left = (above, below) if side == 0 else (below, above)
            inverse = 1.0 / (1.0 + left + done * (1.0 - chains[side]))
            chains[side] = left * inverse
            here = slice(number * ROWS, (number + 1) * ROWS)
            solve[0, here, :] = inverse
            solve[1, here, :] = done * inverse
            solve[2, here, :] = chains[side]
    middle[...] = 1.0 / (1.0 - chains[0] * chains[1])


def interior_kernel(temp, uvel, vvel, mask, inv_dx, inv_dy, spread, coriolis, prov, zeros):
    depth = temp.shape[0] // ROWS
    lane = lane_index(ROWS)
    row = lax.broadcasted_iota(jnp.int32, (ROWS, LANES), 0)
    spread_x = spread[...] * inv_dx[...] * inv_dx[...]
    spread_y = spread[...] * inv_dy[...] * inv_dy[...]
    scale_x = inv_dx[...] * (-1.0 / 24.0)
    scale_y = inv_dy[...] * (-1.0 / 24.0)
    turn = coriolis[...]

    def shifted_rows(ref, number, count):
        start = number * ROWS + count
        if start < 0 or start + ROWS > ref.shape[0]:
            return pltpu.roll(level(ref, number), -count % ROWS, 0)
        return ref[start : start + ROWS, :]

    def weights(face_low, face_high, speed_low, speed_high):
        return (
            speed_low,
            face_low - speed_high - 7.0 * speed_low,
            7.0 * (speed_high - speed_low) - face_low - face_high,
            face_high + speed_low + 7.0 * speed_high,
            -speed_high,
        )

    for number in range(depth):
        here = slice(number * ROWS, (number + 1) * ROWS)
        wet = level(mask, number).astype(jnp.float32)
        u, v = level(uvel, number), level(vvel, number)
        face_w = wet * jnp.where(lane >= 1, turn_lanes(wet, 1), 0.0)
        face_e = wet * jnp.where(lane < LANES - 1, turn_lanes(wet, -1), 0.0)
        face_s = wet * jnp.where(row >= 1, shifted_rows(mask, number, -1).astype(jnp.float32), 0.0)
        face_n = wet * jnp.where(row < ROWS - 1, shifted_rows(mask, number, 1).astype(jnp.float32), 0.0)
        west2, west, here_x, east, east2 = weights(
            spread_x * face_w,
            spread_x * face_e,
            scale_x * face_w * (turn_lanes(u, 1) + u),
            scale_x * face_e * (turn_lanes(u, -1) + u),
        )
        south2, south, here_y, north, north2 = weights(
            spread_y * face_s,
            spread_y * face_n,
            scale_y * face_s * (shifted_rows(vvel, number, -1) + v),
            scale_y * face_n * (shifted_rows(vvel, number, 1) + v),
        )
        south2 = jnp.where(row >= 2, south2, 0.0)
        south = jnp.where(row >= 1, south, 0.0)
        north = jnp.where(row < ROWS - 1, north, 0.0)
        north2 = jnp.where(row < ROWS - 2, north2, 0.0)
        middle = 1.0 + here_x + here_y
        wet_turn = wet * turn
        for index, ref in enumerate((temp, uvel, vvel)):
            q = level(ref, number)
            total = middle * q
            total += west * turn_lanes(q, 1) + east * turn_lanes(q, -1)
            total += west2 * turn_lanes(q, 2) + east2 * turn_lanes(q, -2)
            total += south * shifted_rows(ref, number, -1) + north * shifted_rows(ref, number, 1)
            total += south2 * shifted_rows(ref, number, -2) + north2 * shifted_rows(ref, number, 2)
            if index == 1:
                total += wet_turn * v
            if index == 2:
                total -= wet_turn * u
            prov[index, here, :] = total
            zeros[index, here, :] = jnp.zeros((ROWS, LANES), jnp.float32)


def put_row_ghosts(extra, mine, ghost, near, inv_dy, spread, flip):
    depth = extra.shape[1] // ROWS
    far, side = (1, 1.0) if near == 0 else (near - 1, -1.0)
    wet = piece(mine, 6, depth)
    face = piece(ghost, 6, depth) * wet
    face_next = wet * piece(mine, 7, depth)
    inv0 = inv_dy[near : near + 1, :]
    inv1 = inv_dy[far : far + 1, :] * -side
    mix0 = spread[near : near + 1, :] * inv0 * inv0
    inv0 = inv0 * side
    v0 = piece(mine, 4, depth)
    speed = face * (piece(ghost, 4, depth) * flip + v0) * (1.0 / 24.0)
    speed_next = face_next * (v0 + piece(mine, 5, depth)) * (1.0 / 24.0)
    for number in range(3):
        sign = 1.0 if number == 0 else flip
        g0 = piece(ghost, 2 * number, depth) * sign
        g1 = piece(ghost, 2 * number + 1, depth) * sign
        o0 = piece(mine, 2 * number, depth)
        o1 = piece(mine, 2 * number + 1, depth)
        advect = speed * (7.0 * (g0 + o0) - (g1 + o1))
        reach = speed_next * g0
        view = extra.at[number]
        view[level_rows(near, depth), :] = inv0 * (advect + reach) + mix0 * (face * (g0 - o0))
        view[level_rows(far, depth), :] = inv1 * reach


def column_ghosts(edges, other, west, inv_dx, spread):
    quad = lane_index(ROWS) % 4
    four = jnp.where(quad < 2, LANES - 2 + quad, quad - 2)
    side = jnp.where(west, 1, -1)

    def toward(x, count):
        return pltpu.roll(x, lax.rem(side * count + LANES, LANES), 1)

    def replicate(x):
        return jnp.take_along_axis(x, four, axis=1, mode="promise_in_bounds")

    wide = replicate(inv_dx[...])
    wide2 = replicate(spread[...]) * wide * wide
    wide = wide * side.astype(jnp.float32)
    own = [level(edges, s) for s in range(TAIL + 1)]
    ghost = quad * side < jnp.where(west, 2, -1)
    lane = lane_index(ROWS)
    place = 2 * (lane // 4) + lane % 2

    def spread_out(x, offset):
        return jnp.take_along_axis(x, place + offset, axis=1, mode="promise_in_bounds")

    theirs = [spread_out(level(other, s // 2), 64 * (s % 2)) for s in range(TAIL)]
    theirs.append(spread_out(level(other, 2), 0))
    both = [jnp.where(ghost, theirs[s], own[s]) for s in range(TAIL + 1)]
    near_lane = quad == jnp.where(west, 2, 1)

    def split(slabs):
        tail = [slabs[TAIL] if f == 0 else turn_lanes(slabs[TAIL], -32 * f) for f in range(4)]
        return [slabs[:TAIL], tail]

    corrections = []
    for part, mine in zip(split(both), split(own)):
        face = toward(part[3], 1) * part[3]
        speed = face * (toward(part[1], 1) + part[1]) * (1.0 / 24.0)
        speed_next = toward(speed, -1)
        result = []
        for number in range(3):
            q = part[number]
            ahead = toward(q, 1)
            advect = speed * (7.0 * (ahead + q) - (toward(q, 2) + toward(q, -1)))
            reach = speed_next * toward(q - mine[number], 1)
            near = wide * (advect + reach) + wide2 * (face * (ahead - q))
            result.append(jnp.where(near_lane, near, -wide * toward(reach, 1)))
        corrections.append(result)
    return corrections


def border_part(corrections, border, number, field):
    if number < 32:
        source, start = corrections[0][field], 4 * number
    else:
        source, start = corrections[1][field], 4 * (number - 32)
    return jnp.where(border, turn_lanes(source, -(start + 2)), 0.0)


def arrived_kernel(other, out):
    out[:TILE, :] = other[:TILE, :]


def columns_ghosts_kernel(edges, other, inv_dx, spread, out):
    west = lax.rem(lax.axis_index("lon"), 2) == 1
    for part, slabs in enumerate(column_ghosts(edges, other, west, inv_dx, spread)):
        for field in range(3):
            place = (3 * part + field) * ROWS
            out[place : place + ROWS, :] = slabs[field]


def finish_kernel(
    prov, extra_in, solve, middle, own_south, own_north, got0, got1, got2, edges, packed, second,
    inv_dx, inv_dy, spread, temp_new, uvel_new, vvel_new, extra, work, south, north, sems
):
    depth = prov.shape[1] // ROWS
    half = depth // 2
    used = slice(0, 7 * depth)
    lat = lax.axis_index("lat")
    fold = lat == lax.axis_size("lat") - 1

    def received(exchange):
        return jnp.where(
            exchange == 0, got0[used, :], jnp.where(exchange == 1, got1[used, :], got2[used, :])
        )

    odd = lax.rem(lax.axis_index("lon"), 2)
    columns = column_ghosts(edges, second, odd == 0, inv_dx, spread)
    lane = lane_index(7 * depth)
    lane = jnp.where(fold, LANES - 1 - lane, lane)
    north[...] = jnp.take_along_axis(received(lax.rem(lat, 3)), lane, axis=1, mode="promise_in_bounds")
    south[...] = jnp.where(lat == 0, 0.0, received(lax.rem(lat + 2, 3)))
    flip = jnp.where(fold, -1.0, 1.0)
    put_row_ghosts(extra, own_south, south, 0, inv_dy, spread, 1.0)
    put_row_ghosts(extra, own_north, north, ROWS - 1, inv_dy, spread, flip)

    lane = lane_index(ROWS)
    from_first = lane % 4 // 2 == odd
    corrections = [
        [jnp.where(from_first, level(packed, 3 * part + f), columns[part][f]) for f in range(3)]
        for part in range(2)
    ]
    border = (lane < 2) | (lane >= LANES - 2)

    def border_part(number, field):
        part, start = (0, 4 * number) if number < 32 else (1, 4 * (number - 32))
        return jnp.where(border, turn_lanes(corrections[part][field], -(start + 2)), 0.0)

    outs = (temp_new, uvel_new, vvel_new)
    zero = jnp.zeros((ROWS, LANES), jnp.float32)
    values = [[zero] * 3, [zero] * 3]
    for step in range(half):
        for side, number in enumerate((step, depth - 1 - step)):
            here = slice(number * ROWS, (number + 1) * ROWS)
            inverse, carry = solve[0, here, :], solve[1, here, :]
            for field in range(3):
                known = prov[field, here, :] + (extra[field, here, :] + border_part(number, field))
                value = inverse * known + carry * values[side][field]
                values[side][field] = value
                work[field, here, :] = value
    above, below = half - 1, half
    gain = level(solve.at[2], above)
    scale = middle[...]
    tops = [scale * (values[0][field] + gain * values[1][field]) for field in range(3)]
    for field in range(3):
        work[field, above * ROWS : (above + 1) * ROWS, :] = tops[field]
    chains = [list(tops), list(tops)]
    copies = []

    def store(start, stop):
        rows = pl.ds(start * ROWS, (stop - start) * ROWS)
        for field in range(3):
            copy = pltpu.make_async_copy(
                work.at[field, rows, :], outs[field].at[rows, :], sems.at[len(copies)]
            )
            copy.start()
            copies.append(copy)

    low, high = half, half
    for step in range(half):
        for side, number in enumerate((above - 1 - step, below + step)):
            if number < 0:
                continue
            here = slice(number * ROWS, (number + 1) * ROWS)
            gain = solve[2, here, :]
            for field in range(3):
                value = work[field, here, :] + gain * chains[side][field]
                chains[side][field] = value
                work[field, here, :] = value
        if step in STORE_AFTER:
            start, stop = max(above - 1 - step, 0), below + step + 1
            if low == high:
                store(start, stop)
            else:
                store(start, low)
                store(high, stop)
            low, high = start, stop
    for copy in copies:
        copy.wait()


def swaps(pairs):
    return [route for a, b in pairs for route in ((a, b), (b, a))]


def exchange_routes(lats, lons):
    def at(lat, lon):
        return lat * lons + lon % lons

    lon_first = [(at(l, c), at(l, c + 1)) for l in range(lats) for c in range(0, lons, 2)]
    lon_second = [(at(l, c), at(l, c + 1)) for l in range(lats) for c in range(1, lons, 2)]
    routes = [swaps(lon_first), swaps(lon_second)]
    for exchange in range(3):
        pairs, idle = [], set(range(lats))
        for l in range(exchange, lats, 3):
            if l == lats - 1:
                pairs += [(at(l, c), at(l, lons - 1 - c)) for c in range(lons // 2)]
            else:
                pairs += [(at(l, c), at(l + 1, c)) for c in range(lons)]
            idle -= {l, l + 1}
        pairs += [(at(l, c), at(l, c + 1)) for l in sorted(idle) for c in range(0, lons, 2)]
        routes.append(swaps(pairs))
    return routes


def per_device(
    temp, uvel, vvel, vert_mixing, inv_dx, inv_dy, horiz_mixing, coriolis, wet_mask, levels
):
    depth, rows, lanes = temp.shape
    assert (rows, lanes) == (ROWS, LANES) and depth == 40
    lats, lons = lax.axis_size("lat"), lax.axis_size("lon")
    assert lons % 2 == 0
    flat = depth * rows

    def f32(*shape):
        return jax.ShapeDtypeStruct(shape, jnp.float32)

    def vmem(*shape, dtype=jnp.float32):
        return pltpu.VMEM(shape, dtype)

    limit = pltpu.CompilerParams(vmem_limit_bytes=16 << 20)
    cheap = pl.CostEstimate(flops=1, bytes_accessed=1, transcendentals=0)
    both = ("lat", "lon")
    zonal_first, zonal_second, *meridional = exchange_routes(lats, lons)
    arrays = (temp, uvel, vvel, wet_mask, inv_dx, inv_dy, horiz_mixing, coriolis, levels)
    arrays = [pltpu.with_memory_space_constraint(x, pltpu.HBM) for x in arrays]
    sent0, inv_dx, inv_dy, horiz_mixing, coriolis, levels = pl.pallas_call(
        first_rows_kernel,
        name="first_rows",
        out_shape=(f32(7 * depth + TILE, lanes),)
        + (f32(rows, lanes),) * 4
        + (jax.ShapeDtypeStruct((rows, lanes), jnp.int32),),
        in_specs=[HBM] * 9,
        out_specs=(VMEM,) * 6,
        scratch_shapes=[vmem(depth, lanes, dtype=jnp.int32), pltpu.SemaphoreType.DMA((12,))],
        compiler_params=limit,
        cost_estimate=cheap,
    )(*arrays)
    got0 = lax.ppermute(sent0, both, meridional[0])
    temp, uvel, vvel, vert_mixing, wet_mask = (
        x.reshape(flat, lanes) for x in (temp, uvel, vvel, vert_mixing, wet_mask)
    )
    sent1, sent2, zonal1, zonal2, edges, own_south, own_north = pl.pallas_call(
        edges_pack_kernel,
        name="edges_pack",
        out_shape=(
            f32(7 * depth + TILE, lanes),
            f32(7 * depth, lanes),
            f32(3 * rows, lanes),
            f32(3 * rows + TILE, lanes),
            f32((TAIL + 1) * rows, lanes),
            f32(8 * depth, lanes),
            f32(8 * depth, lanes),
        ),
        in_specs=[VMEM] * 4 + [pl.BlockSpec(memory_space=pl.ANY)],
        out_specs=(VMEM,) * 7,
        compiler_params=limit,
        cost_estimate=cheap,
    )(temp, uvel, vvel, wet_mask, sent0)
    got1 = lax.ppermute(sent1, both, meridional[1])
    got2 = lax.ppermute(sent2, both, meridional[2])
    second = lax.ppermute(zonal2, both, zonal_second)
    first = lax.ppermute(zonal1, both, zonal_first)
    solve, middle = pl.pallas_call(
        columns_kernel,
        name="columns",
        out_shape=(f32(3, flat, lanes), f32(rows, lanes)),
        in_specs=[VMEM] * 2,
        out_specs=(VMEM,) * 2,
        compiler_params=limit,
        cost_estimate=cheap,
    )(vert_mixing, levels)
    prov, zeros = pl.pallas_call(
        interior_kernel,
        name="interior",
        out_shape=(f32(3, flat, lanes),) * 2,
        in_specs=[VMEM] * 8,
        out_specs=(VMEM,) * 2,
        compiler_params=limit,
        cost_estimate=cheap,
    )(temp, uvel, vvel, wet_mask, inv_dx, inv_dy, horiz_mixing, coriolis)
    packed = pl.pallas_call(
        columns_ghosts_kernel,
        name="columns_ghosts",
        out_shape=f32(6 * rows, lanes),
        in_specs=[VMEM] * 4,
        out_specs=VMEM,
        compiler_params=limit,
        cost_estimate=cheap,
    )(edges, first, inv_dx, horiz_mixing)
    second = pl.pallas_call(
        arrived_kernel,
        name="arrived",
        out_shape=f32(3 * rows + TILE, lanes),
        in_specs=[VMEM],
        out_specs=VMEM,
        input_output_aliases={0: 0},
        compiler_params=limit,
        cost_estimate=pl.CostEstimate(flops=1250000000, bytes_accessed=1, transcendentals=0),
    )(second)
    outs = pl.pallas_call(
        finish_kernel,
        name="finish",
        out_shape=(f32(flat, lanes),) * 3 + (f32(3, flat, lanes),),
        in_specs=[VMEM] * 15,
        out_specs=(HBM,) * 3 + (VMEM,),
        input_output_aliases={1: 3},
        scratch_shapes=[
            vmem(3, flat, lanes),
            vmem(7 * depth, lanes),
            vmem(7 * depth, lanes),
            pltpu.SemaphoreType.DMA((15,)),
        ],
        compiler_params=limit,
        cost_estimate=cheap,
    )(
        prov, zeros, solve, middle, own_south, own_north, got0, got1, got2, edges, packed, second,
        inv_dx, inv_dy, horiz_mixing,
    )
    return tuple(x.reshape(depth, rows, lanes) for x in outs[:3])


def solution(mesh):
    field, plane = P(None, "lat", "lon"), P("lat", "lon")
    return jax.shard_map(
        per_device,
        mesh=mesh,
        in_specs=(field,) * 4 + (plane,) * 4 + (field, plane),
        out_specs=(field,) * 3,
        check_vma=False,
    )
```

```python
import jax
import jax.numpy as jnp
from jax import lax
from jax.experimental import pallas as pl
from jax.experimental.pallas import tpu as pltpu
from jax.sharding import PartitionSpec as P

ROWS = 16
LANES = 128
TILE = 8
TAIL = 4
STORE_AFTER = ((9, 19), (9, 19), (9, 19))
VMEM = pl.BlockSpec(memory_space=pltpu.VMEM)
HBM = pl.BlockSpec(memory_space=pltpu.HBM)


def lane_index(rows):
    return lax.broadcasted_iota(jnp.int32, (rows, LANES), 1)


def turn_lanes(x, shift):
    return pltpu.roll(x, shift % LANES, 1)


def level_rows(row, depth):
    return pl.ds(row, depth, stride=ROWS)


def piece(ref, number, depth):
    return ref[number * depth : (number + 1) * depth, :]


def level(ref, number):
    return ref[number * ROWS : (number + 1) * ROWS, :]


def slab_place(number, field):
    if number < 32:
        return field, 4 * number
    return TAIL, 32 * field + 4 * (number - 32)


def sends_north(exchange):
    return jnp.where(lax.rem(lax.axis_index("lat"), 3) == exchange, 1, 0)


def first_rows_kernel(
    temp, uvel, vvel, mask, dx_in, dy_in, spread_in, turn_in, levels_in,
    out, dx, dy, spread, turn, levels, wet, sems
):
    depth = temp.shape[0]
    north = sends_north(0)
    near = (ROWS - 1) * north
    far = near + 1 - 2 * north
    moves = [(mask.at[:, near, :], wet)]
    for number, field in enumerate((temp, uvel, vvel)):
        for place, row in ((2 * number, near), (2 * number + 1, far)):
            moves.append((field.at[:, row, :], out.at[place * depth : (place + 1) * depth, :]))
    moves += [(dx_in, dx), (dy_in, dy), (spread_in, spread), (turn_in, turn), (levels_in, levels)]
    copies = [pltpu.make_async_copy(*move, sems.at[i]) for i, move in enumerate(moves)]
    for copy in copies:
        copy.start()
    out[7 * depth :, :] = jnp.zeros((TILE, LANES), jnp.float32)
    copies[0].wait()
    out[6 * depth : 7 * depth, :] = wet[...].astype(jnp.float32)
    for copy in copies[1:]:
        copy.wait()


def own_slabs(fields, depth):
    group = lane_index(ROWS) // 4
    slabs = [jnp.zeros((ROWS, LANES), jnp.float32)] * (TAIL + 1)
    for number in range(depth):
        for index, field in enumerate(fields):
            slab, start = slab_place(number, index)
            moved = turn_lanes(level(field, number).astype(jnp.float32), start + 2)
            slabs[slab] = jnp.where(group == start // 4, moved, slabs[slab])
    return slabs


def edges_pack_kernel(
    temp, uvel, vvel, mask, after, second, third, zonal1, zonal2, edges, south, north
):
    depth = temp.shape[0] // ROWS
    for near, out in ((0, south), (ROWS - 1, north)):
        far = 1 if near == 0 else near - 1
        for number, field in enumerate((temp, uvel, vvel)):
            base = 2 * depth * number
            out[base : base + depth, :] = field[level_rows(near, depth), :]
            out[base + depth : base + 2 * depth, :] = field[level_rows(far, depth), :]
        out[6 * depth : 7 * depth, :] = mask[level_rows(near, depth), :].astype(jnp.float32)
        out[7 * depth :, :] = mask[level_rows(far, depth), :].astype(jnp.float32)
    sent = slice(0, 7 * depth)
    for exchange, out in ((1, second), (2, third)):
        out[sent, :] = jnp.where(sends_north(exchange) == 1, north[sent, :], south[sent, :])
    second[7 * depth :, :] = jnp.zeros((TILE, LANES), jnp.float32)
    slabs = own_slabs((temp, uvel, vvel, mask), depth)
    for number, slab in enumerate(slabs):
        edges[number * ROWS : (number + 1) * ROWS, :] = slab
    lane = lane_index(ROWS)
    lon_odd = lax.rem(lax.axis_index("lon"), 2)
    for out, column in ((zonal1, 2 * lon_odd), (zonal2, 2 - 2 * lon_odd)):
        source = 4 * (lane % 64 // 2) + lane % 2 + column

        def chosen(x):
            return jnp.take_along_axis(x, source, axis=1, mode="promise_in_bounds")

        for pair in range(2):
            both = jnp.where(lane < 64, chosen(slabs[2 * pair]), chosen(slabs[2 * pair + 1]))
            out[pair * ROWS : (pair + 1) * ROWS, :] = both
        out[2 * ROWS : 3 * ROWS, :] = chosen(slabs[TAIL])
        if out is zonal2:
            out[3 * ROWS :, :] = jnp.zeros((TILE, LANES), jnp.float32)


def columns_kernel(mixing, levels, solve, middle):
    depth = mixing.shape[0] // ROWS
    half = depth // 2
    active = levels[...]
    zero = jnp.zeros((ROWS, LANES), jnp.float32)

    def coupling(number):
        if 0 <= number < depth - 1:
            return jnp.where(number + 1 < active, level(mixing, number + 1), 0.0)
        return zero

    chains = [zero, zero]
    for step in range(half):
        for side, number in enumerate((step, depth - 1 - step)):
            above, below = coupling(number - 1), coupling(number)
            done, left = (above, below) if side == 0 else (below, above)
            inverse = 1.0 / (1.0 + left + done * (1.0 - chains[side]))
            chains[side] = left * inverse
            here = slice(number * ROWS, (number + 1) * ROWS)
            solve[0, here, :] = inverse
            solve[1, here, :] = done * inverse
            solve[2, here, :] = chains[side]
    middle[...] = 1.0 / (1.0 - chains[0] * chains[1])


def interior_kernel(temp, uvel, vvel, mask, inv_dx, inv_dy, spread, coriolis, prov, zeros):
    depth = temp.shape[0] // ROWS
    lane = lane_index(ROWS)
    row = lax.broadcasted_iota(jnp.int32, (ROWS, LANES), 0)
    spread_x = spread[...] * inv_dx[...] * inv_dx[...]
    spread_y = spread[...] * inv_dy[...] * inv_dy[...]
    scale_x = inv_dx[...] * (-1.0 / 24.0)
    scale_y = inv_dy[...] * (-1.0 / 24.0)
    turn = coriolis[...]

    def shifted_rows(ref, number, count):
        start = number * ROWS + count
        if start < 0 or start + ROWS > ref.shape[0]:
            return pltpu.roll(level(ref, number), -count % ROWS, 0)
        return ref[start : start + ROWS, :]

    def weights(face_low, face_high, speed_low, speed_high):
        return (
            speed_low,
            face_low - speed_high - 7.0 * speed_low,
            7.0 * (speed_high - speed_low) - face_low - face_high,
            face_high + speed_low + 7.0 * speed_high,
            -speed_high,
        )

    for number in range(depth):
        here = slice(number * ROWS, (number + 1) * ROWS)
        wet = level(mask, number).astype(jnp.float32)
        u, v = level(uvel, number), level(vvel, number)
        face_w = wet * jnp.where(lane >= 1, turn_lanes(wet, 1), 0.0)
        face_e = wet * jnp.where(lane < LANES - 1, turn_lanes(wet, -1), 0.0)
        face_s = wet * jnp.where(row >= 1, shifted_rows(mask, number, -1).astype(jnp.float32), 0.0)
        face_n = wet * jnp.where(row < ROWS - 1, shifted_rows(mask, number, 1).astype(jnp.float32), 0.0)
        west2, west, here_x, east, east2 = weights(
            spread_x * face_w,
            spread_x * face_e,
            scale_x * face_w * (turn_lanes(u, 1) + u),
            scale_x * face_e * (turn_lanes(u, -1) + u),
        )
        south2, south, here_y, north, north2 = weights(
            spread_y * face_s,
            spread_y * face_n,
            scale_y * face_s * (shifted_rows(vvel, number, -1) + v),
            scale_y * face_n * (shifted_rows(vvel, number, 1) + v),
        )
        south2 = jnp.where(row >= 2, south2, 0.0)
        south = jnp.where(row >= 1, south, 0.0)
        north = jnp.where(row < ROWS - 1, north, 0.0)
        north2 = jnp.where(row < ROWS - 2, north2, 0.0)
        middle = 1.0 + here_x + here_y
        wet_turn = wet * turn
        for index, ref in enumerate((temp, uvel, vvel)):
            q = level(ref, number)
            total = middle * q
            total += west * turn_lanes(q, 1) + east * turn_lanes(q, -1)
            total += west2 * turn_lanes(q, 2) + east2 * turn_lanes(q, -2)
            total += south * shifted_rows(ref, number, -1) + north * shifted_rows(ref, number, 1)
            total += south2 * shifted_rows(ref, number, -2) + north2 * shifted_rows(ref, number, 2)
            if index == 1:
                total += wet_turn * v
            if index == 2:
                total -= wet_turn * u
            prov[index, here, :] = total
            zeros[index, here, :] = jnp.zeros((ROWS, LANES), jnp.float32)


def row_ghosts(extra, mine, ghost, near, inv_dy, spread, flip):
    depth = extra.shape[1] // ROWS
    far, side = (1, 1.0) if near == 0 else (near - 1, -1.0)
    wet = piece(mine, 6, depth)
    face = piece(ghost, 6, depth) * wet
    face_next = wet * piece(mine, 7, depth)
    inv0 = inv_dy[near : near + 1, :]
    inv1 = inv_dy[far : far + 1, :] * -side
    mix0 = spread[near : near + 1, :] * inv0 * inv0
    inv0 = inv0 * side
    v0 = piece(mine, 4, depth)
    speed = face * (piece(ghost, 4, depth) * flip + v0) * (1.0 / 24.0)
    speed_next = face_next * (v0 + piece(mine, 5, depth)) * (1.0 / 24.0)

    def put(number):
        sign = 1.0 if number == 0 else flip
        g0 = piece(ghost, 2 * number, depth) * sign
        g1 = piece(ghost, 2 * number + 1, depth) * sign
        o0 = piece(mine, 2 * number, depth)
        o1 = piece(mine, 2 * number + 1, depth)
        advect = speed * (7.0 * (g0 + o0) - (g1 + o1))
        reach = speed_next * g0
        view = extra.at[number]
        view[level_rows(near, depth), :] = inv0 * (advect + reach) + mix0 * (face * (g0 - o0))
        view[level_rows(far, depth), :] = inv1 * reach

    return put


def column_ghosts(edges, other, west, inv_dx, spread):
    quad = lane_index(ROWS) % 4
    four = jnp.where(quad < 2, LANES - 2 + quad, quad - 2)
    side = jnp.where(west, 1, -1)

    def toward(x, count):
        return pltpu.roll(x, lax.rem(side * count + LANES, LANES), 1)

    def replicate(x):
        return jnp.take_along_axis(x, four, axis=1, mode="promise_in_bounds")

    wide = replicate(inv_dx[...])
    wide2 = replicate(spread[...]) * wide * wide
    wide = wide * side.astype(jnp.float32)
    own = [level(edges, s) for s in range(TAIL + 1)]
    ghost = quad * side < jnp.where(west, 2, -1)
    lane = lane_index(ROWS)
    place = 2 * (lane // 4) + lane % 2

    def spread_out(x, offset):
        return jnp.take_along_axis(x, place + offset, axis=1, mode="promise_in_bounds")

    theirs = [spread_out(level(other, s // 2), 64 * (s % 2)) for s in range(TAIL)]
    theirs.append(spread_out(level(other, 2), 0))
    both = [jnp.where(ghost, theirs[s], own[s]) for s in range(TAIL + 1)]
    near_lane = quad == jnp.where(west, 2, 1)

    def split(slabs):
        tail = [slabs[TAIL] if f == 0 else turn_lanes(slabs[TAIL], -32 * f) for f in range(4)]
        return [slabs[:TAIL], tail]

    corrections = []
    for part, mine in zip(split(both), split(own)):
        face = toward(part[3], 1) * part[3]
        speed = face * (toward(part[1], 1) + part[1]) * (1.0 / 24.0)
        speed_next = toward(speed, -1)
        result = []
        for number in range(3):
            q = part[number]
            ahead = toward(q, 1)
            advect = speed * (7.0 * (ahead + q) - (toward(q, 2) + toward(q, -1)))
            reach = speed_next * toward(q - mine[number], 1)
            near = wide * (advect + reach) + wide2 * (face * (ahead - q))
            result.append(jnp.where(near_lane, near, -wide * toward(reach, 1)))
        corrections.append(result)
    return corrections


def border_part(corrections, border, number, field):
    if number < 32:
        source, start = corrections[0][field], 4 * number
    else:
        source, start = corrections[1][field], 4 * (number - 32)
    return jnp.where(border, turn_lanes(source, -(start + 2)), 0.0)


def arrived_kernel(other, out):
    out[:TILE, :] = other[:TILE, :]


def columns_ghosts_kernel(edges, other, inv_dx, spread, out):
    west = lax.rem(lax.axis_index("lon"), 2) == 1
    for part, slabs in enumerate(column_ghosts(edges, other, west, inv_dx, spread)):
        for field in range(3):
            place = (3 * part + field) * ROWS
            out[place : place + ROWS, :] = slabs[field]


def finish_kernel(
    prov, extra_in, solve, middle, own_south, own_north, got0, got1, got2, edges, packed, second,
    inv_dx, inv_dy, spread, temp_new, uvel_new, vvel_new, extra, work, south, north, sems
):
    depth = prov.shape[1] // ROWS
    half = depth // 2
    used = slice(0, 7 * depth)
    lat = lax.axis_index("lat")
    fold = lat == lax.axis_size("lat") - 1

    def received(exchange):
        return jnp.where(
            exchange == 0, got0[used, :], jnp.where(exchange == 1, got1[used, :], got2[used, :])
        )

    odd = lax.rem(lax.axis_index("lon"), 2)
    columns = column_ghosts(edges, second, odd == 0, inv_dx, spread)
    lane = lane_index(7 * depth)
    lane = jnp.where(fold, LANES - 1 - lane, lane)
    north[...] = jnp.take_along_axis(received(lax.rem(lat, 3)), lane, axis=1, mode="promise_in_bounds")
    south[...] = jnp.where(lat == 0, 0.0, received(lax.rem(lat + 2, 3)))
    flip = jnp.where(fold, -1.0, 1.0)
    put_south = row_ghosts(extra, own_south, south, 0, inv_dy, spread, 1.0)
    put_north = row_ghosts(extra, own_north, north, ROWS - 1, inv_dy, spread, flip)

    lane = lane_index(ROWS)
    from_first = lane % 4 // 2 == odd
    corrections = [
        [jnp.where(from_first, level(packed, 3 * part + f), columns[part][f]) for f in range(3)]
        for part in range(2)
    ]
    border = (lane < 2) | (lane >= LANES - 2)

    def border_part(number, field):
        part, start = (0, 4 * number) if number < 32 else (1, 4 * (number - 32))
        return jnp.where(border, turn_lanes(corrections[part][field], -(start + 2)), 0.0)

    outs = (temp_new, uvel_new, vvel_new)
    zero = jnp.zeros((ROWS, LANES), jnp.float32)
    above, below = half - 1, half
    copies = []
    for field in range(3):
        put_south(field)
        put_north(field)
        values = [zero, zero]
        for step in range(half):
            for side, number in enumerate((step, depth - 1 - step)):
                here = slice(number * ROWS, (number + 1) * ROWS)
                known = prov[field, here, :] + (extra[field, here, :] + border_part(number, field))
                values[side] = solve[0, here, :] * known + solve[1, here, :] * values[side]
                work[field, here, :] = values[side]
        gain = level(solve.at[2], above)
        top = middle[...] * (values[0] + gain * values[1])
        work[field, above * ROWS : (above + 1) * ROWS, :] = top
        chains = [top, top]
        low, high = half, half
        for step in range(half):
            for side, number in enumerate((above - 1 - step, below + step)):
                if number < 0:
                    continue
                here = slice(number * ROWS, (number + 1) * ROWS)
                chains[side] = work[field, here, :] + solve[2, here, :] * chains[side]
                work[field, here, :] = chains[side]
            if step in STORE_AFTER[field]:
                start, stop = max(above - 1 - step, 0), below + step + 1
                for first, last in ((start, stop),) if low == high else ((start, low), (high, stop)):
                    rows = pl.ds(first * ROWS, (last - first) * ROWS)
                    copy = pltpu.make_async_copy(
                        work.at[field, rows, :], outs[field].at[rows, :], sems.at[len(copies)]
                    )
                    copy.start()
                    copies.append(copy)
                low, high = start, stop
    for copy in copies:
        copy.wait()


def swaps(pairs):
    return [route for a, b in pairs for route in ((a, b), (b, a))]


def exchange_routes(lats, lons):
    def at(lat, lon):
        return lat * lons + lon % lons

    lon_first = [(at(l, c), at(l, c + 1)) for l in range(lats) for c in range(0, lons, 2)]
    lon_second = [(at(l, c), at(l, c + 1)) for l in range(lats) for c in range(1, lons, 2)]
    routes = [swaps(lon_first), swaps(lon_second)]
    for exchange in range(3):
        pairs, idle = [], set(range(lats))
        for l in range(exchange, lats, 3):
            if l == lats - 1:
                pairs += [(at(l, c), at(l, lons - 1 - c)) for c in range(lons // 2)]
            else:
                pairs += [(at(l, c), at(l + 1, c)) for c in range(lons)]
            idle -= {l, l + 1}
        pairs += [(at(l, c), at(l, c + 1)) for l in sorted(idle) for c in range(0, lons, 2)]
        routes.append(swaps(pairs))
    return routes


def per_device(
    temp, uvel, vvel, vert_mixing, inv_dx, inv_dy, horiz_mixing, coriolis, wet_mask, levels
):
    depth, rows, lanes = temp.shape
    assert (rows, lanes) == (ROWS, LANES) and depth == 40
    lats, lons = lax.axis_size("lat"), lax.axis_size("lon")
    assert lons % 2 == 0
    flat = depth * rows

    def f32(*shape):
        return jax.ShapeDtypeStruct(shape, jnp.float32)

    def vmem(*shape, dtype=jnp.float32):
        return pltpu.VMEM(shape, dtype)

    limit = pltpu.CompilerParams(vmem_limit_bytes=16 << 20)
    cheap = pl.CostEstimate(flops=1, bytes_accessed=1, transcendentals=0)
    both = ("lat", "lon")
    zonal_first, zonal_second, *meridional = exchange_routes(lats, lons)
    arrays = (temp, uvel, vvel, wet_mask, inv_dx, inv_dy, horiz_mixing, coriolis, levels)
    arrays = [pltpu.with_memory_space_constraint(x, pltpu.HBM) for x in arrays]
    sent0, inv_dx, inv_dy, horiz_mixing, coriolis, levels = pl.pallas_call(
        first_rows_kernel,
        name="first_rows",
        out_shape=(f32(7 * depth + TILE, lanes),)
        + (f32(rows, lanes),) * 4
        + (jax.ShapeDtypeStruct((rows, lanes), jnp.int32),),
        in_specs=[HBM] * 9,
        out_specs=(VMEM,) * 6,
        scratch_shapes=[vmem(depth, lanes, dtype=jnp.int32), pltpu.SemaphoreType.DMA((12,))],
        compiler_params=limit,
        cost_estimate=cheap,
    )(*arrays)
    got0 = lax.ppermute(sent0, both, meridional[0])
    temp, uvel, vvel, vert_mixing, wet_mask = (
        x.reshape(flat, lanes) for x in (temp, uvel, vvel, vert_mixing, wet_mask)
    )
    sent1, sent2, zonal1, zonal2, edges, own_south, own_north = pl.pallas_call(
        edges_pack_kernel,
        name="edges_pack",
        out_shape=(
            f32(7 * depth + TILE, lanes),
            f32(7 * depth, lanes),
            f32(3 * rows, lanes),
            f32(3 * rows + TILE, lanes),
            f32((TAIL + 1) * rows, lanes),
            f32(8 * depth, lanes),
            f32(8 * depth, lanes),
        ),
        in_specs=[VMEM] * 4 + [pl.BlockSpec(memory_space=pl.ANY)],
        out_specs=(VMEM,) * 7,
        compiler_params=limit,
        cost_estimate=cheap,
    )(temp, uvel, vvel, wet_mask, sent0)
    got1 = lax.ppermute(sent1, both, meridional[1])
    got2 = lax.ppermute(sent2, both, meridional[2])
    second = lax.ppermute(zonal2, both, zonal_second)
    first = lax.ppermute(zonal1, both, zonal_first)
    solve, middle = pl.pallas_call(
        columns_kernel,
        name="columns",
        out_shape=(f32(3, flat, lanes), f32(rows, lanes)),
        in_specs=[VMEM] * 2,
        out_specs=(VMEM,) * 2,
        compiler_params=limit,
        cost_estimate=cheap,
    )(vert_mixing, levels)
    prov, zeros = pl.pallas_call(
        interior_kernel,
        name="interior",
        out_shape=(f32(3, flat, lanes),) * 2,
        in_specs=[VMEM] * 8,
        out_specs=(VMEM,) * 2,
        compiler_params=limit,
        cost_estimate=cheap,
    )(temp, uvel, vvel, wet_mask, inv_dx, inv_dy, horiz_mixing, coriolis)
    packed = pl.pallas_call(
        columns_ghosts_kernel,
        name="columns_ghosts",
        out_shape=f32(6 * rows, lanes),
        in_specs=[VMEM] * 4,
        out_specs=VMEM,
        compiler_params=limit,
        cost_estimate=cheap,
    )(edges, first, inv_dx, horiz_mixing)
    second = pl.pallas_call(
        arrived_kernel,
        name="arrived",
        out_shape=f32(3 * rows + TILE, lanes),
        in_specs=[VMEM],
        out_specs=VMEM,
        input_output_aliases={0: 0},
        compiler_params=limit,
        cost_estimate=pl.CostEstimate(flops=1250000000, bytes_accessed=1, transcendentals=0),
    )(second)
    outs = pl.pallas_call(
        finish_kernel,
        name="finish",
        out_shape=(f32(flat, lanes),) * 3 + (f32(3, flat, lanes),),
        in_specs=[VMEM] * 15,
        out_specs=(HBM,) * 3 + (VMEM,),
        input_output_aliases={1: 3},
        scratch_shapes=[
            vmem(3, flat, lanes),
            vmem(7 * depth, lanes),
            vmem(7 * depth, lanes),
            pltpu.SemaphoreType.DMA((15,)),
        ],
        compiler_params=limit,
        cost_estimate=cheap,
    )(
        prov, zeros, solve, middle, own_south, own_north, got0, got1, got2, edges, packed, second,
        inv_dx, inv_dy, horiz_mixing,
    )
    return tuple(x.reshape(depth, rows, lanes) for x in outs[:3])


def solution(mesh):
    field, plane = P(None, "lat", "lon"), P("lat", "lon")
    return jax.shard_map(
        per_device,
        mesh=mesh,
        in_specs=(field,) * 4 + (plane,) * 4 + (field, plane),
        out_specs=(field,) * 3,
        check_vma=False,
    )
```

```python
import jax
import jax.numpy as jnp
from jax import lax
from jax.experimental import pallas as pl
from jax.experimental.pallas import tpu as pltpu
from jax.sharding import PartitionSpec as P

ROWS = 16
LANES = 128
TILE = 8
TAIL = 4
STORE_AFTER = ((9, 19), (9, 19), (9, 19))
VMEM = pl.BlockSpec(memory_space=pltpu.VMEM)
HBM = pl.BlockSpec(memory_space=pltpu.HBM)


def lane_index(rows):
    return lax.broadcasted_iota(jnp.int32, (rows, LANES), 1)


def turn_lanes(x, shift):
    return pltpu.roll(x, shift % LANES, 1)


def level_rows(row, depth):
    return pl.ds(row, depth, stride=ROWS)


def piece(ref, number, depth):
    return ref[number * depth : (number + 1) * depth, :]


def level(ref, number):
    return ref[number * ROWS : (number + 1) * ROWS, :]


def slab_place(number, field):
    if number < 32:
        return field, 4 * number
    return TAIL, 32 * field + 4 * (number - 32)


def sends_north(exchange):
    return jnp.where(lax.rem(lax.axis_index("lat"), 3) == exchange, 1, 0)


def first_rows_kernel(
    temp, uvel, vvel, mask, dx_in, dy_in, spread_in, turn_in, levels_in,
    out, dx, dy, spread, turn, levels, wet, sems
):
    depth = temp.shape[0]
    north = sends_north(0)
    near = (ROWS - 1) * north
    far = near + 1 - 2 * north
    moves = [(mask.at[:, near, :], wet)]
    for number, field in enumerate((temp, uvel, vvel)):
        for place, row in ((2 * number, near), (2 * number + 1, far)):
            moves.append((field.at[:, row, :], out.at[place * depth : (place + 1) * depth, :]))
    moves += [(dx_in, dx), (dy_in, dy), (spread_in, spread), (turn_in, turn), (levels_in, levels)]
    copies = [pltpu.make_async_copy(*move, sems.at[i]) for i, move in enumerate(moves)]
    for copy in copies:
        copy.start()
    out[7 * depth :, :] = jnp.zeros((TILE, LANES), jnp.float32)
    copies[0].wait()
    out[6 * depth : 7 * depth, :] = wet[...].astype(jnp.float32)
    for copy in copies[1:]:
        copy.wait()


def own_slabs(fields, depth):
    group = lane_index(ROWS) // 4
    slabs = [jnp.zeros((ROWS, LANES), jnp.float32)] * (TAIL + 1)
    for number in range(depth):
        for index, field in enumerate(fields):
            slab, start = slab_place(number, index)
            moved = turn_lanes(level(field, number).astype(jnp.float32), start + 2)
            slabs[slab] = jnp.where(group == start // 4, moved, slabs[slab])
    return slabs


def edges_pack_kernel(
    temp, uvel, vvel, mask, after, second, third, zonal1, zonal2, edges, south, north
):
    depth = temp.shape[0] // ROWS
    for near, out in ((0, south), (ROWS - 1, north)):
        far = 1 if near == 0 else near - 1
        for number, field in enumerate((temp, uvel, vvel)):
            base = 2 * depth * number
            out[base : base + depth, :] = field[level_rows(near, depth), :]
            out[base + depth : base + 2 * depth, :] = field[level_rows(far, depth), :]
        out[6 * depth : 7 * depth, :] = mask[level_rows(near, depth), :].astype(jnp.float32)
        out[7 * depth :, :] = mask[level_rows(far, depth), :].astype(jnp.float32)
    sent = slice(0, 7 * depth)
    for exchange, out in ((1, second), (2, third)):
        out[sent, :] = jnp.where(sends_north(exchange) == 1, north[sent, :], south[sent, :])
    second[7 * depth :, :] = jnp.zeros((TILE, LANES), jnp.float32)
    slabs = own_slabs((temp, uvel, vvel, mask), depth)
    for number, slab in enumerate(slabs):
        edges[number * ROWS : (number + 1) * ROWS, :] = slab
    lane = lane_index(ROWS)
    lon_odd = lax.rem(lax.axis_index("lon"), 2)
    for out, column in ((zonal1, 2 * lon_odd), (zonal2, 2 - 2 * lon_odd)):
        source = 4 * (lane % 64 // 2) + lane % 2 + column

        def chosen(x):
            return jnp.take_along_axis(x, source, axis=1, mode="promise_in_bounds")

        for pair in range(2):
            both = jnp.where(lane < 64, chosen(slabs[2 * pair]), chosen(slabs[2 * pair + 1]))
            out[pair * ROWS : (pair + 1) * ROWS, :] = both
        last = chosen(slabs[TAIL])
        place = 2 * ROWS
        out[place : place + TILE, :] = jnp.where(lane[:TILE] < 64, last[:TILE], last[TILE:])
        if out is zonal2:
            out[place + TILE :, :] = jnp.zeros((TILE, LANES), jnp.float32)


def columns_kernel(mixing, levels, solve, middle):
    depth = mixing.shape[0] // ROWS
    half = depth // 2
    active = levels[...]
    zero = jnp.zeros((ROWS, LANES), jnp.float32)

    def coupling(number):
        if 0 <= number < depth - 1:
            return jnp.where(number + 1 < active, level(mixing, number + 1), 0.0)
        return zero

    chains = [zero, zero]
    for step in range(half):
        for side, number in enumerate((step, depth - 1 - step)):
            above, below = coupling(number - 1), coupling(number)
            done, left = (above, below) if side == 0 else (below, above)
            inverse = 1.0 / (1.0 + left + done * (1.0 - chains[side]))
            chains[side] = left * inverse
            here = slice(number * ROWS, (number + 1) * ROWS)
            solve[0, here, :] = inverse
            solve[1, here, :] = done * inverse
            solve[2, here, :] = chains[side]
    middle[...] = 1.0 / (1.0 - chains[0] * chains[1])


def interior_kernel(temp, uvel, vvel, mask, inv_dx, inv_dy, spread, coriolis, prov, zeros):
    depth = temp.shape[0] // ROWS
    lane = lane_index(ROWS)
    row = lax.broadcasted_iota(jnp.int32, (ROWS, LANES), 0)
    spread_x = spread[...] * inv_dx[...] * inv_dx[...]
    spread_y = spread[...] * inv_dy[...] * inv_dy[...]
    scale_x = inv_dx[...] * (-1.0 / 24.0)
    scale_y = inv_dy[...] * (-1.0 / 24.0)
    turn = coriolis[...]

    def shifted_rows(ref, number, count):
        start = number * ROWS + count
        if start < 0 or start + ROWS > ref.shape[0]:
            return pltpu.roll(level(ref, number), -count % ROWS, 0)
        return ref[start : start + ROWS, :]

    def weights(face_low, face_high, speed_low, speed_high):
        return (
            speed_low,
            face_low - speed_high - 7.0 * speed_low,
            7.0 * (speed_high - speed_low) - face_low - face_high,
            face_high + speed_low + 7.0 * speed_high,
            -speed_high,
        )

    for number in range(depth):
        here = slice(number * ROWS, (number + 1) * ROWS)
        wet = level(mask, number).astype(jnp.float32)
        u, v = level(uvel, number), level(vvel, number)
        face_w = wet * jnp.where(lane >= 1, turn_lanes(wet, 1), 0.0)
        face_e = wet * jnp.where(lane < LANES - 1, turn_lanes(wet, -1), 0.0)
        face_s = wet * jnp.where(row >= 1, shifted_rows(mask, number, -1).astype(jnp.float32), 0.0)
        face_n = wet * jnp.where(row < ROWS - 1, shifted_rows(mask, number, 1).astype(jnp.float32), 0.0)
        west2, west, here_x, east, east2 = weights(
            spread_x * face_w,
            spread_x * face_e,
            scale_x * face_w * (turn_lanes(u, 1) + u),
            scale_x * face_e * (turn_lanes(u, -1) + u),
        )
        south2, south, here_y, north, north2 = weights(
            spread_y * face_s,
            spread_y * face_n,
            scale_y * face_s * (shifted_rows(vvel, number, -1) + v),
            scale_y * face_n * (shifted_rows(vvel, number, 1) + v),
        )
        south2 = jnp.where(row >= 2, south2, 0.0)
        south = jnp.where(row >= 1, south, 0.0)
        north = jnp.where(row < ROWS - 1, north, 0.0)
        north2 = jnp.where(row < ROWS - 2, north2, 0.0)
        middle = 1.0 + here_x + here_y
        wet_turn = wet * turn
        for index, ref in enumerate((temp, uvel, vvel)):
            q = level(ref, number)
            total = middle * q
            total += west * turn_lanes(q, 1) + east * turn_lanes(q, -1)
            total += west2 * turn_lanes(q, 2) + east2 * turn_lanes(q, -2)
            total += south * shifted_rows(ref, number, -1) + north * shifted_rows(ref, number, 1)
            total += south2 * shifted_rows(ref, number, -2) + north2 * shifted_rows(ref, number, 2)
            if index == 1:
                total += wet_turn * v
            if index == 2:
                total -= wet_turn * u
            prov[index, here, :] = total
            zeros[index, here, :] = jnp.zeros((ROWS, LANES), jnp.float32)


def row_ghosts(extra, mine, ghost, near, inv_dy, spread, flip):
    depth = extra.shape[1] // ROWS
    far, side = (1, 1.0) if near == 0 else (near - 1, -1.0)
    wet = piece(mine, 6, depth)
    face = piece(ghost, 6, depth) * wet
    face_next = wet * piece(mine, 7, depth)
    inv0 = inv_dy[near : near + 1, :]
    inv1 = inv_dy[far : far + 1, :] * -side
    mix0 = spread[near : near + 1, :] * inv0 * inv0
    inv0 = inv0 * side
    v0 = piece(mine, 4, depth)
    speed = face * (piece(ghost, 4, depth) * flip + v0) * (1.0 / 24.0)
    speed_next = face_next * (v0 + piece(mine, 5, depth)) * (1.0 / 24.0)

    def put(number):
        sign = 1.0 if number == 0 else flip
        g0 = piece(ghost, 2 * number, depth) * sign
        g1 = piece(ghost, 2 * number + 1, depth) * sign
        o0 = piece(mine, 2 * number, depth)
        o1 = piece(mine, 2 * number + 1, depth)
        advect = speed * (7.0 * (g0 + o0) - (g1 + o1))
        reach = speed_next * g0
        view = extra.at[number]
        view[level_rows(near, depth), :] = inv0 * (advect + reach) + mix0 * (face * (g0 - o0))
        view[level_rows(far, depth), :] = inv1 * reach

    return put


def column_ghosts(edges, other, west, inv_dx, spread):
    quad = lane_index(ROWS) % 4
    four = jnp.where(quad < 2, LANES - 2 + quad, quad - 2)
    side = jnp.where(west, 1, -1)

    def toward(x, count):
        return pltpu.roll(x, lax.rem(side * count + LANES, LANES), 1)

    def replicate(x):
        return jnp.take_along_axis(x, four, axis=1, mode="promise_in_bounds")

    wide = replicate(inv_dx[...])
    wide2 = replicate(spread[...]) * wide * wide
    wide = wide * side.astype(jnp.float32)
    own = [level(edges, s) for s in range(TAIL + 1)]
    ghost = quad * side < jnp.where(west, 2, -1)
    lane = lane_index(ROWS)
    place = 2 * (lane // 4) + lane % 2

    def spread_out(x, offset):
        return jnp.take_along_axis(x, place + offset, axis=1, mode="promise_in_bounds")

    theirs = [spread_out(level(other, s // 2), 64 * (s % 2)) for s in range(TAIL)]
    halves = jnp.concatenate([other[2 * ROWS : 2 * ROWS + TILE, :]] * 2, axis=0)
    bottom = lax.broadcasted_iota(jnp.int32, (ROWS, LANES), 0) // TILE
    theirs.append(spread_out(halves, 64 * bottom))
    both = [jnp.where(ghost, theirs[s], own[s]) for s in range(TAIL + 1)]
    near_lane = quad == jnp.where(west, 2, 1)

    def split(slabs):
        tail = [slabs[TAIL] if f == 0 else turn_lanes(slabs[TAIL], -32 * f) for f in range(4)]
        return [slabs[:TAIL], tail]

    corrections = []
    for part, mine in zip(split(both), split(own)):
        face = toward(part[3], 1) * part[3]
        speed = face * (toward(part[1], 1) + part[1]) * (1.0 / 24.0)
        speed_next = toward(speed, -1)
        result = []
        for number in range(3):
            q = part[number]
            ahead = toward(q, 1)
            advect = speed * (7.0 * (ahead + q) - (toward(q, 2) + toward(q, -1)))
            reach = speed_next * toward(q - mine[number], 1)
            near = wide * (advect + reach) + wide2 * (face * (ahead - q))
            result.append(jnp.where(near_lane, near, -wide * toward(reach, 1)))
        corrections.append(result)
    return corrections


def border_part(corrections, border, number, field):
    if number < 32:
        source, start = corrections[0][field], 4 * number
    else:
        source, start = corrections[1][field], 4 * (number - 32)
    return jnp.where(border, turn_lanes(source, -(start + 2)), 0.0)


def arrived_kernel(other, out):
    out[:TILE, :] = other[:TILE, :]


def columns_ghosts_kernel(edges, other, inv_dx, spread, out):
    west = lax.rem(lax.axis_index("lon"), 2) == 1
    for part, slabs in enumerate(column_ghosts(edges, other, west, inv_dx, spread)):
        for field in range(3):
            place = (3 * part + field) * ROWS
            out[place : place + ROWS, :] = slabs[field]


def finish_kernel(
    prov, extra_in, solve, middle, own_south, own_north, got0, got1, got2, edges, packed, second,
    inv_dx, inv_dy, spread, temp_new, uvel_new, vvel_new, extra, work, south, north, sems
):
    depth = prov.shape[1] // ROWS
    half = depth // 2
    used = slice(0, 7 * depth)
    lat = lax.axis_index("lat")
    fold = lat == lax.axis_size("lat") - 1

    def received(exchange):
        return jnp.where(
            exchange == 0, got0[used, :], jnp.where(exchange == 1, got1[used, :], got2[used, :])
        )

    odd = lax.rem(lax.axis_index("lon"), 2)
    columns = column_ghosts(edges, second, odd == 0, inv_dx, spread)
    lane = lane_index(7 * depth)
    lane = jnp.where(fold, LANES - 1 - lane, lane)
    north[...] = jnp.take_along_axis(received(lax.rem(lat, 3)), lane, axis=1, mode="promise_in_bounds")
    south[...] = jnp.where(lat == 0, 0.0, received(lax.rem(lat + 2, 3)))
    flip = jnp.where(fold, -1.0, 1.0)
    put_south = row_ghosts(extra, own_south, south, 0, inv_dy, spread, 1.0)
    put_north = row_ghosts(extra, own_north, north, ROWS - 1, inv_dy, spread, flip)

    lane = lane_index(ROWS)
    from_first = lane % 4 // 2 == odd
    corrections = [
        [jnp.where(from_first, level(packed, 3 * part + f), columns[part][f]) for f in range(3)]
        for part in range(2)
    ]
    border = (lane < 2) | (lane >= LANES - 2)

    def border_part(number, field):
        part, start = (0, 4 * number) if number < 32 else (1, 4 * (number - 32))
        return jnp.where(border, turn_lanes(corrections[part][field], -(start + 2)), 0.0)

    outs = (temp_new, uvel_new, vvel_new)
    zero = jnp.zeros((ROWS, LANES), jnp.float32)
    above, below = half - 1, half
    copies = []
    for field in range(3):
        put_south(field)
        put_north(field)
        values = [zero, zero]
        for step in range(half):
            for side, number in enumerate((step, depth - 1 - step)):
                here = slice(number * ROWS, (number + 1) * ROWS)
                known = prov[field, here, :] + (extra[field, here, :] + border_part(number, field))
                values[side] = solve[0, here, :] * known + solve[1, here, :] * values[side]
                work[field, here, :] = values[side]
        gain = level(solve.at[2], above)
        top = middle[...] * (values[0] + gain * values[1])
        work[field, above * ROWS : (above + 1) * ROWS, :] = top
        chains = [top, top]
        low, high = half, half
        for step in range(half):
            for side, number in enumerate((above - 1 - step, below + step)):
                if number < 0:
                    continue
                here = slice(number * ROWS, (number + 1) * ROWS)
                chains[side] = work[field, here, :] + solve[2, here, :] * chains[side]
                work[field, here, :] = chains[side]
            if step in STORE_AFTER[field]:
                start, stop = max(above - 1 - step, 0), below + step + 1
                for first, last in ((start, stop),) if low == high else ((start, low), (high, stop)):
                    rows = pl.ds(first * ROWS, (last - first) * ROWS)
                    copy = pltpu.make_async_copy(
                        work.at[field, rows, :], outs[field].at[rows, :], sems.at[len(copies)]
                    )
                    copy.start()
                    copies.append(copy)
                low, high = start, stop
    for copy in copies:
        copy.wait()


def swaps(pairs):
    return [route for a, b in pairs for route in ((a, b), (b, a))]


def exchange_routes(lats, lons):
    def at(lat, lon):
        return lat * lons + lon % lons

    lon_first = [(at(l, c), at(l, c + 1)) for l in range(lats) for c in range(0, lons, 2)]
    lon_second = [(at(l, c), at(l, c + 1)) for l in range(lats) for c in range(1, lons, 2)]
    routes = [swaps(lon_first), swaps(lon_second)]
    for exchange in range(3):
        pairs, idle = [], set(range(lats))
        for l in range(exchange, lats, 3):
            if l == lats - 1:
                pairs += [(at(l, c), at(l, lons - 1 - c)) for c in range(lons // 2)]
            else:
                pairs += [(at(l, c), at(l + 1, c)) for c in range(lons)]
            idle -= {l, l + 1}
        pairs += [(at(l, c), at(l, c + 1)) for l in sorted(idle) for c in range(0, lons, 2)]
        routes.append(swaps(pairs))
    return routes


def per_device(
    temp, uvel, vvel, vert_mixing, inv_dx, inv_dy, horiz_mixing, coriolis, wet_mask, levels
):
    depth, rows, lanes = temp.shape
    assert (rows, lanes) == (ROWS, LANES) and depth == 40
    lats, lons = lax.axis_size("lat"), lax.axis_size("lon")
    assert lons % 2 == 0
    flat = depth * rows

    def f32(*shape):
        return jax.ShapeDtypeStruct(shape, jnp.float32)

    def vmem(*shape, dtype=jnp.float32):
        return pltpu.VMEM(shape, dtype)

    limit = pltpu.CompilerParams(vmem_limit_bytes=16 << 20)
    cheap = pl.CostEstimate(flops=1, bytes_accessed=1, transcendentals=0)
    both = ("lat", "lon")
    zonal_first, zonal_second, *meridional = exchange_routes(lats, lons)
    arrays = (temp, uvel, vvel, wet_mask, inv_dx, inv_dy, horiz_mixing, coriolis, levels)
    arrays = [pltpu.with_memory_space_constraint(x, pltpu.HBM) for x in arrays]
    sent0, inv_dx, inv_dy, horiz_mixing, coriolis, levels = pl.pallas_call(
        first_rows_kernel,
        name="first_rows",
        out_shape=(f32(7 * depth + TILE, lanes),)
        + (f32(rows, lanes),) * 4
        + (jax.ShapeDtypeStruct((rows, lanes), jnp.int32),),
        in_specs=[HBM] * 9,
        out_specs=(VMEM,) * 6,
        scratch_shapes=[vmem(depth, lanes, dtype=jnp.int32), pltpu.SemaphoreType.DMA((12,))],
        compiler_params=limit,
        cost_estimate=cheap,
    )(*arrays)
    got0 = lax.ppermute(sent0, both, meridional[0])
    temp, uvel, vvel, vert_mixing, wet_mask = (
        x.reshape(flat, lanes) for x in (temp, uvel, vvel, vert_mixing, wet_mask)
    )
    sent1, sent2, zonal1, zonal2, edges, own_south, own_north = pl.pallas_call(
        edges_pack_kernel,
        name="edges_pack",
        out_shape=(
            f32(7 * depth + TILE, lanes),
            f32(7 * depth, lanes),
            f32(2 * rows + TILE, lanes),
            f32(3 * rows, lanes),
            f32((TAIL + 1) * rows, lanes),
            f32(8 * depth, lanes),
            f32(8 * depth, lanes),
        ),
        in_specs=[VMEM] * 4 + [pl.BlockSpec(memory_space=pl.ANY)],
        out_specs=(VMEM,) * 7,
        compiler_params=limit,
        cost_estimate=cheap,
    )(temp, uvel, vvel, wet_mask, sent0)
    got1 = lax.ppermute(sent1, both, meridional[1])
    got2 = lax.ppermute(sent2, both, meridional[2])
    second = lax.ppermute(zonal2, both, zonal_second)
    first = lax.ppermute(zonal1, both, zonal_first)
    solve, middle = pl.pallas_call(
        columns_kernel,
        name="columns",
        out_shape=(f32(3, flat, lanes), f32(rows, lanes)),
        in_specs=[VMEM] * 2,
        out_specs=(VMEM,) * 2,
        compiler_params=limit,
        cost_estimate=cheap,
    )(vert_mixing, levels)
    prov, zeros = pl.pallas_call(
        interior_kernel,
        name="interior",
        out_shape=(f32(3, flat, lanes),) * 2,
        in_specs=[VMEM] * 8,
        out_specs=(VMEM,) * 2,
        compiler_params=limit,
        cost_estimate=cheap,
    )(temp, uvel, vvel, wet_mask, inv_dx, inv_dy, horiz_mixing, coriolis)
    packed = pl.pallas_call(
        columns_ghosts_kernel,
        name="columns_ghosts",
        out_shape=f32(6 * rows, lanes),
        in_specs=[VMEM] * 4,
        out_specs=VMEM,
        compiler_params=limit,
        cost_estimate=cheap,
    )(edges, first, inv_dx, horiz_mixing)
    second = pl.pallas_call(
        arrived_kernel,
        name="arrived",
        out_shape=f32(3 * rows, lanes),
        in_specs=[VMEM],
        out_specs=VMEM,
        input_output_aliases={0: 0},
        compiler_params=limit,
        cost_estimate=pl.CostEstimate(flops=1280000000, bytes_accessed=1, transcendentals=0),
    )(second)
    outs = pl.pallas_call(
        finish_kernel,
        name="finish",
        out_shape=(f32(flat, lanes),) * 3 + (f32(3, flat, lanes),),
        in_specs=[VMEM] * 15,
        out_specs=(HBM,) * 3 + (VMEM,),
        input_output_aliases={1: 3},
        scratch_shapes=[
            vmem(3, flat, lanes),
            vmem(7 * depth, lanes),
            vmem(7 * depth, lanes),
            pltpu.SemaphoreType.DMA((15,)),
        ],
        compiler_params=limit,
        cost_estimate=cheap,
    )(
        prov, zeros, solve, middle, own_south, own_north, got0, got1, got2, edges, packed, second,
        inv_dx, inv_dy, horiz_mixing,
    )
    return tuple(x.reshape(depth, rows, lanes) for x in outs[:3])


def solution(mesh):
    field, plane = P(None, "lat", "lon"), P("lat", "lon")
    return jax.shard_map(
        per_device,
        mesh=mesh,
        in_specs=(field,) * 4 + (plane,) * 4 + (field, plane),
        out_specs=(field,) * 3,
        check_vma=False,
    )
```

```python
import jax
import jax.numpy as jnp
from jax import lax
from jax.experimental import pallas as pl
from jax.experimental.pallas import tpu as pltpu
from jax.sharding import PartitionSpec as P

ROWS = 16
LANES = 128
TILE = 8
TAIL = 4
STORE_AFTER = ((9, 19), (9, 19), (9, 19))
VMEM = pl.BlockSpec(memory_space=pltpu.VMEM)
HBM = pl.BlockSpec(memory_space=pltpu.HBM)


def lane_index(rows):
    return lax.broadcasted_iota(jnp.int32, (rows, LANES), 1)


def turn_lanes(x, shift):
    return pltpu.roll(x, shift % LANES, 1)


def level_rows(row, depth):
    return pl.ds(row, depth, stride=ROWS)


def piece(ref, number, depth):
    return ref[number * depth : (number + 1) * depth, :]


def level(ref, number):
    return ref[number * ROWS : (number + 1) * ROWS, :]


def slab_place(number, field):
    if number < 32:
        return field, 4 * number
    return TAIL, 32 * field + 4 * (number - 32)


def sends_north(exchange):
    return jnp.where(lax.rem(lax.axis_index("lat"), 3) == exchange, 1, 0)


def first_rows_kernel(
    temp, uvel, vvel, mask, dx_in, dy_in, spread_in, turn_in, levels_in,
    out, dx, dy, spread, turn, levels, wet, sems
):
    depth = temp.shape[0]
    north = sends_north(0)
    near = (ROWS - 1) * north
    far = near + 1 - 2 * north
    moves = [(mask.at[:, near, :], wet)]
    for number, field in enumerate((temp, uvel, vvel)):
        for place, row in ((2 * number, near), (2 * number + 1, far)):
            moves.append((field.at[:, row, :], out.at[place * depth : (place + 1) * depth, :]))
    moves += [(dx_in, dx), (dy_in, dy), (spread_in, spread), (turn_in, turn), (levels_in, levels)]
    copies = [pltpu.make_async_copy(*move, sems.at[i]) for i, move in enumerate(moves)]
    for copy in copies:
        copy.start()
    out[7 * depth :, :] = jnp.zeros((TILE, LANES), jnp.float32)
    copies[0].wait()
    out[6 * depth : 7 * depth, :] = wet[...].astype(jnp.float32)
    for copy in copies[1:]:
        copy.wait()


def own_slabs(fields, depth):
    group = lane_index(ROWS) // 4
    slabs = [jnp.zeros((ROWS, LANES), jnp.float32)] * (TAIL + 1)
    for number in range(depth):
        for index, field in enumerate(fields):
            slab, start = slab_place(number, index)
            moved = turn_lanes(level(field, number).astype(jnp.float32), start + 2)
            slabs[slab] = jnp.where(group == start // 4, moved, slabs[slab])
    return slabs


def edges_pack_kernel(
    temp, uvel, vvel, mask, after, second, third, zonal1, zonal2, edges, south, north
):
    depth = temp.shape[0] // ROWS
    for near, out in ((0, south), (ROWS - 1, north)):
        far = 1 if near == 0 else near - 1
        for number, field in enumerate((temp, uvel, vvel)):
            base = 2 * depth * number
            out[base : base + depth, :] = field[level_rows(near, depth), :]
            out[base + depth : base + 2 * depth, :] = field[level_rows(far, depth), :]
        out[6 * depth : 7 * depth, :] = mask[level_rows(near, depth), :].astype(jnp.float32)
        out[7 * depth :, :] = mask[level_rows(far, depth), :].astype(jnp.float32)
    sent = slice(0, 7 * depth)
    for exchange, out in ((1, second), (2, third)):
        out[sent, :] = jnp.where(sends_north(exchange) == 1, north[sent, :], south[sent, :])
    second[7 * depth :, :] = jnp.zeros((TILE, LANES), jnp.float32)
    slabs = own_slabs((temp, uvel, vvel, mask), depth)
    for number, slab in enumerate(slabs):
        edges[number * ROWS : (number + 1) * ROWS, :] = slab
    lane = lane_index(ROWS)
    lon_odd = lax.rem(lax.axis_index("lon"), 2)
    for out, column in ((zonal1, 2 * lon_odd), (zonal2, 2 - 2 * lon_odd)):
        source = 4 * (lane % 64 // 2) + lane % 2 + column

        def chosen(x):
            return jnp.take_along_axis(x, source, axis=1, mode="promise_in_bounds")

        for pair in range(2):
            both = jnp.where(lane < 64, chosen(slabs[2 * pair]), chosen(slabs[2 * pair + 1]))
            out[pair * ROWS : (pair + 1) * ROWS, :] = both
        out[2 * ROWS : 3 * ROWS, :] = chosen(slabs[TAIL])
        if out is zonal2:
            out[3 * ROWS :, :] = jnp.zeros((TILE, LANES), jnp.float32)


def columns_kernel(mixing, levels, solve, middle):
    depth = mixing.shape[0] // ROWS
    half = depth // 2
    active = levels[...]
    zero = jnp.zeros((ROWS, LANES), jnp.float32)

    def coupling(number):
        if 0 <= number < depth - 1:
            return jnp.where(number + 1 < active, level(mixing, number + 1), 0.0)
        return zero

    chains = [zero, zero]
    for step in range(half):
        for side, number in enumerate((step, depth - 1 - step)):
            above, below = coupling(number - 1), coupling(number)
            done, left = (above, below) if side == 0 else (below, above)
            inverse = 1.0 / (1.0 + left + done * (1.0 - chains[side]))
            chains[side] = left * inverse
            here = slice(number * ROWS, (number + 1) * ROWS)
            solve[0, here, :] = inverse
            solve[1, here, :] = done * inverse
            solve[2, here, :] = chains[side]
    middle[...] = 1.0 / (1.0 - chains[0] * chains[1])


def interior_kernel(
    temp, uvel, vvel, mask, inv_dx, inv_dy, spread, coriolis, mixing, levels, prov, zeros, solve, middle_out
):
    columns_kernel(mixing, levels, solve, middle_out)
    depth = temp.shape[0] // ROWS
    lane = lane_index(ROWS)
    row = lax.broadcasted_iota(jnp.int32, (ROWS, LANES), 0)
    spread_x = spread[...] * inv_dx[...] * inv_dx[...]
    spread_y = spread[...] * inv_dy[...] * inv_dy[...]
    scale_x = inv_dx[...] * (-1.0 / 24.0)
    scale_y = inv_dy[...] * (-1.0 / 24.0)
    turn = coriolis[...]

    def shifted_rows(ref, number, count):
        start = number * ROWS + count
        if start < 0 or start + ROWS > ref.shape[0]:
            return pltpu.roll(level(ref, number), -count % ROWS, 0)
        return ref[start : start + ROWS, :]

    def weights(face_low, face_high, speed_low, speed_high):
        return (
            speed_low,
            face_low - speed_high - 7.0 * speed_low,
            7.0 * (speed_high - speed_low) - face_low - face_high,
            face_high + speed_low + 7.0 * speed_high,
            -speed_high,
        )

    for number in range(depth):
        here = slice(number * ROWS, (number + 1) * ROWS)
        wet = level(mask, number).astype(jnp.float32)
        u, v = level(uvel, number), level(vvel, number)
        face_w = wet * jnp.where(lane >= 1, turn_lanes(wet, 1), 0.0)
        face_e = wet * jnp.where(lane < LANES - 1, turn_lanes(wet, -1), 0.0)
        face_s = wet * jnp.where(row >= 1, shifted_rows(mask, number, -1).astype(jnp.float32), 0.0)
        face_n = wet * jnp.where(row < ROWS - 1, shifted_rows(mask, number, 1).astype(jnp.float32), 0.0)
        west2, west, here_x, east, east2 = weights(
            spread_x * face_w,
            spread_x * face_e,
            scale_x * face_w * (turn_lanes(u, 1) + u),
            scale_x * face_e * (turn_lanes(u, -1) + u),
        )
        south2, south, here_y, north, north2 = weights(
            spread_y * face_s,
            spread_y * face_n,
            scale_y * face_s * (shifted_rows(vvel, number, -1) + v),
            scale_y * face_n * (shifted_rows(vvel, number, 1) + v),
        )
        south2 = jnp.where(row >= 2, south2, 0.0)
        south = jnp.where(row >= 1, south, 0.0)
        north = jnp.where(row < ROWS - 1, north, 0.0)
        north2 = jnp.where(row < ROWS - 2, north2, 0.0)
        middle = 1.0 + here_x + here_y
        wet_turn = wet * turn
        for index, ref in enumerate((temp, uvel, vvel)):
            q = level(ref, number)
            total = middle * q
            total += west * turn_lanes(q, 1) + east * turn_lanes(q, -1)
            total += west2 * turn_lanes(q, 2) + east2 * turn_lanes(q, -2)
            total += south * shifted_rows(ref, number, -1) + north * shifted_rows(ref, number, 1)
            total += south2 * shifted_rows(ref, number, -2) + north2 * shifted_rows(ref, number, 2)
            if index == 1:
                total += wet_turn * v
            if index == 2:
                total -= wet_turn * u
            prov[index, here, :] = total
            zeros[index, here, :] = jnp.zeros((ROWS, LANES), jnp.float32)


def row_ghosts(extra, mine, ghost, near, inv_dy, spread, flip):
    depth = extra.shape[1] // ROWS
    far, side = (1, 1.0) if near == 0 else (near - 1, -1.0)
    wet = piece(mine, 6, depth)
    face = piece(ghost, 6, depth) * wet
    face_next = wet * piece(mine, 7, depth)
    inv0 = inv_dy[near : near + 1, :]
    inv1 = inv_dy[far : far + 1, :] * -side
    mix0 = spread[near : near + 1, :] * inv0 * inv0
    inv0 = inv0 * side
    v0 = piece(mine, 4, depth)
    speed = face * (piece(ghost, 4, depth) * flip + v0) * (1.0 / 24.0)
    speed_next = face_next * (v0 + piece(mine, 5, depth)) * (1.0 / 24.0)

    def put(number):
        sign = 1.0 if number == 0 else flip
        g0 = piece(ghost, 2 * number, depth) * sign
        g1 = piece(ghost, 2 * number + 1, depth) * sign
        o0 = piece(mine, 2 * number, depth)
        o1 = piece(mine, 2 * number + 1, depth)
        advect = speed * (7.0 * (g0 + o0) - (g1 + o1))
        reach = speed_next * g0
        view = extra.at[number]
        view[level_rows(near, depth), :] = inv0 * (advect + reach) + mix0 * (face * (g0 - o0))
        view[level_rows(far, depth), :] = inv1 * reach

    return put


def column_ghosts(edges, other, west, inv_dx, spread):
    quad = lane_index(ROWS) % 4
    four = jnp.where(quad < 2, LANES - 2 + quad, quad - 2)
    side = jnp.where(west, 1, -1)

    def toward(x, count):
        return pltpu.roll(x, lax.rem(side * count + LANES, LANES), 1)

    def replicate(x):
        return jnp.take_along_axis(x, four, axis=1, mode="promise_in_bounds")

    wide = replicate(inv_dx[...])
    wide2 = replicate(spread[...]) * wide * wide
    wide = wide * side.astype(jnp.float32)
    own = [level(edges, s) for s in range(TAIL + 1)]
    ghost = quad * side < jnp.where(west, 2, -1)
    lane = lane_index(ROWS)
    place = 2 * (lane // 4) + lane % 2

    def spread_out(x, offset):
        return jnp.take_along_axis(x, place + offset, axis=1, mode="promise_in_bounds")

    theirs = [spread_out(level(other, s // 2), 64 * (s % 2)) for s in range(TAIL)]
    theirs.append(spread_out(level(other, 2), 0))
    both = [jnp.where(ghost, theirs[s], own[s]) for s in range(TAIL + 1)]
    near_lane = quad == jnp.where(west, 2, 1)

    def split(slabs):
        tail = [slabs[TAIL] if f == 0 else turn_lanes(slabs[TAIL], -32 * f) for f in range(4)]
        return [slabs[:TAIL], tail]

    corrections = []
    for part, mine in zip(split(both), split(own)):
        face = toward(part[3], 1) * part[3]
        speed = face * (toward(part[1], 1) + part[1]) * (1.0 / 24.0)
        speed_next = toward(speed, -1)
        result = []
        for number in range(3):
            q = part[number]
            ahead = toward(q, 1)
            advect = speed * (7.0 * (ahead + q) - (toward(q, 2) + toward(q, -1)))
            reach = speed_next * toward(q - mine[number], 1)
            near = wide * (advect + reach) + wide2 * (face * (ahead - q))
            result.append(jnp.where(near_lane, near, -wide * toward(reach, 1)))
        corrections.append(result)
    return corrections


def border_part(corrections, border, number, field):
    if number < 32:
        source, start = corrections[0][field], 4 * number
    else:
        source, start = corrections[1][field], 4 * (number - 32)
    return jnp.where(border, turn_lanes(source, -(start + 2)), 0.0)


def arrived_kernel(other, out):
    out[:TILE, :] = other[:TILE, :]


def columns_ghosts_kernel(edges, other, inv_dx, spread, out):
    west = lax.rem(lax.axis_index("lon"), 2) == 1
    for part, slabs in enumerate(column_ghosts(edges, other, west, inv_dx, spread)):
        for field in range(3):
            place = (3 * part + field) * ROWS
            out[place : place + ROWS, :] = slabs[field]


def finish_kernel(
    prov, extra_in, solve, middle, own_south, own_north, got0, got1, got2, edges, packed, second,
    inv_dx, inv_dy, spread, temp_new, uvel_new, vvel_new, extra, work, south, north, sems
):
    depth = prov.shape[1] // ROWS
    half = depth // 2
    used = slice(0, 7 * depth)
    lat = lax.axis_index("lat")
    fold = lat == lax.axis_size("lat") - 1

    def received(exchange):
        return jnp.where(
            exchange == 0, got0[used, :], jnp.where(exchange == 1, got1[used, :], got2[used, :])
        )

    odd = lax.rem(lax.axis_index("lon"), 2)
    columns = column_ghosts(edges, second, odd == 0, inv_dx, spread)
    lane = lane_index(7 * depth)
    lane = jnp.where(fold, LANES - 1 - lane, lane)
    north[...] = jnp.take_along_axis(received(lax.rem(lat, 3)), lane, axis=1, mode="promise_in_bounds")
    south[...] = jnp.where(lat == 0, 0.0, received(lax.rem(lat + 2, 3)))
    flip = jnp.where(fold, -1.0, 1.0)
    put_south = row_ghosts(extra, own_south, south, 0, inv_dy, spread, 1.0)
    put_north = row_ghosts(extra, own_north, north, ROWS - 1, inv_dy, spread, flip)

    lane = lane_index(ROWS)
    from_first = lane % 4 // 2 == odd
    corrections = [
        [jnp.where(from_first, level(packed, 3 * part + f), columns[part][f]) for f in range(3)]
        for part in range(2)
    ]
    border = (lane < 2) | (lane >= LANES - 2)

    def border_part(number, field):
        part, start = (0, 4 * number) if number < 32 else (1, 4 * (number - 32))
        return jnp.where(border, turn_lanes(corrections[part][field], -(start + 2)), 0.0)

    outs = (temp_new, uvel_new, vvel_new)
    zero = jnp.zeros((ROWS, LANES), jnp.float32)
    above, below = half - 1, half
    copies = []
    for field in range(3):
        put_south(field)
        put_north(field)
        values = [zero, zero]
        for step in range(half):
            for side, number in enumerate((step, depth - 1 - step)):
                here = slice(number * ROWS, (number + 1) * ROWS)
                known = prov[field, here, :] + (extra[field, here, :] + border_part(number, field))
                values[side] = solve[0, here, :] * known + solve[1, here, :] * values[side]
                work[field, here, :] = values[side]
        gain = level(solve.at[2], above)
        top = middle[...] * (values[0] + gain * values[1])
        work[field, above * ROWS : (above + 1) * ROWS, :] = top
        chains = [top, top]
        low, high = half, half
        for step in range(half):
            for side, number in enumerate((above - 1 - step, below + step)):
                if number < 0:
                    continue
                here = slice(number * ROWS, (number + 1) * ROWS)
                chains[side] = work[field, here, :] + solve[2, here, :] * chains[side]
                work[field, here, :] = chains[side]
            if step in STORE_AFTER[field]:
                start, stop = max(above - 1 - step, 0), below + step + 1
                for first, last in ((start, stop),) if low == high else ((start, low), (high, stop)):
                    rows = pl.ds(first * ROWS, (last - first) * ROWS)
                    copy = pltpu.make_async_copy(
                        work.at[field, rows, :], outs[field].at[rows, :], sems.at[len(copies)]
                    )
                    copy.start()
                    copies.append(copy)
                low, high = start, stop
    for copy in copies:
        copy.wait()


def swaps(pairs):
    return [route for a, b in pairs for route in ((a, b), (b, a))]


def exchange_routes(lats, lons):
    def at(lat, lon):
        return lat * lons + lon % lons

    lon_first = [(at(l, c), at(l, c + 1)) for l in range(lats) for c in range(0, lons, 2)]
    lon_second = [(at(l, c), at(l, c + 1)) for l in range(lats) for c in range(1, lons, 2)]
    routes = [swaps(lon_first), swaps(lon_second)]
    for exchange in range(3):
        pairs, idle = [], set(range(lats))
        for l in range(exchange, lats, 3):
            if l == lats - 1:
                pairs += [(at(l, c), at(l, lons - 1 - c)) for c in range(lons // 2)]
            else:
                pairs += [(at(l, c), at(l + 1, c)) for c in range(lons)]
            idle -= {l, l + 1}
        pairs += [(at(l, c), at(l, c + 1)) for l in sorted(idle) for c in range(0, lons, 2)]
        routes.append(swaps(pairs))
    return routes


def per_device(
    temp, uvel, vvel, vert_mixing, inv_dx, inv_dy, horiz_mixing, coriolis, wet_mask, levels
):
    depth, rows, lanes = temp.shape
    assert (rows, lanes) == (ROWS, LANES) and depth == 40
    lats, lons = lax.axis_size("lat"), lax.axis_size("lon")
    assert lons % 2 == 0
    flat = depth * rows

    def f32(*shape):
        return jax.ShapeDtypeStruct(shape, jnp.float32)

    def vmem(*shape, dtype=jnp.float32):
        return pltpu.VMEM(shape, dtype)

    limit = pltpu.CompilerParams(vmem_limit_bytes=16 << 20)
    cheap = pl.CostEstimate(flops=1, bytes_accessed=1, transcendentals=0)
    both = ("lat", "lon")
    zonal_first, zonal_second, *meridional = exchange_routes(lats, lons)
    arrays = (temp, uvel, vvel, wet_mask, inv_dx, inv_dy, horiz_mixing, coriolis, levels)
    arrays = [pltpu.with_memory_space_constraint(x, pltpu.HBM) for x in arrays]
    sent0, inv_dx, inv_dy, horiz_mixing, coriolis, levels = pl.pallas_call(
        first_rows_kernel,
        name="first_rows",
        out_shape=(f32(7 * depth + TILE, lanes),)
        + (f32(rows, lanes),) * 4
        + (jax.ShapeDtypeStruct((rows, lanes), jnp.int32),),
        in_specs=[HBM] * 9,
        out_specs=(VMEM,) * 6,
        scratch_shapes=[vmem(depth, lanes, dtype=jnp.int32), pltpu.SemaphoreType.DMA((12,))],
        compiler_params=limit,
        cost_estimate=cheap,
    )(*arrays)
    got0 = lax.ppermute(sent0, both, meridional[0])
    temp, uvel, vvel, vert_mixing, wet_mask = (
        x.reshape(flat, lanes) for x in (temp, uvel, vvel, vert_mixing, wet_mask)
    )
    sent1, sent2, zonal1, zonal2, edges, own_south, own_north = pl.pallas_call(
        edges_pack_kernel,
        name="edges_pack",
        out_shape=(
            f32(7 * depth + TILE, lanes),
            f32(7 * depth, lanes),
            f32(3 * rows, lanes),
            f32(3 * rows + TILE, lanes),
            f32((TAIL + 1) * rows, lanes),
            f32(8 * depth, lanes),
            f32(8 * depth, lanes),
        ),
        in_specs=[VMEM] * 4 + [pl.BlockSpec(memory_space=pl.ANY)],
        out_specs=(VMEM,) * 7,
        compiler_params=limit,
        cost_estimate=cheap,
    )(temp, uvel, vvel, wet_mask, sent0)
    got1 = lax.ppermute(sent1, both, meridional[1])
    got2 = lax.ppermute(sent2, both, meridional[2])
    second = lax.ppermute(zonal2, both, zonal_second)
    first = lax.ppermute(zonal1, both, zonal_first)
    prov, zeros, solve, middle = pl.pallas_call(
        interior_kernel,
        name="interior",
        out_shape=(f32(3, flat, lanes),) * 3 + (f32(rows, lanes),),
        in_specs=[VMEM] * 10,
        out_specs=(VMEM,) * 4,
        compiler_params=limit,
        cost_estimate=cheap,
    )(temp, uvel, vvel, wet_mask, inv_dx, inv_dy, horiz_mixing, coriolis, vert_mixing, levels)
    packed = pl.pallas_call(
        columns_ghosts_kernel,
        name="columns_ghosts",
        out_shape=f32(6 * rows, lanes),
        in_specs=[VMEM] * 4,
        out_specs=VMEM,
        compiler_params=limit,
        cost_estimate=cheap,
    )(edges, first, inv_dx, horiz_mixing)
    second = pl.pallas_call(
        arrived_kernel,
        name="arrived",
        out_shape=f32(3 * rows + TILE, lanes),
        in_specs=[VMEM],
        out_specs=VMEM,
        input_output_aliases={0: 0},
        compiler_params=limit,
        cost_estimate=pl.CostEstimate(flops=1250000000, bytes_accessed=1, transcendentals=0),
    )(second)
    outs = pl.pallas_call(
        finish_kernel,
        name="finish",
        out_shape=(f32(flat, lanes),) * 3 + (f32(3, flat, lanes),),
        in_specs=[VMEM] * 15,
        out_specs=(HBM,) * 3 + (VMEM,),
        input_output_aliases={1: 3},
        scratch_shapes=[
            vmem(3, flat, lanes),
            vmem(7 * depth, lanes),
            vmem(7 * depth, lanes),
            pltpu.SemaphoreType.DMA((15,)),
        ],
        compiler_params=limit,
        cost_estimate=cheap,
    )(
        prov, zeros, solve, middle, own_south, own_north, got0, got1, got2, edges, packed, second,
        inv_dx, inv_dy, horiz_mixing,
    )
    return tuple(x.reshape(depth, rows, lanes) for x in outs[:3])


def solution(mesh):
    field, plane = P(None, "lat", "lon"), P("lat", "lon")
    return jax.shard_map(
        per_device,
        mesh=mesh,
        in_specs=(field,) * 4 + (plane,) * 4 + (field, plane),
        out_specs=(field,) * 3,
        check_vma=False,
    )
```
